512 devices in a mesh: gz: 16 (over y, x_hi), gy: 32 (over z, x_lo, core).
Axes of the slice: x: 4 (x_hi: 2, x_lo: 2; x = x_hi * 2 + x_lo), y: 8, z: 8, core: 2. Of those that a mesh axis runs over, the one named last changes fastest.
Arguments:
- field_b: float32 [3, 2, 2048, 2048], P(None, None, 'gy', 'gz'), may hold values from -6 to 6
- density: float32 [2, 2048, 2048], P(None, 'gy', 'gz'), may hold values from 0.5 to 2
- level_y: int32 [2048], P('gy'), may hold values from 0 to 7
- level_z: int32 [2048], P('gz'), may hold values from 0 to 7
- bins: int32 [1024, 2048], P(('gz', 'gy')), may hold values from 0 to 1023
Outputs:
- emf: bfloat16 [3, 2, 2048, 2048], P(None, None, 'gy', 'gz')
- mode_power: float32 [1024, 2048], P(('gz', 'gy'))
- spectrum: float32 [1024], replicated
The draws below stay inside these ranges and needn't reach their ends.
All inputs are finite; a program needn't handle non-finite values.
Results may differ from the reference program's by a relative error of at most 0.0035.
Values may be sent and summed in bfloat16 or wider, within the bound.
No kernel may reach another device: no remote copies, remote signals or barrier semaphores. Data moves between devices by JAX's collectives and lax.ppermute only.
A program may use at most 64 MiB of HBM per device.

```python
import math
import jax
import jax.numpy as jnp
from jax import lax

XW = 2
NY = 2048
NZ = 2048
NB = 1024
LEVELS = 8
KZ = 1024


def plant(values, stream_key, smallest, high):
    spot = [jax.random.randint(jax.random.fold_in(stream_key, axis), (), 0, length) for axis, length in enumerate(values.shape)]
    main_axis = values.shape.index(max(values.shape))
    beside = spot[:main_axis] + [(spot[main_axis] + 1) % values.shape[main_axis]] + spot[main_axis + 1:]
    return values.at[tuple(spot)].set(smallest).at[tuple(beside)].set(high)


def block_levels(key, dims, shards, smallest, high):
    gain, own = 1.0, jax.random.fold_in(key, 6)
    for axis_at, shards_of in shards:
        steps = jnp.exp(jax.random.uniform(jax.random.fold_in(own, axis_at), (shards_of,), jnp.float32, smallest / len(shards), high / len(shards)))
        gain = gain * jnp.repeat(steps, dims[axis_at] // shards_of).reshape([-1 if axis == axis_at else 1 for axis in range(len(dims))])
    return gain


def normal_values(key, shape, deviation, reach, shards=(), held_as=jnp.bfloat16):
    array = jax.random.normal(key, shape, jnp.float32) * deviation
    if len(shards) > 0:
        array = block_levels(key, shape, shards, -0.22, 0.18) * array
    return jnp.clip(array, min=-reach, max=reach).astype(held_as)


def setup_inputs(seed: int = 0) -> dict:
    splits = jax.random.split(jax.random.key(seed), 6)
    return {
        "field_b": normal_values(splits[0], (3, XW, NY, NZ), 1.0, 6.0, ((2, 32), (3, 16)), jnp.float32),
        "density": jnp.clip(jnp.exp(math.log(2.0) - 1.3862944 * jax.random.uniform(splits[1], (XW, NY, NZ), jnp.float32) ** block_levels(splits[1], (XW, NY, NZ), ((1, 32), (2, 16)), -0.2, 0.2)), 0.5, 2.0),
        "level_y": plant(jax.random.randint(splits[2], (NY,), 0, LEVELS), jax.random.fold_in(splits[2], 1), 0, LEVELS - 1).astype(jnp.int32),
        "level_z": plant(jax.random.randint(splits[3], (NZ,), 0, LEVELS), jax.random.fold_in(splits[3], 1), 0, LEVELS - 1).astype(jnp.int32),
        "bins": plant(jax.random.randint(splits[4], (KZ, NY), 0, NB), jax.random.fold_in(splits[4], 1), 0, NB - 1).astype(jnp.int32),
    }


def metric(level):
    return 1.0 / (1.0 + 0.25 * level.astype(jnp.float32))

def twiddle(positions, modes, length):
    phase = positions[:, None] * modes[None, :] % length
    angle = phase.astype(jnp.float32) * (2.0 * math.pi / length)
    factor = 1.0 / math.sqrt(length)
    return ((jnp.cos(angle) * factor).astype(jnp.bfloat16), (jnp.sin(angle) * factor).astype(jnp.bfloat16))

def reference(field_b, density, level_y, level_z, bins):
    metric_y = metric(level_y)[None, :, None]
    metric_z = metric(level_z)[None, None, :]

    def deriv_y(field):
        return 0.5 * (jnp.roll(field, -1, 1) - jnp.roll(field, 1, 1)) * metric_y

    def deriv_z(field):
        return 0.5 * (jnp.roll(field, -1, 2) - jnp.roll(field, 1, 2)) * metric_z

    def deriv_x(field):
        padded = jnp.pad(field, ((1, 1), (0, 0), (0, 0)))
        return 0.5 * (padded[2:] - padded[:-2])
    b_x, b_y, b_z = (field_b[0], field_b[1], field_b[2])
    cur_x = deriv_y(b_z) - deriv_z(b_y)
    cur_y = deriv_z(b_x) - deriv_x(b_z)
    cur_z = deriv_x(b_y) - deriv_y(b_x)
    e_x = (cur_y * b_z - cur_z * b_y) / density
    e_y = (cur_z * b_x - cur_x * b_z) / density
    e_z = (cur_x * b_y - cur_y * b_x) / density
    emf = jnp.stack([e_x, e_y, e_z]).astype(jnp.bfloat16)
    z_pos = jnp.arange(NZ, dtype=jnp.int32)
    z_cos, z_sin = twiddle(z_pos, jnp.arange(KZ, dtype=jnp.int32), NZ)
    table_z = jnp.concatenate([z_cos, -z_sin], axis=1)
    y_pos = jnp.arange(NY, dtype=jnp.int32)
    y_cos, y_sin = twiddle(y_pos, y_pos, NY)
    table_y = jnp.concatenate([y_cos, y_sin], axis=1)
    total = jnp.zeros((KZ, NY), jnp.float32)
    count = KZ * XW
    for comp in range(3):
        flat = emf[comp].reshape(XW * NY, NZ)
        z_modes = jnp.dot(flat, table_z, preferred_element_type=jnp.float32).astype(jnp.bfloat16)
        z_modes = z_modes.reshape(XW, NY, 2, KZ).transpose(2, 3, 0, 1).reshape(2 * count, NY)
        product = jnp.dot(z_modes, table_y, preferred_element_type=jnp.float32)
        re_cos = product[:count, :NY]
        re_sin = product[:count, NY:]
        im_cos = product[count:, :NY]
        im_sin = product[count:, NY:]
        real_part = re_cos + im_sin
        imag_part = im_cos - re_sin
        power = (real_part * real_part + imag_part * imag_part).reshape(KZ, XW, NY)
        total = total + lax.optimization_barrier(jnp.sum(power, axis=1))
    mode_power = total / (3 * XW)
    spectrum = jax.ops.segment_sum(mode_power.reshape(-1), bins.reshape(-1), num_segments=NB) * (NB / (KZ * NY))
    return (emf, mode_power, spectrum)
```

```python
import math

import jax
import jax.numpy as jnp
import numpy as np
from jax import lax
from jax.experimental import pallas as pl
from jax.experimental.pallas import tpu as pltpu
from jax.sharding import PartitionSpec as P

NY = 2048
NZ = 2048
NB = 1024
KZ = 1024
BF = jnp.bfloat16
F32 = jnp.float32


def angle(a, b, length):
    return 2.0 * math.pi * ((a[:, None] * b[None, :]) % length) / length


def pieces(table):
    high = table.astype(jnp.bfloat16)
    low = (table - high.astype(np.float64)).astype(jnp.bfloat16)
    return high, low


def z_tables():
    inner = angle(np.arange(64), np.arange(128), 128)
    high, low = pieces(np.concatenate([np.cos(inner), np.sin(inner)], axis=1))
    turn = angle(np.arange(16), np.arange(128), 2048)
    return np.concatenate([high, low], axis=0), np.stack([np.cos(turn), np.sin(turn)]).astype(np.float32)


def y_tables():
    rows = (8 * np.arange(32)[None, :] + np.arange(8)[:, None]).reshape(-1)
    inner = angle(rows, np.arange(256), 256)
    high, low = pieces(np.concatenate([np.cos(inner), np.sin(inner)], axis=1))
    turn = angle(np.arange(8), np.arange(256), 2048)
    order = np.zeros((128, 128), np.float32)
    for c in range(2):
        for e in range(2):
            for comp in range(4):
                for y0 in range(8):
                    order[c * 64 + y0 * 8 + e * 4 + comp, c * 64 + e * 32 + comp * 8 + y0] = 1.0
    return high, low, np.stack([np.cos(turn), np.sin(turn)]).astype(np.float32), order.astype(jnp.bfloat16)


def emf_kernel(fb, den, my_ref, mz_ref, ylo_ref, yhi_ref, zlo_ref, zhi_ref, emf_ref, msg_ref):
    rows, lanes = fb.shape[2], fb.shape[3]
    row = lax.broadcasted_iota(jnp.int32, (rows, lanes), 0)
    lane = lax.broadcasted_iota(jnp.int32, (rows, lanes), 1)
    my = my_ref[...]
    mz = mz_ref[...]
    zlo = jnp.transpose(zlo_ref[...])
    zhi = jnp.transpose(zhi_ref[...])

    def d_y(f, at):
        up = jnp.where(row == rows - 1, yhi_ref[at : at + 1, :], pltpu.roll(f, rows - 1, 0))
        down = jnp.where(row == 0, ylo_ref[at : at + 1, :], pltpu.roll(f, 1, 0))
        return (up - down) * my

    def d_z(f, at):
        up = jnp.where(lane == lanes - 1, zhi[:, at : at + 1], pltpu.roll(f, lanes - 1, 1))
        down = jnp.where(lane == 0, zlo[:, at : at + 1], pltpu.roll(f, 1, 1))
        return (up - down) * mz

    for p in range(2):
        b_x, b_y, b_z = fb[0, p], fb[1, p], fb[2, p]
        half = 0.5 if p == 0 else -0.5
        cur_x = d_y(b_z, 2 + p) - d_z(b_y, 2 + p)
        cur_y = d_z(b_x, p) - half * fb[2, 1 - p]
        cur_z = half * fb[1, 1 - p] - d_y(b_x, p)
        dens = den[p]
        parts = (
            (cur_y * b_z - cur_z * b_y) / dens,
            (cur_z * b_x - cur_x * b_z) / dens,
            (cur_x * b_y - cur_y * b_x) / dens,
        )
        for comp in range(3):
            value = parts[comp].astype(BF)
            emf_ref[comp, p] = value
            for block in range(8):
                msg_ref[2 * block + p, comp] = parts[comp][8 * block : 8 * block + 8].astype(BF)


def fourier16(x):
    plus = [x[i] + x[i + 8] for i in range(8)]
    minus = [x[i] - x[i + 8] for i in range(8)]
    out = {}
    a = [plus[i] + plus[i + 4] for i in range(4)]
    b = [plus[i] - plus[i + 4] for i in range(4)]
    r = math.sqrt(0.5)
    out[0] = ((a[0] + a[2]) + (a[1] + a[3]), None)
    out[8] = ((a[0] + a[2]) - (a[1] + a[3]), None)
    out[4] = (a[0] - a[2], a[3] - a[1])
    s1, s3 = (b[1] - b[3]) * r, (b[1] + b[3]) * r
    out[2] = (b[0] + s1, -(b[2] + s3))
    out[6] = (b[0] - s1, b[2] - s3)
    even = [minus[i] - minus[8 - i] for i in (1, 2, 3)]
    odd = [minus[i] + minus[8 - i] for i in (1, 2, 3)]
    for k in (1, 3, 5, 7):
        real = minus[0]
        imag = minus[4] * (-math.sin(math.pi * k / 2))
        for i in (1, 2, 3):
            real = real + even[i - 1] * math.cos(math.pi * i * k / 8)
            imag = imag - odd[i - 1] * math.sin(math.pi * i * k / 8)
        out[k] = (real, imag)
    return out


def z_kernel(x_ref, table_ref, turn_ref, out_ref, high_ref, low_ref):
    x = [x_ref[i].astype(F32) for i in range(16)]
    y = fourier16(x)
    zero = jnp.zeros((8, 128), BF)
    for k in range(16):
        cos = turn_ref[0, k : k + 1, :]
        sin = turn_ref[1, k : k + 1, :]
        real, imag = y[k] if k <= 8 else y[16 - k]
        if imag is None:
            t_re, t_im = real * cos, -(real * sin)
        else:
            if k > 8:
                imag = -imag
            t_re, t_im = real * cos + imag * sin, imag * cos - real * sin
        d0, e = k // 2, k % 2
        for value, spots in ((t_re, ((0, 0, 1), (1, 1, -1))), (t_im, ((0, 1, 1), (1, 0, 1)))):
            high = value.astype(BF)
            low = (value - high.astype(F32)).astype(BF)
            for c, side, sign in spots:
                at = d0 * 128 + c * 64 + e * 32
                for ref, piece in ((high_ref, high), (low_ref, low)):
                    ref[at : at + 24, side * 128 : side * 128 + 128] = piece if sign > 0 else -piece
                    ref[at + 24 : at + 32, side * 128 : side * 128 + 128] = zero
    contract = (((1,), (1,)), ((), ()))
    both = lax.dot_general(table_ref[...], high_ref[...], contract, preferred_element_type=F32)
    rest = lax.dot_general(table_ref[0:64, :], low_ref[...], contract, preferred_element_type=F32)
    out = both[0:64] + (both[64:128] + rest)
    for d0 in range(8):
        out_ref[pl.ds(d0, 64, stride=8), :] = out[:, d0 * 128 : d0 * 128 + 128]


def fourier8(re, im):
    def add(a, b):
        return (a[0] + b[0], a[1] + b[1])

    def sub(a, b):
        return (a[0] - b[0], a[1] - b[1])

    def turn(a):
        return (a[1], -a[0])

    def four(x):
        s, d = add(x[0], x[2]), sub(x[0], x[2])
        t, u = add(x[1], x[3]), turn(sub(x[1], x[3]))
        return [add(s, t), add(d, u), sub(s, t), sub(d, u)]

    x = list(zip(re, im))
    r = math.sqrt(0.5)
    even = four([add(x[i], x[i + 4]) for i in range(4)])
    low = [sub(x[i], x[i + 4]) for i in range(4)]
    low[1] = ((low[1][0] + low[1][1]) * r, (low[1][1] - low[1][0]) * r)
    low[2] = turn(low[2])
    low[3] = ((low[3][1] - low[3][0]) * r, -(low[3][0] + low[3][1]) * r)
    odd = four(low)
    return [even[k // 2] if k % 2 == 0 else odd[k // 2] for k in range(8)]


def y_kernel(x_ref, high_ref, low_ref, turn_ref, order_ref, bins_ref, power_ref, sums_ref):
    total = [None] * 8
    for p in range(2):
        held = jnp.concatenate([x_ref[64 * b + 32 * p : 64 * b + 32 * p + 32, :] for b in range(8)], axis=0)
        lhs = lax.dot_general(
            order_ref[...], held.astype(BF), (((1,), (1,)), ((), ())), preferred_element_type=F32
        ).astype(BF)
        product = jnp.dot(lhs, high_ref[...], preferred_element_type=F32) + jnp.dot(
            lhs, low_ref[...], preferred_element_type=F32
        )
        real = product[0:64, 0:256] + product[64:128, 256:512]
        imag = product[64:128, 0:256] - product[0:64, 256:512]
        re, im = [], []
        for y0 in range(8):
            a, b = real[8 * y0 : 8 * y0 + 8], imag[8 * y0 : 8 * y0 + 8]
            if y0 > 0:
                cos, sin = turn_ref[0, y0 : y0 + 1, :], turn_ref[1, y0 : y0 + 1, :]
                a, b = a * cos + b * sin, b * cos - a * sin
            re.append(a)
            im.append(b)
        for q1, (a, b) in enumerate(fourier8(re, im)):
            power = a * a + b * b
            total[q1] = power if p == 0 else total[q1] + power
    scale = 1.0 / (6.0 * 2048.0 * 2048.0)
    for q1 in range(8):
        for e in range(2):
            power_ref[e : e + 1, 256 * q1 : 256 * q1 + 256] = (
                jnp.sum(total[q1][4 * e : 4 * e + 4], axis=0, keepdims=True) * scale
            )
    sums = jnp.zeros((8, 128), F32)
    for e in range(2):
        value = power_ref[e : e + 1, :]
        bins = bins_ref[e : e + 1, :]
        coarse = lax.broadcasted_iota(jnp.int32, (8, 2048), 0) == (bins >> 7)
        fine = (lax.broadcasted_iota(jnp.int32, (128, 2048), 0) == (bins & 127)).astype(F32).astype(BF)
        spread = jnp.where(coarse, value, 0.0)
        first = spread.astype(BF)
        spread = spread - first.astype(F32)
        second = spread.astype(BF)
        third = (spread - second.astype(F32)).astype(BF)
        for piece in (third, second, first):
            sums += lax.dot_general(piece, fine, (((1,), (1,)), ((), ())), preferred_element_type=F32)
    sums_ref[...] = sums * (NB / (KZ * NY))


def metric(level):
    return 1.0 / (1.0 + 0.25 * level.astype(F32))


def everywhere(block, axis):
    count = lax.axis_size(axis)
    copies = jnp.broadcast_to(block[None], (count,) + block.shape)
    return jnp.sum(lax.all_to_all(copies, axis, 0, 0, tiled=True), axis=0)


def on_device(field_b, density, level_y, level_z, bins):
    y_local, z_local = field_b.shape[2], field_b.shape[3]

    def shift(cells, axis, step):
        count = lax.axis_size(axis)
        return lax.ppermute(cells, axis, [(i, (i + step) % count) for i in range(count)])

    zlo = shift(field_b[0:2, :, :, z_local - 1].reshape(4, y_local), "gz", 1)
    zhi = shift(field_b[0:2, :, :, 0].reshape(4, y_local), "gz", -1)
    ylo = shift(field_b[0::2, :, y_local - 1, :].reshape(4, z_local), "gy", 1)
    yhi = shift(field_b[0::2, :, 0, :].reshape(4, z_local), "gy", -1)
    my = jnp.broadcast_to(0.5 * metric(level_y)[:, None], (y_local, z_local))
    mz = (0.5 * metric(level_z))[None, :]
    emf, message = pl.pallas_call(
        emf_kernel,
        out_shape=(
            jax.ShapeDtypeStruct(field_b.shape, BF),
            jax.ShapeDtypeStruct((16, 3, 8, z_local), BF),
        ),
    )(field_b, density, my, mz, ylo, yhi, zlo, zhi)
    lines = lax.all_to_all(message, "gz", 0, 0, tiled=True).reshape(16, 24, z_local)
    z_table, z_turn = z_tables()
    z_modes = pl.pallas_call(
        z_kernel,
        out_shape=jax.ShapeDtypeStruct((512, 128), F32),
        scratch_shapes=[pltpu.VMEM((1024, 256), BF), pltpu.VMEM((1024, 256), BF)],
    )(lines, z_table, z_turn)
    spread = lax.all_to_all(z_modes.reshape(512, 1, 128), ("gz", "gy"), 0, 0, tiled=True).reshape(512, 128)
    y_high, y_low, y_turn, order = y_tables()
    mode_power, sums = pl.pallas_call(
        y_kernel,
        out_shape=(jax.ShapeDtypeStruct((2, NY), F32), jax.ShapeDtypeStruct((8, 128), F32)),
    )(spread, y_high, y_low, y_turn, order, bins)
    spectrum = everywhere(everywhere(sums, "gz"), "gy").reshape(NB)
    return (emf, mode_power, spectrum)


def solution(mesh):
    placed = (
        P(None, None, "gy", "gz"),
        P(None, "gy", "gz"),
        P("gy"),
        P("gz"),
        P(("gz", "gy"), None),
    )
    return jax.shard_map(
        on_device,
        mesh=mesh,
        in_specs=placed,
        out_specs=(P(None, None, "gy", "gz"), P(("gz", "gy"), None), P()),
        check_vma=False,
    )
```

```python
import math

import jax
import jax.numpy as jnp
import numpy as np
from jax import lax
from jax.experimental import pallas as pl
from jax.experimental.pallas import tpu as pltpu
from jax.sharding import Mesh, PartitionSpec as P

NY = 2048
NZ = 2048
NB = 1024
KZ = 1024
BF = jnp.bfloat16
F32 = jnp.float32
GZ = ("yh", "yl", "xh")
GY = ("z", "xl", "c")
ACROSS = (((1,), (1,)), ((), ()))


def angle(a, b, length):
    return 2.0 * math.pi * ((a[:, None] * b[None, :]) % length) / length


def z_table():
    part, kappa, yh, jh = np.meshgrid(*(np.arange(n) for n in (4, 16, 4, 4)), indexing="ij")
    modes = (16 * (16 * yh + 4 * part + jh) + kappa).reshape(4, 1, 256, 1)
    turn = (modes * np.arange(128) % NZ + 128 * np.arange(8).reshape(1, 8, 1, 1)) % NZ
    return (np.cos(2.0 * math.pi * turn / NZ) / math.sqrt(NZ)).astype(jnp.bfloat16)


def y_tables():
    inner = angle((4 * np.arange(32)[None, :] + np.arange(4)[:, None]).reshape(-1), np.arange(128), 128)
    table = np.zeros((128, 2, 2, 2, 2, 128))
    for e in range(2):
        table[:, 0, e, e, 0] = np.cos(inner)
        table[:, 0, e, e, 1] = -np.sin(inner)
        table[:, 1, e, e, 0] = np.sin(inner)
        table[:, 1, e, e, 1] = np.cos(inner)
    turn = angle(np.arange(16), np.arange(128), NY)
    order = np.zeros((128, 128), np.float32)
    for cp in range(6):
        for y0 in range(16):
            order[y0 * 8 + cp, cp * 16 + y0] = 1.0
    return (
        table.reshape(512, 512).astype(jnp.bfloat16),
        np.stack([np.cos(turn), np.sin(turn)]).astype(np.float32),
        order.astype(jnp.bfloat16),
    )


def metric(level):
    return 1.0 / (1.0 + 0.25 * level.astype(F32))


def emf_kernel(
    fb_far, den_far, ly_far, lz_far, ylo_ref, yhi_ref, zlo_ref, zhi_ref, emf_ref, msg_ref, fb, den, ly_ref, lz_ref, sems
):
    far_near = ((ly_far, ly_ref), (lz_far, lz_ref), (fb_far, fb), (den_far, den))
    copies = [pltpu.make_async_copy(far, near, sems.at[n]) for n, (far, near) in enumerate(far_near)]
    for copy in copies:
        copy.start()
    copies[0].wait()
    copies[1].wait()
    rows, lanes = fb.shape[2], fb.shape[3]
    row = lax.broadcasted_iota(jnp.int32, (rows, lanes), 0)
    lane = lax.broadcasted_iota(jnp.int32, (rows, lanes), 1)
    half_y = jnp.broadcast_to(0.5 * metric(ly_ref[...]), (8, rows))
    upright = jnp.transpose(jnp.concatenate([zlo_ref[...], zhi_ref[...], half_y], axis=0))
    my = jnp.broadcast_to(upright[:, 8:9], (rows, lanes))
    mz = 0.5 * metric(lz_ref[...])

    def d_y(f, at):
        up = jnp.where(row == rows - 1, yhi_ref[at : at + 1, :], pltpu.roll(f, rows - 1, 0))
        down = jnp.where(row == 0, ylo_ref[at : at + 1, :], pltpu.roll(f, 1, 0))
        return (up - down) * my

    def d_z(f, at):
        up = jnp.where(lane == lanes - 1, upright[:, 4 + at : 5 + at], pltpu.roll(f, lanes - 1, 1))
        down = jnp.where(lane == 0, upright[:, at : at + 1], pltpu.roll(f, 1, 1))
        return (up - down) * mz

    copies[2].wait()
    copies[3].wait()
    for p in range(2):
        b_x, b_y, b_z = fb[0, p], fb[1, p], fb[2, p]
        half = 0.5 if p == 0 else -0.5
        cur_x = d_y(b_z, 2 + p) - d_z(b_y, 2 + p)
        cur_y = d_z(b_x, p) - half * fb[2, 1 - p]
        cur_z = half * fb[1, 1 - p] - d_y(b_x, p)
        dens = den[p]
        parts = (
            (cur_y * b_z - cur_z * b_y) / dens,
            (cur_z * b_x - cur_x * b_z) / dens,
            (cur_x * b_y - cur_y * b_x) / dens,
        )
        for comp in range(3):
            value = parts[comp].astype(BF)
            emf_ref[comp, p] = value
            at = 16 * (2 * comp + p)
            for block in range(4):
                for copy in range(4):
                    msg_ref[4 * block + copy, at : at + 16, :] = value[16 * block : 16 * block + 16]


def z_kernel(x_ref, table_ref, out_ref, mix_ref):
    zero = jnp.zeros((32, 512), BF)
    total = None
    for n in range(4):
        lines = jnp.concatenate([x_ref[4 * n + i] for i in range(4)], axis=1)
        lines = jnp.concatenate([lines, zero], axis=0)
        blocks = []
        for c in range(2):
            for kappa in range(16):
                turns = [(kappa * i + 4 * c) % 16 for i in range(4 * n, 4 * n + 4)]
                cells = [table_ref[m % 8, 16 * kappa : 16 * kappa + 16, :] for m in turns]
                blocks.append(jnp.concatenate([-x if m >= 8 else x for m, x in zip(turns, cells)], axis=1))
        product = lax.dot_general(jnp.concatenate(blocks, axis=0), lines, ACROSS, preferred_element_type=F32)
        total = product if n == 0 else total + product
    for c in range(2):
        for kappa in range(16):
            spot = 4 * (kappa // 2) + 2 * c + kappa % 2
            at = 16 * (16 * c + kappa)
            mix_ref[pl.ds(spot, 16, stride=32), :] = total[at : at + 16]
    out_ref[...] = mix_ref[...].astype(BF)


def add(a, b):
    return (a[0] + b[0], a[1] + b[1])


def sub(a, b):
    return (a[0] - b[0], a[1] - b[1])


def turned(a, eighths):
    eighths %= 16
    if eighths == 0:
        return a
    if eighths == 4:
        return (a[1], -a[0])
    if eighths == 2:
        r = math.sqrt(0.5)
        return ((a[0] + a[1]) * r, (a[1] - a[0]) * r)
    if eighths == 6:
        r = math.sqrt(0.5)
        return ((a[1] - a[0]) * r, -(a[0] + a[1]) * r)
    cos, sin = math.cos(math.pi * eighths / 8), math.sin(math.pi * eighths / 8)
    return (a[0] * cos + a[1] * sin, a[1] * cos - a[0] * sin)


def fourier4(x):
    s, d = add(x[0], x[2]), sub(x[0], x[2])
    t, u = add(x[1], x[3]), turned(sub(x[1], x[3]), 4)
    return [add(s, t), add(d, u), sub(s, t), sub(d, u)]


def fourier16(x):
    inner = [fourier4([x[4 * i + n] for i in range(4)]) for n in range(4)]
    out = [None] * 16
    for k in range(4):
        for b, value in enumerate(fourier4([turned(inner[n][k], n * k) for n in range(4)])):
            out[k + 4 * b] = value
    return out


def y_kernel(x_ref, table_ref, turn_ref, order_ref, bins_ref, power_ref, sums_ref):
    lhs = lax.dot_general(order_ref[...], x_ref[...], ACROSS, preferred_element_type=F32).astype(BF)
    product = jnp.dot(lhs, table_ref[...], preferred_element_type=F32)
    scale = 1.0 / (6.0 * NY)
    for e in range(2):
        held = []
        for y0 in range(16):
            a = product[8 * y0 : 8 * y0 + 8, 256 * e : 256 * e + 128]
            b = product[8 * y0 : 8 * y0 + 8, 256 * e + 128 : 256 * e + 256]
            if y0 > 0:
                cos, sin = turn_ref[0, y0 : y0 + 1, :], turn_ref[1, y0 : y0 + 1, :]
                a, b = a * cos + b * sin, b * cos - a * sin
            held.append((a, b))
        for q1, (a, b) in enumerate(fourier16(held)):
            power_ref[e : e + 1, 128 * q1 : 128 * q1 + 128] = (
                jnp.sum(a * a + b * b, axis=0, keepdims=True) * scale
            )
    sums = jnp.zeros((8, 128), F32)
    for e in range(2):
        value = power_ref[e : e + 1, :]
        bins = bins_ref[e : e + 1, :]
        coarse = lax.broadcasted_iota(jnp.int32, (8, NY), 0) == (bins >> 7)
        fine = (lax.broadcasted_iota(jnp.int32, (128, NY), 0) == (bins & 127)).astype(F32).astype(BF)
        spread = jnp.where(coarse, value, 0.0)
        first = spread.astype(BF)
        spread = spread - first.astype(F32)
        second = spread.astype(BF)
        third = (spread - second.astype(F32)).astype(BF)
        for piece in (third, second, first):
            sums += lax.dot_general(piece, fine, ACROSS, preferred_element_type=F32)
    sums = sums * (NB / (KZ * NY))
    for copy in range(sums_ref.shape[0]):
        sums_ref[copy] = sums


def on_device(field_b, density, level_y, level_z, bins):
    y_local, z_local = field_b.shape[2], field_b.shape[3]

    def shift(cells, axis, step):
        count = lax.axis_size(axis)
        return lax.ppermute(cells, axis, [(i, (i + step) % count) for i in range(count)])

    zlo = shift(field_b[0:2, :, :, z_local - 1].reshape(4, y_local), GZ, 1)
    zhi = shift(field_b[0:2, :, :, 0].reshape(4, y_local), GZ, -1)
    ylo = shift(field_b[0::2, :, y_local - 1, :].reshape(4, z_local), GY, 1)
    yhi = shift(field_b[0::2, :, 0, :].reshape(4, z_local), GY, -1)
    small = pltpu.CompilerParams(vmem_limit_bytes=16 * 2**20)
    far = [
        pltpu.with_memory_space_constraint(x, pltpu.HBM)
        for x in (field_b, density, level_y[None, :], level_z[None, :])
    ]
    emf, message = pl.pallas_call(
        emf_kernel,
        out_shape=(
            jax.ShapeDtypeStruct(field_b.shape, BF),
            jax.ShapeDtypeStruct((16, 96, z_local), BF),
        ),
        in_specs=[pl.BlockSpec(memory_space=pltpu.HBM)] * 4 + [pl.BlockSpec(memory_space=pltpu.VMEM)] * 4,
        scratch_shapes=[
            pltpu.VMEM(field_b.shape, F32),
            pltpu.VMEM(density.shape, F32),
            pltpu.VMEM((1, y_local), jnp.int32),
            pltpu.VMEM((1, z_local), jnp.int32),
            pltpu.SemaphoreType.DMA((4,)),
        ],
        compiler_params=small,
    )(*far, ylo, yhi, zlo, zhi)
    part = lax.axis_index("yl") * 2 + lax.axis_index("xh")
    quarter = lax.dynamic_index_in_dim(jnp.asarray(z_table()), part, keepdims=False)
    lines = lax.all_to_all(message, GZ, 0, 0, tiled=True)
    z_modes = pl.pallas_call(
        z_kernel,
        out_shape=jax.ShapeDtypeStruct((512, 128), BF),
        scratch_shapes=[pltpu.VMEM((512, 128), F32)],
        compiler_params=small,
    )(lines, quarter)
    spread = lax.all_to_all(z_modes.reshape(128, 4, 128), ("yh",) + GY, 0, 0, tiled=True).reshape(512, 128)
    first = ("yh", "yl", "c")
    second = ("xh", "z", "xl")
    mode_power, sums = pl.pallas_call(
        y_kernel,
        out_shape=(
            jax.ShapeDtypeStruct((2, NY), F32),
            jax.ShapeDtypeStruct((lax.axis_size(first), 8, 128), F32),
        ),
        compiler_params=small,
    )(spread, *y_tables(), bins)
    sums = jnp.sum(lax.all_to_all(sums, first, 0, 0, tiled=True), axis=0)
    copies = jnp.broadcast_to(sums[None], (lax.axis_size(second), 8, 128))
    spectrum = jnp.sum(lax.all_to_all(copies, second, 0, 0, tiled=True), axis=0).reshape(NB)
    return (emf, mode_power, spectrum)


def solution(mesh):
    fine = Mesh(mesh.devices.reshape(4, 2, 2, 8, 2, 2), GZ + GY)
    placed = (
        P(None, None, GY, GZ),
        P(None, GY, GZ),
        P(GY),
        P(GZ),
        P(GZ + GY, None),
    )
    return jax.shard_map(
        on_device,
        mesh=fine,
        in_specs=placed,
        out_specs=(P(None, None, GY, GZ), P(GZ + GY, None), P()),
        check_vma=False,
    )
```

```python
import math

import jax
import jax.numpy as jnp
import numpy as np
from jax import lax
from jax.experimental import pallas as pl
from jax.experimental.pallas import tpu as pltpu
from jax.sharding import Mesh, PartitionSpec as P

NY = 2048
NZ = 2048
NB = 1024
KZ = 1024
BF = jnp.bfloat16
F32 = jnp.float32
GZ = ("yh", "yl", "xh")
GY = ("z", "xl", "c")
ACROSS = (((1,), (1,)), ((), ()))


def angle(a, b, length):
    return 2.0 * math.pi * ((a[:, None] * b[None, :]) % length) / length


def z_table():
    part, kappa, yh, jh = np.meshgrid(*(np.arange(n) for n in (4, 16, 4, 4)), indexing="ij")
    modes = (16 * (16 * yh + 4 * part + jh) + kappa).reshape(4, 1, 256, 1)
    turn = (modes * np.arange(128) % NZ + 128 * np.arange(8).reshape(1, 8, 1, 1)) % NZ
    return (np.cos(2.0 * math.pi * turn / NZ) / math.sqrt(NZ)).astype(jnp.bfloat16)


def y_tables():
    inner = angle((4 * np.arange(32)[None, :] + np.arange(4)[:, None]).reshape(-1), np.arange(128), 128)
    table = np.zeros((128, 2, 2, 2, 2, 128))
    for e in range(2):
        table[:, 0, e, e, 0] = np.cos(inner)
        table[:, 0, e, e, 1] = -np.sin(inner)
        table[:, 1, e, e, 0] = np.sin(inner)
        table[:, 1, e, e, 1] = np.cos(inner)
    turn = angle(np.arange(16), np.arange(128), NY)
    order = np.zeros((128, 128), np.float32)
    for cp in range(6):
        for y0 in range(16):
            order[y0 * 8 + cp, cp * 16 + y0] = 1.0
    return (
        table.reshape(512, 512).astype(jnp.bfloat16),
        np.stack([np.cos(turn), np.sin(turn)]).astype(np.float32),
        order.astype(jnp.bfloat16),
    )


def metric(level):
    return 1.0 / (1.0 + 0.25 * level.astype(F32))


def roll(x, by, axis):
    return pltpu.roll(x, by % x.shape[axis], axis)


def hall(p, fb, den, my, mz, ylo_ref, yhi_ref, zlo, zhi):
    rows, lanes = fb.shape[2], fb.shape[3]
    row = lax.broadcasted_iota(jnp.int32, (rows, lanes), 0)
    lane = lax.broadcasted_iota(jnp.int32, (rows, lanes), 1)

    def d_y(f, at):
        up = jnp.where(row == rows - 1, yhi_ref[at : at + 1, :], roll(f, -1, 0))
        down = jnp.where(row == 0, ylo_ref[at : at + 1, :], roll(f, 1, 0))
        return (up - down) * my

    def d_z(f, at):
        up = jnp.where(lane == lanes - 1, zhi[at], roll(f, -1, 1))
        down = jnp.where(lane == 0, zlo[at], roll(f, 1, 1))
        return (up - down) * mz

    b_x, b_y, b_z = fb[0, p], fb[1, p], fb[2, p]
    half = 0.5 if p == 0 else -0.5
    cur_x = d_y(b_z, 2 + p) - d_z(b_y, 2 + p)
    cur_y = d_z(b_x, p) - half * fb[2, 1 - p]
    cur_z = half * fb[1, 1 - p] - d_y(b_x, p)
    dens = den[p]
    return (
        (cur_y * b_z - cur_z * b_y) / dens,
        (cur_z * b_x - cur_x * b_z) / dens,
        (cur_x * b_y - cur_y * b_x) / dens,
    )


def fetched(far, near, sems):
    copies = [pltpu.make_async_copy(a, b, sems.at[n]) for n, (a, b) in enumerate(zip(far, near))]
    for copy in copies:
        copy.start()
    for copy in copies:
        copy.wait()


def metrics(ly_ref, lz_ref, shape):
    half_y = jnp.broadcast_to(0.5 * metric(ly_ref[...]), (8, shape[0]))
    return jnp.broadcast_to(jnp.transpose(half_y)[:, 0:1], shape), 0.5 * metric(lz_ref[...])


def message_kernel(*refs):
    far, (ylo_ref, yhi_ref, msg_ref), near, sems = refs[0:4], refs[4:7], refs[7:11], refs[11]
    fetched(far, near, sems)
    ly_ref, lz_ref, fb, den = near
    shape = fb.shape[2:]
    my, mz = metrics(ly_ref, lz_ref, shape)
    lane = lax.broadcasted_iota(jnp.int32, shape, 1)
    edge = (lane == 0) | (lane == 127)
    slot = (lane + 1) >> 1
    signed = jnp.where(lane == 0, -mz, mz)
    none = [0.0] * 4
    held = jnp.zeros(shape, F32)
    own = jnp.zeros(shape, F32)
    for p in range(2):
        parts = hall(p, fb, den, my, mz, ylo_ref, yhi_ref, none, none)
        weight = signed / den[p]
        fields = [fb[comp, p] for comp in range(3)]
        for comp in range(3):
            value = jnp.where(edge, 0.0, parts[comp]).astype(BF)
            at = 16 * (2 * comp + p)
            for block in range(4):
                for copy in range(4):
                    msg_ref[4 * block + copy, at : at + 16, :] = value[16 * block : 16 * block + 16]
        terms = list(parts) + [f * weight for f in fields] + fields[0:2]
        for q, term in enumerate(terms):
            k = 8 * p + q + 1
            held = jnp.where(slot == k, roll(term, 2 * k, 1), held)
        for comp in range(2):
            k = 2 * p + comp + 1
            own = jnp.where(slot == k, roll(fields[comp], 2 * k, 1), own)
    high = held.astype(BF).astype(F32)
    low = (held - high).astype(BF).astype(F32)
    held = (high + roll(low, 64, 1)).astype(BF)
    first = own.astype(BF).astype(F32)
    own = own - first
    second = own.astype(BF).astype(F32)
    own = first + roll(second, 8, 1) + roll(own - second, 16, 1)
    folded = own[0:16]
    for block in range(1, 4):
        folded = folded + roll(own[16 * block : 16 * block + 16], 32 * block, 1)
    folded = folded.astype(BF)
    for block in range(4):
        for copy in range(4):
            msg_ref[4 * block + copy, 96:112, :] = held[16 * block : 16 * block + 16]
            msg_ref[4 * block + copy, 112:128, :] = folded


def emf_kernel(*refs):
    far, (ylo_ref, yhi_ref, lines_ref, emf_ref), near, sems = refs[0:4], refs[4:8], refs[8:12], refs[12]
    fetched(far, near, sems)
    ly_ref, lz_ref, fb, den = near
    my, mz = metrics(ly_ref, lz_ref, fb.shape[2:])
    me = lax.axis_index("yh") * 4 + lax.axis_index("yl") * 2 + lax.axis_index("xh")

    def columns(block, side):
        folded = lines_ref[block, 112:128, :].astype(F32)
        rows = []
        for n in range(4):
            own = roll(folded, -32 * n, 1)
            rows.append(own + (roll(own, -8, 1) + roll(own, -16, 1)))
        rows = jnp.concatenate(rows, axis=0)
        at = [2 * (2 * p + comp + 1) - side for comp in range(2) for p in range(2)]
        return [rows[:, n : n + 1] for n in at]

    zlo = columns(lax.rem(me + 15, 16), 1)
    zhi = columns(lax.rem(me + 1, 16), 0)
    for p in range(2):
        parts = hall(p, fb, den, my, mz, ylo_ref, yhi_ref, zlo, zhi)
        for comp in range(3):
            emf_ref[comp, p] = parts[comp].astype(BF)


def finished_edges(x_ref):
    held = jnp.concatenate([x_ref[i, 96:112, :] for i in range(16)], axis=0).astype(F32)
    held = held + roll(held, 64, 1)
    lane = lax.broadcasted_iota(jnp.int32, held.shape, 1)
    slot = ((lane + 1) >> 1) & 7
    beside = jnp.where((lane & 1) == 1, roll(roll(held, -16, 0), -1, 1), roll(roll(held, 16, 0), 1, 1))
    flat = roll(beside, -12, 1) * jnp.where(slot == 1, roll(held, -10, 1), roll(held, -8, 1))
    upright = roll(beside, -10, 1) * roll(held, -4, 1) + roll(beside, -8, 1) * roll(held, -2, 1)
    held = held + jnp.where(slot == 3, -upright, flat)
    edge = (lane == 0) | (lane == 127)
    out = []
    for comp in range(3):
        for p in range(2):
            k = 8 * p + comp + 1
            out.append(jnp.where(edge, roll(held, -2 * k, 1), 0.0).astype(BF))
    return out


def z_kernel(x_ref, table_ref, out_ref, mix_ref):
    edges = finished_edges(x_ref)
    zero = jnp.zeros((32, 512), BF)
    total = None
    for n in range(4):
        lines = []
        for i in range(4 * n, 4 * n + 4):
            lines.append(x_ref[i, 0:96, :] + jnp.concatenate([x[16 * i : 16 * i + 16] for x in edges], axis=0))
        lines = jnp.concatenate([jnp.concatenate(lines, axis=1), zero], axis=0)
        blocks = []
        for c in range(2):
            for kappa in range(16):
                turns = [(kappa * i + 4 * c) % 16 for i in range(4 * n, 4 * n + 4)]
                cells = [table_ref[m % 8, 16 * kappa : 16 * kappa + 16, :] for m in turns]
                blocks.append(jnp.concatenate([-x if m >= 8 else x for m, x in zip(turns, cells)], axis=1))
        product = lax.dot_general(jnp.concatenate(blocks, axis=0), lines, ACROSS, preferred_element_type=F32)
        total = product if n == 0 else total + product
    for c in range(2):
        for kappa in range(16):
            spot = 4 * (kappa // 2) + 2 * c + kappa % 2
            at = 16 * (16 * c + kappa)
            mix_ref[pl.ds(spot, 16, stride=32), :] = total[at : at + 16]
    out_ref[...] = mix_ref[...].astype(BF)


def add(a, b):
    return (a[0] + b[0], a[1] + b[1])


def sub(a, b):
    return (a[0] - b[0], a[1] - b[1])


def turned(a, eighths):
    eighths %= 16
    if eighths == 0:
        return a
    if eighths == 4:
        return (a[1], -a[0])
    if eighths == 2:
        r = math.sqrt(0.5)
        return ((a[0] + a[1]) * r, (a[1] - a[0]) * r)
    if eighths == 6:
        r = math.sqrt(0.5)
        return ((a[1] - a[0]) * r, -(a[0] + a[1]) * r)
    cos, sin = math.cos(math.pi * eighths / 8), math.sin(math.pi * eighths / 8)
    return (a[0] * cos + a[1] * sin, a[1] * cos - a[0] * sin)


def fourier4(x):
    s, d = add(x[0], x[2]), sub(x[0], x[2])
    t, u = add(x[1], x[3]), turned(sub(x[1], x[3]), 4)
    return [add(s, t), add(d, u), sub(s, t), sub(d, u)]


def fourier16(x):
    inner = [fourier4([x[4 * i + n] for i in range(4)]) for n in range(4)]
    out = [None] * 16
    for k in range(4):
        for b, value in enumerate(fourier4([turned(inner[n][k], n * k) for n in range(4)])):
            out[k + 4 * b] = value
    return out


def y_kernel(x_ref, table_ref, turn_ref, order_ref, bins_ref, power_ref, sums_ref):
    lhs = lax.dot_general(order_ref[...], x_ref[...], ACROSS, preferred_element_type=F32).astype(BF)
    product = jnp.dot(lhs, table_ref[...], preferred_element_type=F32)
    scale = 1.0 / (6.0 * NY)
    for e in range(2):
        held = []
        for y0 in range(16):
            a = product[8 * y0 : 8 * y0 + 8, 256 * e : 256 * e + 128]
            b = product[8 * y0 : 8 * y0 + 8, 256 * e + 128 : 256 * e + 256]
            if y0 > 0:
                cos, sin = turn_ref[0, y0 : y0 + 1, :], turn_ref[1, y0 : y0 + 1, :]
                a, b = a * cos + b * sin, b * cos - a * sin
            held.append((a, b))
        for q1, (a, b) in enumerate(fourier16(held)):
            power_ref[e : e + 1, 128 * q1 : 128 * q1 + 128] = (
                jnp.sum(a * a + b * b, axis=0, keepdims=True) * scale
            )
    sums = jnp.zeros((8, 128), F32)
    for e in range(2):
        value = power_ref[e : e + 1, :]
        bins = bins_ref[e : e + 1, :]
        coarse = lax.broadcasted_iota(jnp.int32, (8, NY), 0) == (bins >> 7)
        fine = (lax.broadcasted_iota(jnp.int32, (128, NY), 0) == (bins & 127)).astype(F32).astype(BF)
        spread = jnp.where(coarse, value, 0.0)
        first = spread.astype(BF)
        spread = spread - first.astype(F32)
        second = spread.astype(BF)
        third = (spread - second.astype(F32)).astype(BF)
        for piece in (third, second, first):
            sums += lax.dot_general(piece, fine, ACROSS, preferred_element_type=F32)
    sums = sums * (NB / (KZ * NY))
    for copy in range(sums_ref.shape[0]):
        sums_ref[copy] = sums


def on_device(field_b, density, level_y, level_z, bins):
    y_local, z_local = field_b.shape[2], field_b.shape[3]

    def shift(cells, axis, step):
        count = lax.axis_size(axis)
        return lax.ppermute(cells, axis, [(i, (i + step) % count) for i in range(count)])

    ylo = shift(field_b[0::2, :, y_local - 1, :].reshape(4, z_local), GY, 1)
    yhi = shift(field_b[0::2, :, 0, :].reshape(4, z_local), GY, -1)
    small = pltpu.CompilerParams(vmem_limit_bytes=16 * 2**20)
    far = [
        pltpu.with_memory_space_constraint(x, pltpu.HBM)
        for x in (level_y[None, :], level_z[None, :], field_b, density)
    ]
    scratch = [
        pltpu.VMEM((1, y_local), jnp.int32),
        pltpu.VMEM((1, z_local), jnp.int32),
        pltpu.VMEM(field_b.shape, F32),
        pltpu.VMEM(density.shape, F32),
        pltpu.SemaphoreType.DMA((4,)),
    ]
    message = pl.pallas_call(
        message_kernel,
        out_shape=jax.ShapeDtypeStruct((16, 128, z_local), BF),
        in_specs=[pl.BlockSpec(memory_space=pltpu.HBM)] * 4 + [pl.BlockSpec(memory_space=pltpu.VMEM)] * 2,
        scratch_shapes=scratch,
        compiler_params=small,
    )(*far, ylo, yhi)
    part = lax.axis_index("yl") * 2 + lax.axis_index("xh")
    quarter = lax.dynamic_index_in_dim(jnp.asarray(z_table()), part, keepdims=False)
    lines = lax.all_to_all(message, GZ, 0, 0, tiled=True)
    z_modes = pl.pallas_call(
        z_kernel,
        out_shape=jax.ShapeDtypeStruct((512, 128), BF),
        scratch_shapes=[pltpu.VMEM((512, 128), F32)],
        compiler_params=small,
    )(lines, quarter)
    emf = pl.pallas_call(
        emf_kernel,
        out_shape=jax.ShapeDtypeStruct(field_b.shape, BF),
        in_specs=[pl.BlockSpec(memory_space=pltpu.HBM)] * 4 + [pl.BlockSpec(memory_space=pltpu.VMEM)] * 3,
        scratch_shapes=scratch,
        compiler_params=small,
        cost_estimate=pl.CostEstimate(flops=2_000_000, bytes_accessed=1_000_000, transcendentals=0),
    )(*far, ylo, yhi, lines)
    spread = lax.all_to_all(z_modes.reshape(128, 4, 128), ("yh",) + GY, 0, 0, tiled=True).reshape(512, 128)
    first = ("yh", "yl", "c")
    second = ("xh", "z", "xl")
    mode_power, sums = pl.pallas_call(
        y_kernel,
        out_shape=(
            jax.ShapeDtypeStruct((2, NY), F32),
            jax.ShapeDtypeStruct((lax.axis_size(first), 8, 128), F32),
        ),
        compiler_params=small,
    )(spread, *y_tables(), bins)
    sums = jnp.sum(lax.all_to_all(sums, first, 0, 0, tiled=True), axis=0)
    copies = jnp.broadcast_to(sums[None], (lax.axis_size(second), 8, 128))
    spectrum = jnp.sum(lax.all_to_all(copies, second, 0, 0, tiled=True), axis=0).reshape(NB)
    return (emf, mode_power, spectrum)


def solution(mesh):
    fine = Mesh(mesh.devices.reshape(4, 2, 2, 8, 2, 2), GZ + GY)
    placed = (
        P(None, None, GY, GZ),
        P(None, GY, GZ),
        P(GY),
        P(GZ),
        P(GZ + GY, None),
    )
    return jax.shard_map(
        on_device,
        mesh=fine,
        in_specs=placed,
        out_specs=(P(None, None, GY, GZ), P(GZ + GY, None), P()),
        check_vma=False,
    )
```

```python
import math

import jax
import jax.numpy as jnp
import numpy as np
from jax import lax
from jax.experimental import pallas as pl
from jax.experimental.pallas import tpu as pltpu
from jax.sharding import Mesh, PartitionSpec as P

NY = 2048
NZ = 2048
NB = 1024
KZ = 1024
BF = jnp.bfloat16
F32 = jnp.float32
GZ = ("yh", "yl", "xh")
GY = ("z", "xl", "c")
ACROSS = (((1,), (1,)), ((), ()))


def angle(a, b, length):
    return 2.0 * math.pi * ((a[:, None] * b[None, :]) % length) / length


def z_table():
    part, kappa, yh, jh = np.meshgrid(*(np.arange(n) for n in (4, 16, 4, 4)), indexing="ij")
    modes = (16 * (16 * yh + 4 * part + jh) + kappa).reshape(4, 1, 256, 1)
    turn = (modes * np.arange(128) % NZ + 128 * np.arange(8).reshape(1, 8, 1, 1)) % NZ
    return (np.cos(2.0 * math.pi * turn / NZ) / math.sqrt(NZ)).astype(jnp.bfloat16)


def y_tables():
    inner = angle((4 * np.arange(32)[None, :] + np.arange(4)[:, None]).reshape(-1), np.arange(128), 128)
    table = np.zeros((128, 2, 2, 2, 2, 128))
    for e in range(2):
        table[:, 0, e, e, 0] = np.cos(inner)
        table[:, 0, e, e, 1] = -np.sin(inner)
        table[:, 1, e, e, 0] = np.sin(inner)
        table[:, 1, e, e, 1] = np.cos(inner)
    turn = angle(np.arange(16), np.arange(128), NY)
    order = np.zeros((128, 128), np.float32)
    for cp in range(6):
        for y0 in range(16):
            order[y0 * 8 + cp, cp * 16 + y0] = 1.0
    return (
        table.reshape(512, 512).astype(jnp.bfloat16),
        np.stack([np.cos(turn), np.sin(turn)]).astype(np.float32),
        order.astype(jnp.bfloat16),
    )


def metric(level):
    return 1.0 / (1.0 + 0.25 * level.astype(F32))


def roll(x, by, axis):
    return pltpu.roll(x, by % x.shape[axis], axis)


def hall(p, fb, den, my, mz, ylo_ref, yhi_ref, zlo, zhi):
    rows, lanes = fb.shape[2], fb.shape[3]
    row = lax.broadcasted_iota(jnp.int32, (rows, lanes), 0)
    lane = lax.broadcasted_iota(jnp.int32, (rows, lanes), 1)

    def d_y(f, at):
        up = jnp.where(row == rows - 1, yhi_ref[at : at + 1, :], roll(f, -1, 0))
        down = jnp.where(row == 0, ylo_ref[at : at + 1, :], roll(f, 1, 0))
        return (up - down) * my

    def d_z(f, at):
        up = jnp.where(lane == lanes - 1, zhi[at], roll(f, -1, 1))
        down = jnp.where(lane == 0, zlo[at], roll(f, 1, 1))
        return (up - down) * mz

    b_x, b_y, b_z = fb[0, p], fb[1, p], fb[2, p]
    half = 0.5 if p == 0 else -0.5
    cur_x = d_y(b_z, 2 + p) - d_z(b_y, 2 + p)
    cur_y = d_z(b_x, p) - half * fb[2, 1 - p]
    cur_z = half * fb[1, 1 - p] - d_y(b_x, p)
    dens = den[p]
    return (
        (cur_y * b_z - cur_z * b_y) / dens,
        (cur_z * b_x - cur_x * b_z) / dens,
        (cur_x * b_y - cur_y * b_x) / dens,
    )


def fetched(far, near, sems):
    copies = [pltpu.make_async_copy(a, b, sems.at[n]) for n, (a, b) in enumerate(zip(far, near))]
    for copy in copies:
        copy.start()
    for copy in copies:
        copy.wait()


def metrics(ly_ref, lz_ref, shape):
    half_y = jnp.broadcast_to(0.5 * metric(ly_ref[...]), (8, shape[0]))
    return jnp.broadcast_to(jnp.transpose(half_y)[:, 0:1], shape), 0.5 * metric(lz_ref[...])


def message_kernel(*refs):
    far, (ylo_ref, yhi_ref, msg_ref), near, sems = refs[0:4], refs[4:7], refs[7:11], refs[11]
    fetched(far, near, sems)
    ly_ref, lz_ref, fb, den = near
    shape = fb.shape[2:]
    my, mz = metrics(ly_ref, lz_ref, shape)
    lane = lax.broadcasted_iota(jnp.int32, shape, 1)
    edge = (lane == 0) | (lane == 127)
    slot = (lane + 1) >> 1
    signed = jnp.where(lane == 0, -mz, mz)
    none = [0.0] * 4
    held = jnp.zeros(shape, F32)
    own = jnp.zeros(shape, F32)
    for p in range(2):
        parts = hall(p, fb, den, my, mz, ylo_ref, yhi_ref, none, none)
        weight = signed / den[p]
        fields = [fb[comp, p] for comp in range(3)]
        for comp in range(3):
            value = jnp.where(edge, 0.0, parts[comp]).astype(BF)
            at = 16 * (2 * comp + p)
            for block in range(4):
                for copy in range(4):
                    msg_ref[4 * block + copy, at : at + 16, :] = value[16 * block : 16 * block + 16]
        terms = list(parts) + [f * weight for f in fields] + fields[0:2]
        for q, term in enumerate(terms):
            k = 8 * p + q + 1
            held = jnp.where(slot == k, roll(term, 2 * k, 1), held)
        for comp in range(2):
            k = 2 * p + comp + 1
            own = jnp.where(slot == k, roll(fields[comp], 2 * k, 1), own)
    high = held.astype(BF).astype(F32)
    low = (held - high).astype(BF).astype(F32)
    held = (high + roll(low, 64, 1)).astype(BF)
    first = own.astype(BF).astype(F32)
    own = own - first
    second = own.astype(BF).astype(F32)
    own = first + roll(second, 8, 1) + roll(own - second, 16, 1)
    folded = own[0:16]
    for block in range(1, 4):
        folded = folded + roll(own[16 * block : 16 * block + 16], 32 * block, 1)
    folded = folded.astype(BF)
    for block in range(4):
        for copy in range(4):
            msg_ref[4 * block + copy, 96:112, :] = held[16 * block : 16 * block + 16]
            msg_ref[4 * block + copy, 112:128, :] = folded


def emf_kernel(*refs):
    far, (ylo_ref, yhi_ref, lines_ref, emf_ref), near, sems = refs[0:4], refs[4:8], refs[8:12], refs[12]
    fetched(far, near, sems)
    ly_ref, lz_ref, fb, den = near
    my, mz = metrics(ly_ref, lz_ref, fb.shape[2:])
    me = lax.axis_index("yh") * 4 + lax.axis_index("yl") * 2 + lax.axis_index("xh")

    def columns(block, side):
        folded = lines_ref[block, 112:128, :].astype(F32)
        rows = []
        for n in range(4):
            own = roll(folded, -32 * n, 1)
            rows.append(own + (roll(own, -8, 1) + roll(own, -16, 1)))
        rows = jnp.concatenate(rows, axis=0)
        at = [2 * (2 * p + comp + 1) - side for comp in range(2) for p in range(2)]
        return [rows[:, n : n + 1] for n in at]

    zlo = columns(lax.rem(me + 15, 16), 1)
    zhi = columns(lax.rem(me + 1, 16), 0)
    for p in range(2):
        parts = hall(p, fb, den, my, mz, ylo_ref, yhi_ref, zlo, zhi)
        for comp in range(3):
            emf_ref[comp, p] = parts[comp].astype(BF)


def finished_edges(x_ref):
    held = jnp.concatenate([x_ref[i, 96:112, :] for i in range(16)], axis=0).astype(F32)
    held = held + roll(held, 64, 1)
    lane = lax.broadcasted_iota(jnp.int32, held.shape, 1)
    slot = ((lane + 1) >> 1) & 7
    beside = jnp.where((lane & 1) == 1, roll(roll(held, -16, 0), -1, 1), roll(roll(held, 16, 0), 1, 1))
    flat = roll(beside, -12, 1) * jnp.where(slot == 1, roll(held, -10, 1), roll(held, -8, 1))
    upright = roll(beside, -10, 1) * roll(held, -4, 1) + roll(beside, -8, 1) * roll(held, -2, 1)
    held = held + jnp.where(slot == 3, -upright, flat)
    edge = (lane == 0) | (lane == 127)
    out = []
    for comp in range(3):
        for p in range(2):
            k = 8 * p + comp + 1
            out.append(jnp.where(edge, roll(held, -2 * k, 1), 0.0).astype(BF))
    return out


def z_kernel(x_ref, table_ref, out_ref, mix_ref):
    edges = finished_edges(x_ref)
    zero = jnp.zeros((32, 512), BF)
    total = None
    for n in range(4):
        lines = []
        for i in range(4 * n, 4 * n + 4):
            lines.append(x_ref[i, 0:96, :] + jnp.concatenate([x[16 * i : 16 * i + 16] for x in edges], axis=0))
        lines = jnp.concatenate([jnp.concatenate(lines, axis=1), zero], axis=0)
        blocks = []
        for c in range(2):
            for kappa in range(16):
                turns = [(kappa * i + 4 * c) % 16 for i in range(4 * n, 4 * n + 4)]
                cells = [table_ref[m % 8, 16 * kappa : 16 * kappa + 16, :] for m in turns]
                blocks.append(jnp.concatenate([-x if m >= 8 else x for m, x in zip(turns, cells)], axis=1))
        product = lax.dot_general(jnp.concatenate(blocks, axis=0), lines, ACROSS, preferred_element_type=F32)
        total = product if n == 0 else total + product
    for c in range(2):
        for kappa in range(16):
            spot = 4 * (kappa // 2) + 2 * c + kappa % 2
            at = 16 * (16 * c + kappa)
            mix_ref[pl.ds(spot, 16, stride=32), :] = total[at : at + 16]
    out_ref[...] = mix_ref[...].astype(BF)


def add(a, b):
    return (a[0] + b[0], a[1] + b[1])


def sub(a, b):
    return (a[0] - b[0], a[1] - b[1])


def turned(a, eighths):
    eighths %= 16
    if eighths == 0:
        return a
    if eighths == 4:
        return (a[1], -a[0])
    if eighths == 2:
        r = math.sqrt(0.5)
        return ((a[0] + a[1]) * r, (a[1] - a[0]) * r)
    if eighths == 6:
        r = math.sqrt(0.5)
        return ((a[1] - a[0]) * r, -(a[0] + a[1]) * r)
    cos, sin = math.cos(math.pi * eighths / 8), math.sin(math.pi * eighths / 8)
    return (a[0] * cos + a[1] * sin, a[1] * cos - a[0] * sin)


def fourier4(x):
    s, d = add(x[0], x[2]), sub(x[0], x[2])
    t, u = add(x[1], x[3]), turned(sub(x[1], x[3]), 4)
    return [add(s, t), add(d, u), sub(s, t), sub(d, u)]


def fourier16(x):
    inner = [fourier4([x[4 * i + n] for i in range(4)]) for n in range(4)]
    out = [None] * 16
    for k in range(4):
        for b, value in enumerate(fourier4([turned(inner[n][k], n * k) for n in range(4)])):
            out[k + 4 * b] = value
    return out


def y_kernel(x_ref, table_ref, turn_ref, order_ref, bins_ref, power_ref, sums_ref):
    lhs = lax.dot_general(order_ref[...], x_ref[...], ACROSS, preferred_element_type=F32).astype(BF)
    product = jnp.dot(lhs, table_ref[...], preferred_element_type=F32)
    scale = 1.0 / (6.0 * NY)
    for e in range(2):
        held = []
        for y0 in range(16):
            a = product[8 * y0 : 8 * y0 + 8, 256 * e : 256 * e + 128]
            b = product[8 * y0 : 8 * y0 + 8, 256 * e + 128 : 256 * e + 256]
            if y0 > 0:
                cos, sin = turn_ref[0, y0 : y0 + 1, :], turn_ref[1, y0 : y0 + 1, :]
                a, b = a * cos + b * sin, b * cos - a * sin
            held.append((a, b))
        for q1, (a, b) in enumerate(fourier16(held)):
            power_ref[e : e + 1, 128 * q1 : 128 * q1 + 128] = (
                jnp.sum(a * a + b * b, axis=0, keepdims=True) * scale
            )
    sums = jnp.zeros((8, 128), F32)
    for e in range(2):
        value = power_ref[e : e + 1, :]
        bins = bins_ref[e : e + 1, :]
        coarse = lax.broadcasted_iota(jnp.int32, (8, NY), 0) == (bins >> 7)
        fine = (lax.broadcasted_iota(jnp.int32, (128, NY), 0) == (bins & 127)).astype(F32).astype(BF)
        spread = jnp.where(coarse, value, 0.0)
        first = spread.astype(BF)
        spread = spread - first.astype(F32)
        second = spread.astype(BF)
        third = (spread - second.astype(F32)).astype(BF)
        for piece in (third, second, first):
            sums += lax.dot_general(piece, fine, ACROSS, preferred_element_type=F32)
    sums = sums * (NB / (KZ * NY))
    for copy in range(sums_ref.shape[0]):
        sums_ref[copy] = sums


def on_device(field_b, density, level_y, level_z, bins):
    y_local, z_local = field_b.shape[2], field_b.shape[3]

    def shift(cells, axis, step):
        count = lax.axis_size(axis)
        return lax.ppermute(cells, axis, [(i, (i + step) % count) for i in range(count)])

    ylo = shift(field_b[0::2, :, y_local - 1, :].reshape(4, z_local), GY, 1)
    yhi = shift(field_b[0::2, :, 0, :].reshape(4, z_local), GY, -1)
    part = lax.axis_index("yl") * 2 + lax.axis_index("xh")
    quarter = lax.dynamic_index_in_dim(jnp.asarray(z_table()), part, keepdims=False)
    quarter, ylo, yhi = lax.optimization_barrier((quarter, ylo, yhi))
    small = pltpu.CompilerParams(vmem_limit_bytes=16 * 2**20)
    far = [
        pltpu.with_memory_space_constraint(x, pltpu.HBM)
        for x in (level_y[None, :], level_z[None, :], field_b, density)
    ]
    scratch = [
        pltpu.VMEM((1, y_local), jnp.int32),
        pltpu.VMEM((1, z_local), jnp.int32),
        pltpu.VMEM(field_b.shape, F32),
        pltpu.VMEM(density.shape, F32),
        pltpu.SemaphoreType.DMA((4,)),
    ]
    message = pl.pallas_call(
        message_kernel,
        out_shape=jax.ShapeDtypeStruct((16, 128, z_local), BF),
        in_specs=[pl.BlockSpec(memory_space=pltpu.HBM)] * 4 + [pl.BlockSpec(memory_space=pltpu.VMEM)] * 2,
        scratch_shapes=scratch,
        compiler_params=small,
    )(*far, ylo, yhi)
    lines = lax.all_to_all(message, GZ, 0, 0, tiled=True)
    z_modes = pl.pallas_call(
        z_kernel,
        out_shape=jax.ShapeDtypeStruct((512, 128), BF),
        scratch_shapes=[pltpu.VMEM((512, 128), F32)],
        compiler_params=small,
    )(lines, quarter)
    emf = pl.pallas_call(
        emf_kernel,
        out_shape=jax.ShapeDtypeStruct(field_b.shape, BF),
        in_specs=[pl.BlockSpec(memory_space=pltpu.HBM)] * 4 + [pl.BlockSpec(memory_space=pltpu.VMEM)] * 3,
        scratch_shapes=scratch,
        compiler_params=small,
        cost_estimate=pl.CostEstimate(flops=2_000_000, bytes_accessed=1_000_000, transcendentals=0),
    )(*far, ylo, yhi, lines)
    spread = lax.all_to_all(z_modes.reshape(128, 4, 128), ("yh",) + GY, 0, 0, tiled=True).reshape(512, 128)
    first = ("yh", "yl", "c")
    second = ("xh", "z", "xl")
    mode_power, sums = pl.pallas_call(
        y_kernel,
        out_shape=(
            jax.ShapeDtypeStruct((2, NY), F32),
            jax.ShapeDtypeStruct((lax.axis_size(first), 8, 128), F32),
        ),
        compiler_params=small,
    )(spread, *y_tables(), bins)
    sums = jnp.sum(lax.all_to_all(sums, first, 0, 0, tiled=True), axis=0)
    copies = jnp.broadcast_to(sums[None], (lax.axis_size(second), 8, 128))
    spectrum = jnp.sum(lax.all_to_all(copies, second, 0, 0, tiled=True), axis=0).reshape(NB)
    return (emf, mode_power, spectrum)


def solution(mesh):
    fine = Mesh(mesh.devices.reshape(4, 2, 2, 8, 2, 2), GZ + GY)
    placed = (
        P(None, None, GY, GZ),
        P(None, GY, GZ),
        P(GY),
        P(GZ),
        P(GZ + GY, None),
    )
    return jax.shard_map(
        on_device,
        mesh=fine,
        in_specs=placed,
        out_specs=(P(None, None, GY, GZ), P(GZ + GY, None), P()),
        check_vma=False,
    )
```

```python
import math

import jax
import jax.numpy as jnp
import numpy as np
from jax import lax
from jax.experimental import pallas as pl
from jax.experimental.pallas import tpu as pltpu
from jax.sharding import Mesh, PartitionSpec as P

NY = 2048
NZ = 2048
NB = 1024
KZ = 1024
BF = jnp.bfloat16
F32 = jnp.float32
GZ = ("yh", "yl", "xh")
GY = ("z", "xl", "c")
ACROSS = (((1,), (1,)), ((), ()))


def angle(a, b, length):
    return 2.0 * math.pi * ((a[:, None] * b[None, :]) % length) / length


def z_table():
    part, kappa, y, jh = np.meshgrid(*(np.arange(n) for n in (2, 16, 8, 4)), indexing="ij")
    modes = (16 * (8 * y + 4 * part + jh) + kappa).reshape(2, 1, 512, 1)
    turn = (modes * np.arange(128) % NZ + 128 * np.arange(8).reshape(1, 8, 1, 1)) % NZ
    return (np.cos(2.0 * math.pi * turn / NZ) / math.sqrt(NZ)).astype(jnp.bfloat16)


def y_tables():
    inner = angle((8 * np.arange(32)[None, :] + np.arange(8)[:, None]).reshape(-1), np.arange(256), 256)
    cos, sin = np.cos(inner), np.sin(inner)
    table = np.stack([np.stack([cos, -sin], axis=1), np.stack([sin, cos], axis=1)], axis=1)
    turn = angle(np.arange(8), np.arange(256), NY)
    order = np.zeros((128, 128), np.float32)
    for e in range(2):
        for cp in range(6):
            for y0 in range(8):
                order[16 * y0 + 8 * e + cp, 64 * e + 8 * cp + y0] = 1.0
    return (
        table.reshape(512, 512).astype(jnp.bfloat16),
        np.stack([np.cos(turn), np.sin(turn)]).astype(np.float32),
        order.astype(jnp.bfloat16),
    )


def metric(level):
    return 1.0 / (1.0 + 0.25 * level.astype(F32))


def roll(x, by, axis):
    return pltpu.roll(x, by % x.shape[axis], axis)


def hall(p, fb, den, my, mz, ylo_ref, yhi_ref, zlo, zhi):
    rows, lanes = fb.shape[2], fb.shape[3]
    row = lax.broadcasted_iota(jnp.int32, (rows, lanes), 0)
    lane = lax.broadcasted_iota(jnp.int32, (rows, lanes), 1)

    def d_y(f, at):
        up = jnp.where(row == rows - 1, yhi_ref[at : at + 1, :], roll(f, -1, 0))
        down = jnp.where(row == 0, ylo_ref[at : at + 1, :], roll(f, 1, 0))
        return (up - down) * my

    def d_z(f, at):
        up = jnp.where(lane == lanes - 1, zhi[at], roll(f, -1, 1))
        down = jnp.where(lane == 0, zlo[at], roll(f, 1, 1))
        return (up - down) * mz

    b_x, b_y, b_z = fb[0, p], fb[1, p], fb[2, p]
    half = 0.5 if p == 0 else -0.5
    cur_x = d_y(b_z, 2 + p) - d_z(b_y, 2 + p)
    cur_y = d_z(b_x, p) - half * fb[2, 1 - p]
    cur_z = half * fb[1, 1 - p] - d_y(b_x, p)
    dens = den[p]
    return (
        (cur_y * b_z - cur_z * b_y) / dens,
        (cur_z * b_x - cur_x * b_z) / dens,
        (cur_x * b_y - cur_y * b_x) / dens,
    )


def fetched(far, near, sems):
    copies = [pltpu.make_async_copy(a, b, sems.at[n]) for n, (a, b) in enumerate(zip(far, near))]
    for copy in copies:
        copy.start()
    for copy in copies:
        copy.wait()


def metrics(ly_ref, lz_ref, shape):
    half_y = jnp.broadcast_to(0.5 * metric(ly_ref[...]), (8, shape[0]))
    return jnp.broadcast_to(jnp.transpose(half_y)[:, 0:1], shape), 0.5 * metric(lz_ref[...])


def message_kernel(*refs):
    far, (ylo_ref, yhi_ref, msg_ref, held_ref, emf_ref), near, sems = refs[0:4], refs[4:9], refs[9:13], refs[13]
    fetched(far, near, sems)
    ly_ref, lz_ref, fb, den = near
    shape = fb.shape[2:]
    my, mz = metrics(ly_ref, lz_ref, shape)
    lane = lax.broadcasted_iota(jnp.int32, shape, 1)
    edge = (lane == 0) | (lane == 127)
    slot = lane >> 1
    signed = jnp.where(lane == 0, -mz, mz)
    none = [0.0] * 4
    inside, held = [], []
    own = jnp.zeros(shape, F32)
    for p in range(2):
        parts = hall(p, fb, den, my, mz, ylo_ref, yhi_ref, none, none)
        weight = signed / den[p]
        fields = [fb[comp, p] for comp in range(3)]
        inside.append([jnp.where(edge, 0.0, part) for part in parts])
        terms = list(parts) + [f * weight for f in fields] + fields[0:2]
        packed = jnp.zeros(shape, F32)
        for q, term in enumerate(terms):
            packed = jnp.where(slot == q, roll(term, 2 * q + 1, 1), packed)
        held.append(packed)
        for comp in range(2):
            k = 2 * p + comp
            own = jnp.where(slot == k, roll(fields[comp], 2 * k + 1, 1), own)
        for comp in range(3):
            emf_ref[comp, p] = inside[p][comp].astype(BF)
    held_ref[...] = held[0] + roll(held[1], 16, 1)
    first = own.astype(BF).astype(F32)
    own = own - first
    second = own.astype(BF).astype(F32)
    own = first + roll(second, 8, 1) + roll(own - second, 16, 1)
    folded = roll(own[0:16], 32, 1)
    for block in range(1, 4):
        folded = folded + roll(own[16 * block : 16 * block + 16], 32 + 24 * block, 1)
    for block in range(8):
        rows = slice(8 * block, 8 * block + 8)
        tile = jnp.concatenate([held[0][rows], held[1][rows]], axis=0)
        high = tile.astype(BF).astype(F32)
        low = (tile - high).astype(BF).astype(F32)
        values = [jnp.concatenate([inside[0][comp][rows], inside[1][comp][rows]], axis=0) for comp in range(3)]
        values.append(high + roll(low, 16, 1) + folded)
        for n, value in enumerate(values):
            for copy in range(2):
                msg_ref[2 * block + copy, 16 * n : 16 * n + 16, :] = value.astype(BF)


def finished(held, beside):
    slot = (lax.broadcasted_iota(jnp.int32, held.shape, 1) >> 1) & 7
    flat = roll(beside, -12, 1) * jnp.where(slot == 0, roll(held, -10, 1), roll(held, -8, 1))
    upright = roll(beside, -10, 1) * roll(held, -4, 1) + roll(beside, -8, 1) * roll(held, -2, 1)
    return held + jnp.where(slot == 2, -upright, flat)


def at_edges(values, spot):
    lane = lax.broadcasted_iota(jnp.int32, values.shape, 1)
    return jnp.where((lane == 0) | (lane == 127), roll(values, -spot, 1), 0.0).astype(BF)


def line_edges(x_ref):
    held = jnp.concatenate([x_ref[i, 48:64, :] for i in range(16)], axis=0).astype(F32)
    held = held + roll(held, -16, 1)
    lane = lax.broadcasted_iota(jnp.int32, held.shape, 1)
    beside = jnp.where((lane & 1) == 0, roll(roll(held, -16, 0), -1, 1), roll(roll(held, 16, 0), 1, 1))
    values = finished(held, beside)
    return [at_edges(values, 2 * comp + 1) for comp in range(3)]


def finish_emf(x_ref, held_ref, inside_ref, emf_ref):
    me = lax.axis_index("yh") * 4 + lax.axis_index("yl") * 2 + lax.axis_index("xh")

    def fields(block):
        folded = x_ref[block, 48:64, :].astype(F32)
        rows = []
        for n in range(4):
            own = roll(folded, -(32 + 24 * n), 1)
            rows.append(own + (roll(own, -8, 1) + roll(own, -16, 1)))
        return jnp.concatenate(rows, axis=0)

    low, high = fields(lax.rem(me + 15, 16)), fields(lax.rem(me + 1, 16))
    lane = lax.broadcasted_iota(jnp.int32, low.shape, 1)
    beside = jnp.where((lane & 1) == 0, roll(high, -1, 1), roll(low, 1, 1))
    beside = jnp.where(lane < 16, roll(beside, 12, 1), roll(beside, 24, 1))
    values = finished(held_ref[...], beside)
    for comp in range(3):
        for p in range(2):
            emf_ref[comp, p] = inside_ref[comp, p] + at_edges(values, 16 * p + 2 * comp + 1)


def z_kernel(x_ref, table_ref, held_ref, inside_ref, out_ref, emf_ref, mix_ref):
    edges = line_edges(x_ref)
    zero = jnp.zeros((80, 512), BF)
    total = None
    for n in range(4):
        lines = []
        for i in range(4 * n, 4 * n + 4):
            tiles = [x_ref[i, 16 * c : 16 * c + 16, :] + edges[c][16 * i : 16 * i + 16] for c in range(3)]
            lines.append(jnp.concatenate(tiles, axis=0))
        lines = jnp.concatenate([jnp.concatenate(lines, axis=1), zero], axis=0)
        blocks = []
        for e in range(2):
            for c in range(2):
                for jl in range(8):
                    kappa = 2 * jl + e
                    turns = [(kappa * i + 4 * c) % 16 for i in range(4 * n, 4 * n + 4)]
                    cells = [table_ref[m % 8, 32 * kappa : 32 * kappa + 32, :] for m in turns]
                    blocks.append(jnp.concatenate([-x if m >= 8 else x for m, x in zip(turns, cells)], axis=1))
        product = lax.dot_general(jnp.concatenate(blocks, axis=0), lines, ACROSS, preferred_element_type=F32)
        total = product if n == 0 else total + product
    total = total[0:512] + roll(total[512:1024], 64, 1)
    for c in range(2):
        for jl in range(8):
            at = 32 * (8 * c + jl)
            mix_ref[pl.ds(2 * jl + c, 32, stride=16), :] = total[at : at + 32]
    out_ref[...] = mix_ref[...].astype(BF)
    finish_emf(x_ref, held_ref, inside_ref, emf_ref)


def add(a, b):
    return (a[0] + b[0], a[1] + b[1])


def sub(a, b):
    return (a[0] - b[0], a[1] - b[1])


def turned(a, eighths):
    eighths %= 16
    if eighths == 0:
        return a
    if eighths == 4:
        return (a[1], -a[0])
    if eighths == 2:
        r = math.sqrt(0.5)
        return ((a[0] + a[1]) * r, (a[1] - a[0]) * r)
    if eighths == 6:
        r = math.sqrt(0.5)
        return ((a[1] - a[0]) * r, -(a[0] + a[1]) * r)
    cos, sin = math.cos(math.pi * eighths / 8), math.sin(math.pi * eighths / 8)
    return (a[0] * cos + a[1] * sin, a[1] * cos - a[0] * sin)


def fourier4(x):
    s, d = add(x[0], x[2]), sub(x[0], x[2])
    t, u = add(x[1], x[3]), turned(sub(x[1], x[3]), 4)
    return [add(s, t), add(d, u), sub(s, t), sub(d, u)]


def fourier8(x):
    even = fourier4([x[0], x[2], x[4], x[6]])
    odd = fourier4([x[1], x[3], x[5], x[7]])
    odd = [turned(value, 2 * k) for k, value in enumerate(odd)]
    return [add(a, b) for a, b in zip(even, odd)] + [sub(a, b) for a, b in zip(even, odd)]


def y_kernel(x_ref, table_ref, turn_ref, order_ref, bins_ref, power_ref, sums_ref):
    lhs = lax.dot_general(order_ref[...], x_ref[...], ACROSS, preferred_element_type=F32).astype(BF)
    product = jnp.dot(lhs, table_ref[...], preferred_element_type=F32)
    scale = 1.0 / (6.0 * NY)
    for e in range(2):
        held = []
        for y0 in range(8):
            at = 16 * y0 + 8 * e
            a, b = product[at : at + 8, 0:256], product[at : at + 8, 256:512]
            if y0 > 0:
                cos, sin = turn_ref[0, y0 : y0 + 1, :], turn_ref[1, y0 : y0 + 1, :]
                a, b = a * cos + b * sin, b * cos - a * sin
            held.append((a, b))
        for q1, (a, b) in enumerate(fourier8(held)):
            power_ref[e : e + 1, 256 * q1 : 256 * q1 + 256] = (
                jnp.sum(a * a + b * b, axis=0, keepdims=True) * scale
            )
    sums = jnp.zeros((8, 128), F32)
    for e in range(2):
        value = power_ref[e : e + 1, :]
        bins = bins_ref[e : e + 1, :]
        coarse = lax.broadcasted_iota(jnp.int32, (8, NY), 0) == (bins >> 7)
        fine = (lax.broadcasted_iota(jnp.int32, (128, NY), 0) == (bins & 127)).astype(F32).astype(BF)
        spread = jnp.where(coarse, value, 0.0)
        first = spread.astype(BF)
        spread = spread - first.astype(F32)
        second = spread.astype(BF)
        third = (spread - second.astype(F32)).astype(BF)
        for piece in (third, second, first):
            sums += lax.dot_general(piece, fine, ACROSS, preferred_element_type=F32)
    sums = sums * (NB / (KZ * NY))
    for copy in range(sums_ref.shape[0]):
        sums_ref[copy] = sums


def on_device(field_b, density, level_y, level_z, bins):
    y_local, z_local = field_b.shape[2], field_b.shape[3]

    def shift(cells, axis, step):
        count = lax.axis_size(axis)
        return lax.ppermute(cells, axis, [(i, (i + step) % count) for i in range(count)])

    ylo = shift(field_b[0::2, :, y_local - 1, :].reshape(4, z_local), GY, 1)
    yhi = shift(field_b[0::2, :, 0, :].reshape(4, z_local), GY, -1)
    half = lax.dynamic_index_in_dim(jnp.asarray(z_table()), lax.axis_index("xh"), keepdims=False)
    half, ylo, yhi = lax.optimization_barrier((half, ylo, yhi))
    small = pltpu.CompilerParams(vmem_limit_bytes=16 * 2**20)
    far = [
        pltpu.with_memory_space_constraint(x, pltpu.HBM)
        for x in (level_y[None, :], level_z[None, :], field_b, density)
    ]
    scratch = [
        pltpu.VMEM((1, y_local), jnp.int32),
        pltpu.VMEM((1, z_local), jnp.int32),
        pltpu.VMEM(field_b.shape, F32),
        pltpu.VMEM(density.shape, F32),
        pltpu.SemaphoreType.DMA((4,)),
    ]
    message, held, inside = pl.pallas_call(
        message_kernel,
        out_shape=(
            jax.ShapeDtypeStruct((16, 64, z_local), BF),
            jax.ShapeDtypeStruct((y_local, z_local), F32),
            jax.ShapeDtypeStruct(field_b.shape, BF),
        ),
        in_specs=[pl.BlockSpec(memory_space=pltpu.HBM)] * 4 + [pl.BlockSpec(memory_space=pltpu.VMEM)] * 2,
        scratch_shapes=scratch,
        compiler_params=small,
    )(*far, ylo, yhi)
    lines = lax.all_to_all(message, GZ, 0, 0, tiled=True)
    z_modes, emf = pl.pallas_call(
        z_kernel,
        out_shape=(jax.ShapeDtypeStruct((512, 128), BF), jax.ShapeDtypeStruct(field_b.shape, BF)),
        scratch_shapes=[pltpu.VMEM((512, 128), F32)],
        compiler_params=small,
    )(lines, half, held, inside)
    spread = lax.all_to_all(z_modes.reshape(256, 2, 128), ("yh", "yl") + GY, 0, 0, tiled=True).reshape(512, 128)
    first = ("yh", "yl", "c")
    second = ("xh", "z", "xl")
    mode_power, sums = pl.pallas_call(
        y_kernel,
        out_shape=(
            jax.ShapeDtypeStruct((2, NY), F32),
            jax.ShapeDtypeStruct((lax.axis_size(first), 8, 128), F32),
        ),
        compiler_params=small,
    )(spread, *y_tables(), bins)
    sums = jnp.sum(lax.all_to_all(sums, first, 0, 0, tiled=True), axis=0)
    copies = jnp.broadcast_to(sums[None], (lax.axis_size(second), 8, 128))
    spectrum = jnp.sum(lax.all_to_all(copies, second, 0, 0, tiled=True), axis=0).reshape(NB)
    return (emf, mode_power, spectrum)


def solution(mesh):
    fine = Mesh(mesh.devices.reshape(4, 2, 2, 8, 2, 2), GZ + GY)
    placed = (
        P(None, None, GY, GZ),
        P(None, GY, GZ),
        P(GY),
        P(GZ),
        P(GZ + GY, None),
    )
    return jax.shard_map(
        on_device,
        mesh=fine,
        in_specs=placed,
        out_specs=(P(None, None, GY, GZ), P(GZ + GY, None), P()),
        check_vma=False,
    )
```

```python
import math

import jax
import jax.numpy as jnp
import numpy as np
from jax import lax
from jax.experimental import pallas as pl
from jax.experimental.pallas import tpu as pltpu
from jax.sharding import Mesh, PartitionSpec as P

NY = 2048
NZ = 2048
NB = 1024
KZ = 1024
BF = jnp.bfloat16
F32 = jnp.float32
GZ = ("yh", "yl", "xh")
GY = ("z", "xl", "c")
ACROSS = (((1,), (1,)), ((), ()))


def angle(a, b, length):
    return 2.0 * math.pi * ((a[:, None] * b[None, :]) % length) / length


def z_table():
    part, kappa, y, jh = np.meshgrid(*(np.arange(n) for n in (2, 16, 8, 4)), indexing="ij")
    modes = (16 * (8 * y + 4 * part + jh) + kappa).reshape(2, 1, 512, 1)
    turn = (modes * np.arange(128) % NZ + 128 * np.arange(8).reshape(1, 8, 1, 1)) % NZ
    return (np.cos(2.0 * math.pi * turn / NZ) / math.sqrt(NZ)).astype(jnp.bfloat16)


def y_tables():
    inner = angle((8 * np.arange(32)[None, :] + np.arange(8)[:, None]).reshape(-1), np.arange(256), 256)
    cos, sin = np.cos(inner), np.sin(inner)
    table = np.stack([np.stack([cos, -sin], axis=1), np.stack([sin, cos], axis=1)], axis=1)
    turn = angle(np.arange(8), np.arange(256), NY)
    order = np.zeros((128, 128), np.float32)
    for e in range(2):
        for cp in range(6):
            for y0 in range(8):
                order[16 * y0 + 8 * e + cp, 64 * e + 8 * cp + y0] = 1.0
    return (
        table.reshape(512, 512).astype(jnp.bfloat16),
        np.stack([np.cos(turn), np.sin(turn)]).astype(np.float32),
        order.astype(jnp.bfloat16),
    )


def metric(level):
    return 1.0 / (1.0 + 0.25 * level.astype(F32))


def roll(x, by, axis):
    return pltpu.roll(x, by % x.shape[axis], axis)


def hall(p, fb, den, my, mz, ylo_ref, yhi_ref, zlo, zhi):
    rows, lanes = fb.shape[2], fb.shape[3]
    row = lax.broadcasted_iota(jnp.int32, (rows, lanes), 0)
    lane = lax.broadcasted_iota(jnp.int32, (rows, lanes), 1)

    def d_y(f, at):
        up = jnp.where(row == rows - 1, yhi_ref[at : at + 1, :], roll(f, -1, 0))
        down = jnp.where(row == 0, ylo_ref[at : at + 1, :], roll(f, 1, 0))
        return (up - down) * my

    def d_z(f, at):
        up = jnp.where(lane == lanes - 1, zhi[at], roll(f, -1, 1))
        down = jnp.where(lane == 0, zlo[at], roll(f, 1, 1))
        return (up - down) * mz

    b_x, b_y, b_z = fb[0, p], fb[1, p], fb[2, p]
    half = 0.5 if p == 0 else -0.5
    cur_x = d_y(b_z, 2 + p) - d_z(b_y, 2 + p)
    cur_y = d_z(b_x, p) - half * fb[2, 1 - p]
    cur_z = half * fb[1, 1 - p] - d_y(b_x, p)
    dens = den[p]
    return (
        (cur_y * b_z - cur_z * b_y) / dens,
        (cur_z * b_x - cur_x * b_z) / dens,
        (cur_x * b_y - cur_y * b_x) / dens,
    )


def fetched(far, near, sems):
    copies = [pltpu.make_async_copy(a, b, sems.at[n]) for n, (a, b) in enumerate(zip(far, near))]
    for copy in copies:
        copy.start()
    for copy in copies:
        copy.wait()


def metrics(ly_ref, lz_ref, shape):
    half_y = jnp.broadcast_to(0.5 * metric(ly_ref[...]), (8, shape[0]))
    return jnp.broadcast_to(jnp.transpose(half_y)[:, 0:1], shape), 0.5 * metric(lz_ref[...])


def message_kernel(*refs):
    far, (ylo_ref, yhi_ref, msg_ref, held_ref, emf_ref), near, sems = refs[0:4], refs[4:9], refs[9:13], refs[13]
    fetched(far, near, sems)
    ly_ref, lz_ref, fb, den = near
    shape = fb.shape[2:]
    my, mz = metrics(ly_ref, lz_ref, shape)
    lane = lax.broadcasted_iota(jnp.int32, shape, 1)
    edge = (lane == 0) | (lane == 127)
    slot = lane >> 1
    signed = jnp.where(lane == 0, -mz, mz)
    none = [0.0] * 4
    inside, held = [], []
    own = jnp.zeros(shape, F32)
    for p in range(2):
        parts = hall(p, fb, den, my, mz, ylo_ref, yhi_ref, none, none)
        weight = signed / den[p]
        fields = [fb[comp, p] for comp in range(3)]
        inside.append([jnp.where(edge, 0.0, part) for part in parts])
        terms = list(parts) + [f * weight for f in fields] + fields[0:2]
        packed = jnp.zeros(shape, F32)
        for q, term in enumerate(terms):
            packed = jnp.where(slot == q, roll(term, 2 * q + 1, 1), packed)
        held.append(packed)
        for comp in range(2):
            k = 2 * p + comp
            own = jnp.where(slot == k, roll(fields[comp], 2 * k + 1, 1), own)
        for comp in range(3):
            emf_ref[comp, p] = inside[p][comp].astype(BF)
    held_ref[...] = held[0] + roll(held[1], 16, 1)
    first = own.astype(BF).astype(F32)
    own = own - first
    second = own.astype(BF).astype(F32)
    own = first + roll(second, 8, 1) + roll(own - second, 16, 1)
    folded = roll(own[0:16], 32, 1)
    for block in range(1, 4):
        folded = folded + roll(own[16 * block : 16 * block + 16], 32 + 24 * block, 1)
    for block in range(8):
        rows = slice(8 * block, 8 * block + 8)
        tile = jnp.concatenate([held[0][rows], held[1][rows]], axis=0)
        high = tile.astype(BF).astype(F32)
        low = (tile - high).astype(BF).astype(F32)
        values = [jnp.concatenate([inside[0][comp][rows], inside[1][comp][rows]], axis=0) for comp in range(3)]
        values.append(high + roll(low, 16, 1) + folded)
        for n, value in enumerate(values):
            for copy in range(2):
                msg_ref[2 * block + copy, 16 * n : 16 * n + 16, :] = value.astype(BF)


def finished(held, beside):
    slot = (lax.broadcasted_iota(jnp.int32, held.shape, 1) >> 1) & 7
    flat = roll(beside, -12, 1) * jnp.where(slot == 0, roll(held, -10, 1), roll(held, -8, 1))
    upright = roll(beside, -10, 1) * roll(held, -4, 1) + roll(beside, -8, 1) * roll(held, -2, 1)
    return held + jnp.where(slot == 2, -upright, flat)


def at_edges(values, spot):
    lane = lax.broadcasted_iota(jnp.int32, values.shape, 1)
    return jnp.where((lane == 0) | (lane == 127), roll(values, -spot, 1), 0.0).astype(BF)


def line_edges(x_ref):
    held = jnp.concatenate([x_ref[i, 48:64, :] for i in range(16)], axis=0).astype(F32)
    held = held + roll(held, -16, 1)
    lane = lax.broadcasted_iota(jnp.int32, held.shape, 1)
    beside = jnp.where((lane & 1) == 0, roll(roll(held, -16, 0), -1, 1), roll(roll(held, 16, 0), 1, 1))
    values = finished(held, beside)
    return [at_edges(values, 2 * comp + 1) for comp in range(3)]


def finish_emf(x_ref, held_ref, inside_ref, emf_ref):
    me = lax.axis_index("yh") * 4 + lax.axis_index("yl") * 2 + lax.axis_index("xh")

    def fields(block):
        folded = x_ref[block, 48:64, :].astype(F32)
        rows = []
        for n in range(4):
            own = roll(folded, -(32 + 24 * n), 1)
            rows.append(own + (roll(own, -8, 1) + roll(own, -16, 1)))
        return jnp.concatenate(rows, axis=0)

    low, high = fields(lax.rem(me + 15, 16)), fields(lax.rem(me + 1, 16))
    lane = lax.broadcasted_iota(jnp.int32, low.shape, 1)
    beside = jnp.where((lane & 1) == 0, roll(high, -1, 1), roll(low, 1, 1))
    beside = jnp.where(lane < 16, roll(beside, 12, 1), roll(beside, 24, 1))
    values = finished(held_ref[...], beside)
    for comp in range(3):
        for p in range(2):
            emf_ref[comp, p] = inside_ref[comp, p] + at_edges(values, 16 * p + 2 * comp + 1)


def z_kernel(x_ref, table_ref, held_ref, inside_ref, out_ref, emf_ref, mix_ref):
    edges = line_edges(x_ref)
    zero = jnp.zeros((16, 512), BF)
    total = None
    for n in range(2):
        sums, gaps = [], []
        for i in range(4 * n, 4 * n + 4):
            for side, pair in ((sums, 1), (gaps, -1)):
                tiles = []
                for c in range(3):
                    near, far = (
                        x_ref[m, 16 * c : 16 * c + 16, :] + edges[c][16 * m : 16 * m + 16] for m in (i, i + 8)
                    )
                    tiles.append(near + far if pair > 0 else near - far)
                side.append(jnp.concatenate(tiles, axis=0))
        sums, gaps = (jnp.concatenate([jnp.concatenate(x, axis=1), zero], axis=0) for x in (sums, gaps))
        empty = jnp.zeros((64, 512), BF)
        lines = jnp.concatenate(
            [jnp.concatenate([sums, empty], axis=0), jnp.concatenate([empty, gaps], axis=0)], axis=1
        )
        blocks = []
        for c in range(2):
            for jl in range(8):
                row = []
                for kappa in (2 * jl, 2 * jl + 1):
                    for i in range(4 * n, 4 * n + 4):
                        m = (kappa * i + 4 * c) % 16
                        cell = table_ref[m % 8, 32 * kappa : 32 * kappa + 32, :]
                        row.append(-cell if m >= 8 else cell)
                blocks.append(jnp.concatenate(row, axis=1))
        product = lax.dot_general(jnp.concatenate(blocks, axis=0), lines, ACROSS, preferred_element_type=F32)
        total = product if n == 0 else total + product
    for c in range(2):
        for jl in range(8):
            at = 32 * (8 * c + jl)
            mix_ref[pl.ds(2 * jl + c, 32, stride=16), :] = total[at : at + 32]
    out_ref[...] = mix_ref[...].astype(BF)
    finish_emf(x_ref, held_ref, inside_ref, emf_ref)


def add(a, b):
    return (a[0] + b[0], a[1] + b[1])


def sub(a, b):
    return (a[0] - b[0], a[1] - b[1])


def turned(a, eighths):
    eighths %= 16
    if eighths == 0:
        return a
    if eighths == 4:
        return (a[1], -a[0])
    if eighths == 2:
        r = math.sqrt(0.5)
        return ((a[0] + a[1]) * r, (a[1] - a[0]) * r)
    if eighths == 6:
        r = math.sqrt(0.5)
        return ((a[1] - a[0]) * r, -(a[0] + a[1]) * r)
    cos, sin = math.cos(math.pi * eighths / 8), math.sin(math.pi * eighths / 8)
    return (a[0] * cos + a[1] * sin, a[1] * cos - a[0] * sin)


def fourier4(x):
    s, d = add(x[0], x[2]), sub(x[0], x[2])
    t, u = add(x[1], x[3]), turned(sub(x[1], x[3]), 4)
    return [add(s, t), add(d, u), sub(s, t), sub(d, u)]


def fourier8(x):
    even = fourier4([x[0], x[2], x[4], x[6]])
    odd = fourier4([x[1], x[3], x[5], x[7]])
    odd = [turned(value, 2 * k) for k, value in enumerate(odd)]
    return [add(a, b) for a, b in zip(even, odd)] + [sub(a, b) for a, b in zip(even, odd)]


def y_kernel(x_ref, table_ref, turn_ref, order_ref, bins_ref, power_ref, sums_ref):
    lhs = lax.dot_general(order_ref[...], x_ref[...], ACROSS, preferred_element_type=F32).astype(BF)
    product = jnp.dot(lhs, table_ref[...], preferred_element_type=F32)
    scale = 1.0 / (6.0 * NY)
    for e in range(2):
        held = []
        for y0 in range(8):
            at = 16 * y0 + 8 * e
            a, b = product[at : at + 8, 0:256], product[at : at + 8, 256:512]
            if y0 > 0:
                cos, sin = turn_ref[0, y0 : y0 + 1, :], turn_ref[1, y0 : y0 + 1, :]
                a, b = a * cos + b * sin, b * cos - a * sin
            held.append((a, b))
        for q1, (a, b) in enumerate(fourier8(held)):
            power_ref[e : e + 1, 256 * q1 : 256 * q1 + 256] = (
                jnp.sum(a * a + b * b, axis=0, keepdims=True) * scale
            )
    sums = jnp.zeros((32, 128), F32)
    steps = lax.broadcasted_iota(jnp.int32, (128, 128), 0).astype(F32).astype(BF)
    one, none = jnp.ones((128, 128), BF), jnp.zeros((128, 128), BF)
    for e in range(2):
        value = power_ref[e : e + 1, :]
        bins = bins_ref[e : e + 1, :]
        coarse = lax.broadcasted_iota(jnp.int32, (8, NY), 0) == (bins >> 7)
        within = jnp.broadcast_to((bins & 127).astype(F32), (16, NY)).astype(BF)
        fine = []
        for n in range(NY // 128):
            tile = within[:, 128 * n : 128 * n + 128]
            fine.append(jnp.where(steps == jnp.concatenate([tile] * 8, axis=0), one, none))
        spread = jnp.where(coarse, value, 0.0)
        first = spread.astype(BF).astype(F32)
        second = (spread - first).astype(BF).astype(F32)
        third = spread - first - second
        pieces = jnp.concatenate([third, second, first, jnp.zeros_like(first)], axis=0).astype(BF)
        sums += lax.dot_general(pieces, jnp.concatenate(fine, axis=1), ACROSS, preferred_element_type=F32)
    sums = sums[0:8] + sums[8:16] + sums[16:24]
    sums = sums * (NB / (KZ * NY))
    for copy in range(sums_ref.shape[0]):
        sums_ref[copy] = sums


def on_device(field_b, density, level_y, level_z, bins):
    y_local, z_local = field_b.shape[2], field_b.shape[3]

    def shift(cells, axis, step):
        count = lax.axis_size(axis)
        return lax.ppermute(cells, axis, [(i, (i + step) % count) for i in range(count)])

    ylo = shift(field_b[0::2, :, y_local - 1, :].reshape(4, z_local), GY, 1)
    yhi = shift(field_b[0::2, :, 0, :].reshape(4, z_local), GY, -1)
    half = lax.dynamic_index_in_dim(jnp.asarray(z_table()), lax.axis_index("xh"), keepdims=False)
    half, ylo, yhi = lax.optimization_barrier((half, ylo, yhi))
    small = pltpu.CompilerParams(vmem_limit_bytes=16 * 2**20)
    far = [
        pltpu.with_memory_space_constraint(x, pltpu.HBM)
        for x in (level_y[None, :], level_z[None, :], field_b, density)
    ]
    scratch = [
        pltpu.VMEM((1, y_local), jnp.int32),
        pltpu.VMEM((1, z_local), jnp.int32),
        pltpu.VMEM(field_b.shape, F32),
        pltpu.VMEM(density.shape, F32),
        pltpu.SemaphoreType.DMA((4,)),
    ]
    message, held, inside = pl.pallas_call(
        message_kernel,
        out_shape=(
            jax.ShapeDtypeStruct((16, 64, z_local), BF),
            jax.ShapeDtypeStruct((y_local, z_local), F32),
            jax.ShapeDtypeStruct(field_b.shape, BF),
        ),
        in_specs=[pl.BlockSpec(memory_space=pltpu.HBM)] * 4 + [pl.BlockSpec(memory_space=pltpu.VMEM)] * 2,
        scratch_shapes=scratch,
        compiler_params=small,
    )(*far, ylo, yhi)
    lines = lax.all_to_all(message, GZ, 0, 0, tiled=True)
    z_modes, emf = pl.pallas_call(
        z_kernel,
        out_shape=(jax.ShapeDtypeStruct((512, 128), BF), jax.ShapeDtypeStruct(field_b.shape, BF)),
        scratch_shapes=[pltpu.VMEM((512, 128), F32)],
        compiler_params=small,
    )(lines, half, held, inside)
    spread = lax.all_to_all(z_modes.reshape(256, 2, 128), ("yh", "yl") + GY, 0, 0, tiled=True).reshape(512, 128)
    first = ("yh", "yl", "c")
    second = ("xh", "z", "xl")
    mode_power, sums = pl.pallas_call(
        y_kernel,
        out_shape=(
            jax.ShapeDtypeStruct((2, NY), F32),
            jax.ShapeDtypeStruct((lax.axis_size(first), 8, 128), F32),
        ),
        compiler_params=small,
    )(spread, *y_tables(), bins)
    sums = jnp.sum(lax.all_to_all(sums, first, 0, 0, tiled=True), axis=0)
    copies = jnp.broadcast_to(sums.astype(BF)[None], (lax.axis_size(second), 8, 128))
    spectrum = jnp.sum(lax.all_to_all(copies, second, 0, 0, tiled=True).astype(F32), axis=0).reshape(NB)
    return (emf, mode_power, spectrum)


def solution(mesh):
    fine = Mesh(mesh.devices.reshape(4, 2, 2, 8, 2, 2), GZ + GY)
    placed = (
        P(None, None, GY, GZ),
        P(None, GY, GZ),
        P(GY),
        P(GZ),
        P(GZ + GY, None),
    )
    return jax.shard_map(
        on_device,
        mesh=fine,
        in_specs=placed,
        out_specs=(P(None, None, GY, GZ), P(GZ + GY, None), P()),
        check_vma=False,
    )
```

```python
import math

import jax
import jax.numpy as jnp
import numpy as np
from jax import lax
from jax.experimental import pallas as pl
from jax.experimental.pallas import tpu as pltpu
from jax.sharding import Mesh, PartitionSpec as P

NY = 2048
NZ = 2048
NB = 1024
KZ = 1024
BF = jnp.bfloat16
F32 = jnp.float32
GZ = ("yh", "yl", "xh")
GY = ("z", "xl", "c")
ACROSS = (((1,), (1,)), ((), ()))


def angle(a, b, length):
    return 2.0 * math.pi * ((a[:, None] * b[None, :]) % length) / length


def z_table():
    part, kappa, y, jh = np.meshgrid(*(np.arange(n) for n in (2, 16, 8, 4)), indexing="ij")
    modes = (16 * (8 * y + 4 * part + jh) + kappa).reshape(2, 1, 512, 1)
    turn = (modes * np.arange(128) % NZ + 128 * np.arange(8).reshape(1, 8, 1, 1)) % NZ
    return (np.cos(2.0 * math.pi * turn / NZ) / math.sqrt(NZ)).astype(jnp.bfloat16)


def y_tables():
    inner = angle((8 * np.arange(32)[None, :] + np.arange(8)[:, None]).reshape(-1), np.arange(256), 256)
    cos, sin = np.cos(inner), np.sin(inner)
    table = np.stack([np.stack([cos, -sin], axis=1), np.stack([sin, cos], axis=1)], axis=1)
    turn = angle(np.arange(8), np.arange(256), NY)
    order = np.zeros((128, 128), np.float32)
    for e in range(2):
        for cp in range(6):
            for y0 in range(8):
                order[16 * y0 + 8 * e + cp, 64 * e + 8 * cp + y0] = 1.0
    return (
        table.reshape(512, 512).astype(jnp.bfloat16),
        np.stack([np.cos(turn), np.sin(turn)]).astype(np.float32),
        order.astype(jnp.bfloat16),
    )


def metric(level):
    return 1.0 / (1.0 + 0.25 * level.astype(F32))


def roll(x, by, axis):
    return pltpu.roll(x, by % x.shape[axis], axis)


def hall(p, fb, den, my, mz):
    rows, lanes = fb.shape[2], fb.shape[3]
    row = lax.broadcasted_iota(jnp.int32, (rows, lanes), 0)
    lane = lax.broadcasted_iota(jnp.int32, (rows, lanes), 1)

    def d_y(f):
        return (jnp.where(row == rows - 1, 0.0, roll(f, -1, 0)) - jnp.where(row == 0, 0.0, roll(f, 1, 0))) * my

    def d_z(f):
        return (jnp.where(lane == lanes - 1, 0.0, roll(f, -1, 1)) - jnp.where(lane == 0, 0.0, roll(f, 1, 1))) * mz

    b_x, b_y, b_z = fb[0, p], fb[1, p], fb[2, p]
    half = 0.5 if p == 0 else -0.5
    cur_x = d_y(b_z) - d_z(b_y)
    cur_y = d_z(b_x) - half * fb[2, 1 - p]
    cur_z = half * fb[1, 1 - p] - d_y(b_x)
    dens = den[p]
    return (
        (cur_y * b_z - cur_z * b_y) / dens,
        (cur_z * b_x - cur_x * b_z) / dens,
        (cur_x * b_y - cur_y * b_x) / dens,
    )


def fetched(far, near, sems):
    copies = [pltpu.make_async_copy(a, b, sems.at[n]) for n, (a, b) in enumerate(zip(far, near))]
    for copy in copies:
        copy.start()
    for copy in copies:
        copy.wait()


def metrics(ly_ref, lz_ref, shape):
    half_y = jnp.broadcast_to(0.5 * metric(ly_ref[...]), (8, shape[0]))
    return jnp.broadcast_to(jnp.transpose(half_y)[:, 0:1], shape), 0.5 * metric(lz_ref[...])


def message_kernel(*refs):
    far, (msg_ref, held_ref, emf_ref, tips_ref, weights_ref), near, sems = refs[0:4], refs[4:9], refs[9:13], refs[13]
    fetched(far, near, sems)
    ly_ref, lz_ref, fb, den = near
    shape = fb.shape[2:]
    my, mz = metrics(ly_ref, lz_ref, shape)
    lane = lax.broadcasted_iota(jnp.int32, shape, 1)
    edge = (lane == 0) | (lane == 127)
    slot = lane >> 1
    signed = jnp.where(lane == 0, -mz, mz)
    inside, held = [], []
    own = jnp.zeros(shape, F32)
    for p in range(2):
        parts = hall(p, fb, den, my, mz)
        inverse = 1.0 / den[p]
        weight = signed * inverse
        for side, sign in ((0, -1.0), (1, 1.0)):
            at = side * (shape[0] - 1)
            upward = sign * my[at : at + 1] * inverse[at : at + 1]
            for comp in range(3):
                tips_ref[side, 2 * comp + p] = parts[comp][56 * side : 56 * side + 8]
                weights_ref[side, 3 * p + comp : 3 * p + comp + 1, :] = upward * fb[comp, p, at : at + 1, :]
        fields = [fb[comp, p] for comp in range(3)]
        inside.append([jnp.where(edge, 0.0, part) for part in parts])
        terms = list(parts) + [f * weight for f in fields] + fields[0:2]
        packed = jnp.zeros(shape, F32)
        for q, term in enumerate(terms):
            packed = jnp.where(slot == q, roll(term, 2 * q + 1, 1), packed)
        held.append(packed)
        for comp in range(2):
            k = 2 * p + comp
            own = jnp.where(slot == k, roll(fields[comp], 2 * k + 1, 1), own)
        for comp in range(3):
            emf_ref[comp, p] = inside[p][comp].astype(BF)
    held_ref[...] = held[0] + roll(held[1], 16, 1)
    first = own.astype(BF).astype(F32)
    own = own - first
    second = own.astype(BF).astype(F32)
    own = first + roll(second, 8, 1) + roll(own - second, 16, 1)
    folded = roll(own[0:16], 32, 1)
    for block in range(1, 4):
        folded = folded + roll(own[16 * block : 16 * block + 16], 32 + 24 * block, 1)
    for block in range(8):
        rows = slice(8 * block, 8 * block + 8)
        tile = jnp.concatenate([held[0][rows], held[1][rows]], axis=0)
        high = tile.astype(BF).astype(F32)
        low = (tile - high).astype(BF).astype(F32)
        values = [jnp.concatenate([inside[0][comp][rows], inside[1][comp][rows]], axis=0) for comp in range(3)]
        values.append(high + roll(low, 16, 1) + folded)
        for n, value in enumerate(values):
            for copy in range(2):
                msg_ref[2 * block + copy, 16 * n : 16 * n + 16, :] = value.astype(BF)


def rim_kernel(
    ylo_ref, yhi_ref, msg_ref, held_ref, emf_ref, tips_ref, weights_ref, msg_out, held_out, emf_out
):
    msg_out[...] = msg_ref[...]
    held_out[...] = held_ref[...]
    emf_out[...] = emf_ref[...]
    shape = (8, emf_ref.shape[3])
    row = lax.broadcasted_iota(jnp.int32, shape, 0)
    lane = lax.broadcasted_iota(jnp.int32, shape, 1)
    inner = (lane > 0) & (lane < 127)
    slot = lane >> 1
    for side, rim_ref in ((0, ylo_ref), (1, yhi_ref)):
        block = 7 * side
        rows = slice(8 * block, 8 * block + 8)
        held = held_ref[rows, :]
        values = []
        for p in range(2):
            f_x, f_z = rim_ref[p : p + 1, :], rim_ref[2 + p : 3 + p, :]
            w_x, w_y, w_z = (weights_ref[side, 3 * p + comp : 3 * p + comp + 1, :] for comp in range(3))
            extra = (f_x * w_y, -(f_x * w_x + f_z * w_z), f_z * w_y)
            for comp in range(3):
                change = jnp.where(row == 7 * side, extra[comp], 0.0)
                value = jnp.where(inner, tips_ref[side, 2 * comp + p] + change, 0.0)
                emf_out[comp, p, rows, :] = value.astype(BF)
                values.append(value)
                moved = roll(change, 16 * p + 2 * comp + 1, 1)
                held = held + jnp.where(slot == 8 * p + comp, moved, 0.0)
        held_out[rows, :] = held
        tile = jnp.concatenate([held, roll(held, -16, 1)], axis=0)
        wide = lax.broadcasted_iota(jnp.int32, tile.shape, 1)
        tile = jnp.where(wide < 16, tile, 0.0)
        high = tile.astype(BF).astype(F32)
        low = (tile - high).astype(BF).astype(F32)
        old = msg_ref[2 * block, 48:64, :].astype(F32)
        tiles = [jnp.concatenate([values[comp], values[3 + comp]], axis=0) for comp in range(3)]
        tiles.append(jnp.where(wide < 32, high + roll(low, 16, 1), old))
        for n, value in enumerate(tiles):
            for copy in range(2):
                msg_out[2 * block + copy, 16 * n : 16 * n + 16, :] = value.astype(BF)


def finished(held, beside):
    slot = (lax.broadcasted_iota(jnp.int32, held.shape, 1) >> 1) & 7
    flat = roll(beside, -12, 1) * jnp.where(slot == 0, roll(held, -10, 1), roll(held, -8, 1))
    upright = roll(beside, -10, 1) * roll(held, -4, 1) + roll(beside, -8, 1) * roll(held, -2, 1)
    return held + jnp.where(slot == 2, -upright, flat)


def at_edges(values, spot):
    lane = lax.broadcasted_iota(jnp.int32, values.shape, 1)
    return jnp.where((lane == 0) | (lane == 127), roll(values, -spot, 1), 0.0).astype(BF)


def line_edges(x_ref):
    held = jnp.concatenate([x_ref[i, 48:64, :] for i in range(16)], axis=0).astype(F32)
    held = held + roll(held, -16, 1)
    lane = lax.broadcasted_iota(jnp.int32, held.shape, 1)
    beside = jnp.where((lane & 1) == 0, roll(roll(held, -16, 0), -1, 1), roll(roll(held, 16, 0), 1, 1))
    values = finished(held, beside)
    return [at_edges(values, 2 * comp + 1) for comp in range(3)]


def finish_emf(x_ref, held_ref, inside_ref, emf_ref):
    me = lax.axis_index("yh") * 4 + lax.axis_index("yl") * 2 + lax.axis_index("xh")

    def fields(block):
        folded = x_ref[block, 48:64, :].astype(F32)
        rows = []
        for n in range(4):
            own = roll(folded, -(32 + 24 * n), 1)
            rows.append(own + (roll(own, -8, 1) + roll(own, -16, 1)))
        return jnp.concatenate(rows, axis=0)

    low, high = fields(lax.rem(me + 15, 16)), fields(lax.rem(me + 1, 16))
    lane = lax.broadcasted_iota(jnp.int32, low.shape, 1)
    beside = jnp.where((lane & 1) == 0, roll(high, -1, 1), roll(low, 1, 1))
    beside = jnp.where(lane < 16, roll(beside, 12, 1), roll(beside, 24, 1))
    values = finished(held_ref[...], beside)
    for comp in range(3):
        for p in range(2):
            emf_ref[comp, p] = inside_ref[comp, p] + at_edges(values, 16 * p + 2 * comp + 1)


def z_kernel(x_ref, table_ref, held_ref, inside_ref, out_ref, emf_ref, mix_ref):
    edges = line_edges(x_ref)
    zero = jnp.zeros((16, 512), BF)
    total = None
    for n in range(2):
        sums, gaps = [], []
        for i in range(4 * n, 4 * n + 4):
            for side, pair in ((sums, 1), (gaps, -1)):
                tiles = []
                for c in range(3):
                    near, far = (
                        x_ref[m, 16 * c : 16 * c + 16, :] + edges[c][16 * m : 16 * m + 16] for m in (i, i + 8)
                    )
                    tiles.append(near + far if pair > 0 else near - far)
                side.append(jnp.concatenate(tiles, axis=0))
        sums, gaps = (jnp.concatenate([jnp.concatenate(x, axis=1), zero], axis=0) for x in (sums, gaps))
        empty = jnp.zeros((64, 512), BF)
        lines = jnp.concatenate(
            [jnp.concatenate([sums, empty], axis=0), jnp.concatenate([empty, gaps], axis=0)], axis=1
        )
        blocks = []
        for c in range(2):
            for jl in range(8):
                row = []
                for kappa in (2 * jl, 2 * jl + 1):
                    for i in range(4 * n, 4 * n + 4):
                        m = (kappa * i + 4 * c) % 16
                        cell = table_ref[m % 8, 32 * kappa : 32 * kappa + 32, :]
                        row.append(-cell if m >= 8 else cell)
                blocks.append(jnp.concatenate(row, axis=1))
        product = lax.dot_general(jnp.concatenate(blocks, axis=0), lines, ACROSS, preferred_element_type=F32)
        total = product if n == 0 else total + product
    for c in range(2):
        for jl in range(8):
            at = 32 * (8 * c + jl)
            mix_ref[pl.ds(2 * jl + c, 32, stride=16), :] = total[at : at + 32]
    out_ref[...] = mix_ref[...].astype(BF)
    finish_emf(x_ref, held_ref, inside_ref, emf_ref)


def add(a, b):
    return (a[0] + b[0], a[1] + b[1])


def sub(a, b):
    return (a[0] - b[0], a[1] - b[1])


def turned(a, eighths):
    eighths %= 16
    if eighths == 0:
        return a
    if eighths == 4:
        return (a[1], -a[0])
    if eighths == 2:
        r = math.sqrt(0.5)
        return ((a[0] + a[1]) * r, (a[1] - a[0]) * r)
    if eighths == 6:
        r = math.sqrt(0.5)
        return ((a[1] - a[0]) * r, -(a[0] + a[1]) * r)
    cos, sin = math.cos(math.pi * eighths / 8), math.sin(math.pi * eighths / 8)
    return (a[0] * cos + a[1] * sin, a[1] * cos - a[0] * sin)


def fourier4(x):
    s, d = add(x[0], x[2]), sub(x[0], x[2])
    t, u = add(x[1], x[3]), turned(sub(x[1], x[3]), 4)
    return [add(s, t), add(d, u), sub(s, t), sub(d, u)]


def fourier8(x):
    even = fourier4([x[0], x[2], x[4], x[6]])
    odd = fourier4([x[1], x[3], x[5], x[7]])
    odd = [turned(value, 2 * k) for k, value in enumerate(odd)]
    return [add(a, b) for a, b in zip(even, odd)] + [sub(a, b) for a, b in zip(even, odd)]


def y_kernel(x_ref, table_ref, turn_ref, order_ref, bins_ref, power_ref, sums_ref):
    lhs = lax.dot_general(order_ref[...], x_ref[...], ACROSS, preferred_element_type=F32).astype(BF)
    product = jnp.dot(lhs, table_ref[...], preferred_element_type=F32)
    scale = 1.0 / (6.0 * NY)
    for e in range(2):
        held = []
        for y0 in range(8):
            at = 16 * y0 + 8 * e
            a, b = product[at : at + 8, 0:256], product[at : at + 8, 256:512]
            if y0 > 0:
                cos, sin = turn_ref[0, y0 : y0 + 1, :], turn_ref[1, y0 : y0 + 1, :]
                a, b = a * cos + b * sin, b * cos - a * sin
            held.append((a, b))
        for q1, (a, b) in enumerate(fourier8(held)):
            power_ref[e : e + 1, 256 * q1 : 256 * q1 + 256] = (
                jnp.sum(a * a + b * b, axis=0, keepdims=True) * scale
            )
    sums = jnp.zeros((32, 128), F32)
    steps = lax.broadcasted_iota(jnp.int32, (128, 128), 0).astype(F32).astype(BF)
    one, none = jnp.ones((128, 128), BF), jnp.zeros((128, 128), BF)
    for e in range(2):
        value = power_ref[e : e + 1, :]
        bins = bins_ref[e : e + 1, :]
        coarse = lax.broadcasted_iota(jnp.int32, (8, NY), 0) == (bins >> 7)
        within = jnp.broadcast_to((bins & 127).astype(F32), (16, NY)).astype(BF)
        fine = []
        for n in range(NY // 128):
            tile = within[:, 128 * n : 128 * n + 128]
            fine.append(jnp.where(steps == jnp.concatenate([tile] * 8, axis=0), one, none))
        spread = jnp.where(coarse, value, 0.0)
        first = spread.astype(BF).astype(F32)
        second = (spread - first).astype(BF).astype(F32)
        third = spread - first - second
        pieces = jnp.concatenate([third, second, first, jnp.zeros_like(first)], axis=0).astype(BF)
        sums += lax.dot_general(pieces, jnp.concatenate(fine, axis=1), ACROSS, preferred_element_type=F32)
    sums = sums[0:8] + sums[8:16] + sums[16:24]
    sums = sums * (NB / (KZ * NY))
    for copy in range(sums_ref.shape[0]):
        sums_ref[copy] = sums


def on_device(field_b, density, level_y, level_z, bins):
    y_local, z_local = field_b.shape[2], field_b.shape[3]

    def shift(cells, axis, step):
        count = lax.axis_size(axis)
        return lax.ppermute(cells, axis, [(i, (i + step) % count) for i in range(count)])

    ylo = shift(field_b[0::2, :, y_local - 1, :].reshape(4, z_local), GY, 1)
    yhi = shift(field_b[0::2, :, 0, :].reshape(4, z_local), GY, -1)
    half = lax.dynamic_index_in_dim(jnp.asarray(z_table()), lax.axis_index("xh"), keepdims=False)
    half, ylo, yhi = lax.optimization_barrier((half, ylo, yhi))
    small = pltpu.CompilerParams(vmem_limit_bytes=16 * 2**20)
    far = [
        pltpu.with_memory_space_constraint(x, pltpu.HBM)
        for x in (level_y[None, :], level_z[None, :], field_b, density)
    ]
    scratch = [
        pltpu.VMEM((1, y_local), jnp.int32),
        pltpu.VMEM((1, z_local), jnp.int32),
        pltpu.VMEM(field_b.shape, F32),
        pltpu.VMEM(density.shape, F32),
        pltpu.SemaphoreType.DMA((4,)),
    ]
    made = (
        jax.ShapeDtypeStruct((16, 64, z_local), BF),
        jax.ShapeDtypeStruct((y_local, z_local), F32),
        jax.ShapeDtypeStruct(field_b.shape, BF),
    )
    rims = (jax.ShapeDtypeStruct((2, 6, 8, z_local), F32), jax.ShapeDtypeStruct((2, 8, z_local), F32))
    local = pl.pallas_call(
        message_kernel,
        out_shape=made + rims,
        in_specs=[pl.BlockSpec(memory_space=pltpu.HBM)] * 4,
        scratch_shapes=scratch,
        compiler_params=small,
        cost_estimate=pl.CostEstimate(flops=2_000_000, bytes_accessed=1_000_000, transcendentals=0),
    )(*far)
    message, held, inside = pl.pallas_call(rim_kernel, out_shape=made, compiler_params=small)(ylo, yhi, *local)
    lines = lax.all_to_all(message, GZ, 0, 0, tiled=True)
    z_modes, emf = pl.pallas_call(
        z_kernel,
        out_shape=(jax.ShapeDtypeStruct((512, 128), BF), jax.ShapeDtypeStruct(field_b.shape, BF)),
        scratch_shapes=[pltpu.VMEM((512, 128), F32)],
        compiler_params=small,
    )(lines, half, held, inside)
    spread = lax.all_to_all(z_modes.reshape(256, 2, 128), ("yh", "yl") + GY, 0, 0, tiled=True).reshape(512, 128)
    first = ("yh", "yl", "c")
    second = ("xh", "z", "xl")
    mode_power, sums = pl.pallas_call(
        y_kernel,
        out_shape=(
            jax.ShapeDtypeStruct((2, NY), F32),
            jax.ShapeDtypeStruct((lax.axis_size(first), 8, 128), F32),
        ),
        compiler_params=small,
    )(spread, *y_tables(), bins)
    sums = jnp.sum(lax.all_to_all(sums, first, 0, 0, tiled=True), axis=0)
    copies = jnp.broadcast_to(sums.astype(BF)[None], (lax.axis_size(second), 8, 128))
    spectrum = jnp.sum(lax.all_to_all(copies, second, 0, 0, tiled=True).astype(F32), axis=0).reshape(NB)
    return (emf, mode_power, spectrum)


def solution(mesh):
    fine = Mesh(mesh.devices.reshape(4, 2, 2, 8, 2, 2), GZ + GY)
    placed = (
        P(None, None, GY, GZ),
        P(None, GY, GZ),
        P(GY),
        P(GZ),
        P(GZ + GY, None),
    )
    return jax.shard_map(
        on_device,
        mesh=fine,
        in_specs=placed,
        out_specs=(P(None, None, GY, GZ), P(GZ + GY, None), P()),
        check_vma=False,
    )
```

```python
import math

import jax
import jax.numpy as jnp
import numpy as np
from jax import lax
from jax.experimental import pallas as pl
from jax.experimental.pallas import tpu as pltpu
from jax.sharding import Mesh, PartitionSpec as P

NY = 2048
NZ = 2048
NB = 1024
KZ = 1024
BF = jnp.bfloat16
F32 = jnp.float32
GZ = ("yh", "yl", "xh")
GY = ("z", "xl", "c")
ACROSS = (((1,), (1,)), ((), ()))


def angle(a, b, length):
    return 2.0 * math.pi * ((a[:, None] * b[None, :]) % length) / length


def z_table():
    part, kappa, y, jh = np.meshgrid(*(np.arange(n) for n in (2, 16, 8, 4)), indexing="ij")
    modes = (16 * (8 * y + 4 * part + jh) + kappa).reshape(2, 1, 512, 1)
    turn = (modes * np.arange(128) % NZ + 128 * np.arange(8).reshape(1, 8, 1, 1)) % NZ
    return (np.cos(2.0 * math.pi * turn / NZ) / math.sqrt(NZ)).astype(jnp.bfloat16)


def y_tables():
    inner = angle((8 * np.arange(32)[None, :] + np.arange(8)[:, None]).reshape(-1), np.arange(256), 256)
    cos, sin = np.cos(inner), np.sin(inner)
    table = np.stack([np.stack([cos, -sin], axis=1), np.stack([sin, cos], axis=1)], axis=1)
    turn = angle(np.arange(8), np.arange(256), NY)
    order = np.zeros((128, 128), np.float32)
    for e in range(2):
        for cp in range(6):
            for y0 in range(8):
                order[16 * y0 + 8 * e + cp, 64 * e + 8 * cp + y0] = 1.0
    return (
        table.reshape(512, 512).astype(jnp.bfloat16),
        np.stack([np.cos(turn), np.sin(turn)]).astype(np.float32),
        order.astype(jnp.bfloat16),
    )


def metric(level):
    return 1.0 / (1.0 + 0.25 * level.astype(F32))


def roll(x, by, axis):
    return pltpu.roll(x, by % x.shape[axis], axis)


def hall(p, fb, den, my, mz):
    rows, lanes = fb.shape[2], fb.shape[3]
    row = lax.broadcasted_iota(jnp.int32, (rows, lanes), 0)
    lane = lax.broadcasted_iota(jnp.int32, (rows, lanes), 1)

    def d_y(f):
        return (jnp.where(row == rows - 1, 0.0, roll(f, -1, 0)) - jnp.where(row == 0, 0.0, roll(f, 1, 0))) * my

    def d_z(f):
        return (jnp.where(lane == lanes - 1, 0.0, roll(f, -1, 1)) - jnp.where(lane == 0, 0.0, roll(f, 1, 1))) * mz

    b_x, b_y, b_z = fb[0, p], fb[1, p], fb[2, p]
    half = 0.5 if p == 0 else -0.5
    cur_x = d_y(b_z) - d_z(b_y)
    cur_y = d_z(b_x) - half * fb[2, 1 - p]
    cur_z = half * fb[1, 1 - p] - d_y(b_x)
    dens = den[p]
    return (
        (cur_y * b_z - cur_z * b_y) / dens,
        (cur_z * b_x - cur_x * b_z) / dens,
        (cur_x * b_y - cur_y * b_x) / dens,
    )


def fetched(far, near, sems):
    copies = [pltpu.make_async_copy(a, b, sems.at[n]) for n, (a, b) in enumerate(zip(far, near))]
    for copy in copies:
        copy.start()
    for copy in copies:
        copy.wait()


def metrics(ly_ref, lz_ref, shape):
    half_y = jnp.broadcast_to(0.5 * metric(ly_ref[...]), (8, shape[0]))
    return jnp.broadcast_to(jnp.transpose(half_y)[:, 0:1], shape), 0.5 * metric(lz_ref[...])


def border_kernel(ly_far, fb_far, den_far, upper_ref, lower_ref, levels, top, bottom, dens, sems):
    last = fb_far.shape[2] - 8
    far = (ly_far, fb_far.at[:, :, 0:8, :], fb_far.at[:, :, last : last + 8, :], den_far.at[:, 0:8, :])
    fetched(far, (levels, top, bottom, dens), sems)
    for p in range(2):
        for comp in range(3):
            upper_ref[2 * comp + p : 2 * comp + p + 1, :] = top[comp, p, 0:1, :]
        for n, comp in enumerate((0, 2)):
            upper_ref[6 + 2 * n + p : 7 + 2 * n + p, :] = top[comp, p, 1:2, :]
            lower_ref[2 * n + p : 2 * n + p + 1, :] = bottom[comp, p, 7:8, :]
        upper_ref[10 + p : 11 + p, :] = dens[p, 0:1, :]
    scale = 0.5 * metric(levels[...])[:, 0:1]
    upper_ref[12:16, :] = jnp.broadcast_to(scale, (4, upper_ref.shape[1]))


def message_kernel(*refs):
    far, table_ref, outs, near, sems = refs[0:4], refs[4], refs[5:12], refs[12:16], refs[16]
    msg_ref, held_ref, emf_ref, tips_ref, low_ref, last_ref, half_ref = outs
    table_copy = pltpu.make_async_copy(table_ref.at[lax.axis_index("xh")], half_ref, sems.at[4])
    table_copy.start()
    fetched(far, near, sems)
    ly_ref, lz_ref, fb, den = near
    shape = fb.shape[2:]
    my, mz = metrics(ly_ref, lz_ref, shape)
    lane = lax.broadcasted_iota(jnp.int32, shape, 1)
    edge = (lane == 0) | (lane == 127)
    slot = lane >> 1
    signed = jnp.where(lane == 0, -mz, mz)
    inside, held = [], []
    own = jnp.zeros(shape, F32)
    for p in range(2):
        parts = hall(p, fb, den, my, mz)
        inverse = 1.0 / den[p]
        weight = signed * inverse
        downward, upward = -my[0:1] * inverse[0:1], my[63:64] * inverse[63:64]
        for comp in range(3):
            tips_ref[2 * comp + p] = parts[comp][56:64]
            low_ref[2 * comp + p : 2 * comp + p + 1, :] = parts[comp][0:1]
            low_ref[6 + 3 * p + comp : 7 + 3 * p + comp, :] = downward * fb[comp, p, 0:1, :]
            last_ref[3 * p + comp : 3 * p + comp + 1, :] = upward * fb[comp, p, 63:64, :]
            last_ref[6 + 2 * comp + p : 7 + 2 * comp + p, :] = fb[comp, p, 63:64, :]
        fields = [fb[comp, p] for comp in range(3)]
        inside.append([jnp.where(edge, 0.0, part) for part in parts])
        terms = list(parts) + [f * weight for f in fields] + fields[0:2]
        packed = jnp.zeros(shape, F32)
        for q, term in enumerate(terms):
            packed = jnp.where(slot == q, roll(term, 2 * q + 1, 1), packed)
        held.append(packed)
        for comp in range(2):
            k = 2 * p + comp
            own = jnp.where(slot == k, roll(fields[comp], 2 * k + 1, 1), own)
        for comp in range(3):
            emf_ref[comp, p] = inside[p][comp].astype(BF)
    last_ref[12:13, :] = mz
    last_ref[13:16, :] = jnp.zeros((3, shape[1]), F32)
    low_ref[12:16, :] = jnp.zeros((4, shape[1]), F32)
    held_ref[...] = held[0] + roll(held[1], 16, 1)
    first = own.astype(BF).astype(F32)
    own = own - first
    second = own.astype(BF).astype(F32)
    own = first + roll(second, 8, 1) + roll(own - second, 16, 1)
    folded = roll(own[0:16], 32, 1)
    for block in range(1, 4):
        folded = folded + roll(own[16 * block : 16 * block + 16], 32 + 24 * block, 1)
    held = [roll(x, -1, 0) for x in held]
    inside = [[roll(x, -1, 0) for x in plane] for plane in inside]
    for block in range(8):
        rows = slice(8 * block, 8 * block + 8)
        tile = jnp.concatenate([held[0][rows], held[1][rows]], axis=0)
        high = tile.astype(BF).astype(F32)
        low = (tile - high).astype(BF).astype(F32)
        values = [jnp.concatenate([inside[0][comp][rows], inside[1][comp][rows]], axis=0) for comp in range(3)]
        values.append(high + roll(low, 16, 1) + folded)
        for n, value in enumerate(values):
            for copy in range(2):
                msg_ref[2 * block + copy, 16 * n : 16 * n + 16, :] = value.astype(BF)
    table_copy.wait()


def changes(f_x, f_z, weights_ref, at):
    w_x, w_y, w_z = (weights_ref[at + comp : at + comp + 1, :] for comp in range(3))
    return (f_x * w_y, -(f_x * w_x + f_z * w_z), f_z * w_y)


def rim_kernel(next_ref, msg_ref, held_ref, emf_ref, tips_ref, last_ref, msg_out, held_out, emf_out):
    msg_out[...] = msg_ref[...]
    held_out[...] = held_ref[...]
    emf_out[...] = emf_ref[...]
    shape = (8, emf_ref.shape[3])
    row = lax.broadcasted_iota(jnp.int32, shape, 0)
    lane = lax.broadcasted_iota(jnp.int32, shape, 1)
    inner = (lane > 0) & (lane < 127)
    slot = lane >> 1
    mz = last_ref[12:13, :]
    line = lax.broadcasted_iota(jnp.int32, (1, shape[1]), 1)
    signed = jnp.where(line == 0, -mz, mz)
    beyond = next_ref[...]
    wide = lax.broadcasted_iota(jnp.int32, beyond.shape, 1)
    slope = (jnp.where(wide == 127, 0.0, roll(beyond, -1, 1)) - jnp.where(wide == 0, 0.0, roll(beyond, 1, 1))) * mz
    my = beyond[12:13]
    rows = slice(56, 64)
    held = held_ref[rows, :]
    values, tiles = [], []
    for p in range(2):
        f = [beyond[2 * comp + p : 2 * comp + p + 1] for comp in range(3)]
        g = [beyond[2 * comp + 1 - p : 2 * comp + 2 - p] for comp in range(3)]
        d_z = [slope[2 * comp + p : 2 * comp + p + 1] for comp in range(2)]
        dy_x = (beyond[6 + p : 7 + p] - last_ref[6 + p : 7 + p, :]) * my
        dy_z = (beyond[8 + p : 9 + p] - last_ref[10 + p : 11 + p, :]) * my
        half = 0.5 if p == 0 else -0.5
        cur_x, cur_y, cur_z = dy_z - d_z[1], d_z[0] - half * g[2], half * g[1] - dy_x
        dens = beyond[10 + p : 11 + p]
        made = [
            (cur_y * f[2] - cur_z * f[1]) / dens,
            (cur_z * f[0] - cur_x * f[2]) / dens,
            (cur_x * f[1] - cur_y * f[0]) / dens,
        ]
        weight = signed / dens
        terms = made + [x * weight for x in f] + f[0:2]
        packed = jnp.zeros(shape, F32)
        for q, term in enumerate(terms):
            packed = jnp.where(slot == q, roll(jnp.broadcast_to(term, shape), 2 * q + 1, 1), packed)
        extra = changes(f[0], f[2], last_ref, 3 * p)
        for comp in range(3):
            change = jnp.where(row == 7, extra[comp], 0.0)
            value = jnp.where(inner, tips_ref[2 * comp + p] + change, 0.0)
            emf_out[comp, p, rows, :] = value.astype(BF)
            values.append(jnp.where(row == 7, jnp.where(inner, made[comp], 0.0), roll(value, -1, 0)))
            held = held + jnp.where(slot == 8 * p + comp, roll(change, 16 * p + 2 * comp + 1, 1), 0.0)
        tiles.append(packed)
    held_out[rows, :] = held
    for p in range(2):
        moved = roll(held if p == 0 else roll(held, -16, 1), -1, 0)
        tiles[p] = jnp.where(lane < 16, jnp.where(row == 7, tiles[p], moved), 0.0)
    tile = jnp.concatenate(tiles, axis=0)
    high = tile.astype(BF).astype(F32)
    low = (tile - high).astype(BF).astype(F32)
    old = msg_ref[14, 48:64, :].astype(F32)
    tiles = [jnp.concatenate([values[comp], values[3 + comp]], axis=0) for comp in range(3)]
    tiles.append(jnp.where(wide < 32, high + roll(low, 16, 1), old))
    for n, value in enumerate(tiles):
        for copy in range(2):
            msg_out[14 + copy, 16 * n : 16 * n + 16, :] = value.astype(BF)


def finished(held, beside):
    slot = (lax.broadcasted_iota(jnp.int32, held.shape, 1) >> 1) & 7
    flat = roll(beside, -12, 1) * jnp.where(slot == 0, roll(held, -10, 1), roll(held, -8, 1))
    upright = roll(beside, -10, 1) * roll(held, -4, 1) + roll(beside, -8, 1) * roll(held, -2, 1)
    return held + jnp.where(slot == 2, -upright, flat)


def at_edges(values, spot):
    lane = lax.broadcasted_iota(jnp.int32, values.shape, 1)
    return jnp.where((lane == 0) | (lane == 127), roll(values, -spot, 1), 0.0).astype(BF)


def line_edges(x_ref):
    held = jnp.concatenate([x_ref[i, 48:64, :] for i in range(16)], axis=0).astype(F32)
    held = held + roll(held, -16, 1)
    lane = lax.broadcasted_iota(jnp.int32, held.shape, 1)
    beside = jnp.where((lane & 1) == 0, roll(roll(held, -16, 0), -1, 1), roll(roll(held, 16, 0), 1, 1))
    values = finished(held, beside)
    return [at_edges(values, 2 * comp + 1) for comp in range(3)]


def finish_emf(x_ref, held_ref, inside_ref, low_ref, before_ref, emf_ref):
    me = lax.axis_index("yh") * 4 + lax.axis_index("yl") * 2 + lax.axis_index("xh")

    def fields(block):
        folded = x_ref[block, 48:64, :].astype(F32)
        rows = []
        for n in range(4):
            own = roll(folded, -(32 + 24 * n), 1)
            rows.append(own + (roll(own, -8, 1) + roll(own, -16, 1)))
        return jnp.concatenate(rows, axis=0)

    low, high = fields(lax.rem(me + 15, 16)), fields(lax.rem(me + 1, 16))
    lane = lax.broadcasted_iota(jnp.int32, low.shape, 1)
    beside = jnp.where((lane & 1) == 0, roll(high, -1, 1), roll(low, 1, 1))
    beside = jnp.where(lane < 16, roll(beside, 12, 1), roll(beside, 24, 1))
    shape = (8, low.shape[1])
    row = lax.broadcasted_iota(jnp.int32, shape, 0)
    lane = lax.broadcasted_iota(jnp.int32, shape, 1)
    inner = (lane > 0) & (lane < 127)
    tips = {}
    held = held_ref[0:8, :]
    for p in range(2):
        extra = changes(before_ref[p : p + 1, :], before_ref[2 + p : 3 + p, :], low_ref, 6 + 3 * p)
        for comp in range(3):
            change = jnp.where(row == 0, extra[comp], 0.0)
            value = low_ref[2 * comp + p : 2 * comp + p + 1, :] + extra[comp]
            plain = inside_ref[comp, p, 0:8, :].astype(F32)
            tips[comp, p] = jnp.where(row == 0, jnp.where(inner, value, 0.0), plain)
            moved = roll(change, 16 * p + 2 * comp + 1, 1)
            held = held + jnp.where((lane >> 1) == 8 * p + comp, moved, 0.0)
    values = finished(jnp.concatenate([held, held_ref[8:64, :]], axis=0), beside)
    for comp in range(3):
        for p in range(2):
            edges = at_edges(values, 16 * p + 2 * comp + 1)
            emf_ref[comp, p] = inside_ref[comp, p] + edges
            emf_ref[comp, p, 0:8, :] = (tips[comp, p] + edges[0:8].astype(F32)).astype(BF)


def z_kernel(x_ref, table_ref, held_ref, inside_ref, low_ref, before_ref, out_ref, emf_ref, mix_ref):
    edges = line_edges(x_ref)
    zero = jnp.zeros((16, 512), BF)
    total = None
    for n in range(2):
        sums, gaps = [], []
        for i in range(4 * n, 4 * n + 4):
            for side, pair in ((sums, 1), (gaps, -1)):
                tiles = []
                for c in range(3):
                    near, far = (
                        x_ref[m, 16 * c : 16 * c + 16, :] + edges[c][16 * m : 16 * m + 16] for m in (i, i + 8)
                    )
                    tiles.append(near + far if pair > 0 else near - far)
                side.append(jnp.concatenate(tiles, axis=0))
        sums, gaps = (jnp.concatenate([jnp.concatenate(x, axis=1), zero], axis=0) for x in (sums, gaps))
        empty = jnp.zeros((64, 512), BF)
        lines = jnp.concatenate(
            [jnp.concatenate([sums, empty], axis=0), jnp.concatenate([empty, gaps], axis=0)], axis=1
        )
        blocks = []
        for c in range(2):
            for jl in range(8):
                row = []
                for kappa in (2 * jl, 2 * jl + 1):
                    for i in range(4 * n, 4 * n + 4):
                        m = (kappa * i + 4 * c) % 16
                        cell = table_ref[m % 8, 32 * kappa : 32 * kappa + 32, :]
                        row.append(-cell if m >= 8 else cell)
                blocks.append(jnp.concatenate(row, axis=1))
        product = lax.dot_general(jnp.concatenate(blocks, axis=0), lines, ACROSS, preferred_element_type=F32)
        total = product if n == 0 else total + product
    for c in range(2):
        for jl in range(8):
            at = 32 * (8 * c + jl)
            mix_ref[pl.ds(2 * jl + c, 32, stride=16), :] = total[at : at + 32]
    out_ref[...] = mix_ref[...].astype(BF)
    finish_emf(x_ref, held_ref, inside_ref, low_ref, before_ref, emf_ref)


def add(a, b):
    return (a[0] + b[0], a[1] + b[1])


def sub(a, b):
    return (a[0] - b[0], a[1] - b[1])


def turned(a, eighths):
    eighths %= 16
    if eighths == 0:
        return a
    if eighths == 4:
        return (a[1], -a[0])
    if eighths == 2:
        r = math.sqrt(0.5)
        return ((a[0] + a[1]) * r, (a[1] - a[0]) * r)
    if eighths == 6:
        r = math.sqrt(0.5)
        return ((a[1] - a[0]) * r, -(a[0] + a[1]) * r)
    cos, sin = math.cos(math.pi * eighths / 8), math.sin(math.pi * eighths / 8)
    return (a[0] * cos + a[1] * sin, a[1] * cos - a[0] * sin)


def fourier4(x):
    s, d = add(x[0], x[2]), sub(x[0], x[2])
    t, u = add(x[1], x[3]), turned(sub(x[1], x[3]), 4)
    return [add(s, t), add(d, u), sub(s, t), sub(d, u)]


def fourier8(x):
    even = fourier4([x[0], x[2], x[4], x[6]])
    odd = fourier4([x[1], x[3], x[5], x[7]])
    odd = [turned(value, 2 * k) for k, value in enumerate(odd)]
    return [add(a, b) for a, b in zip(even, odd)] + [sub(a, b) for a, b in zip(even, odd)]


def y_kernel(x_ref, table_ref, turn_ref, order_ref, bins_ref, power_ref, sums_ref):
    lhs = lax.dot_general(order_ref[...], x_ref[...], ACROSS, preferred_element_type=F32).astype(BF)
    product = jnp.dot(lhs, table_ref[...], preferred_element_type=F32)
    scale = 1.0 / (6.0 * NY)
    for e in range(2):
        held = []
        for y0 in range(8):
            at = 16 * y0 + 8 * e
            a, b = product[at : at + 8, 0:256], product[at : at + 8, 256:512]
            if y0 > 0:
                cos, sin = turn_ref[0, y0 : y0 + 1, :], turn_ref[1, y0 : y0 + 1, :]
                a, b = a * cos + b * sin, b * cos - a * sin
            held.append((a, b))
        for q1, (a, b) in enumerate(fourier8(held)):
            power_ref[e : e + 1, 256 * q1 : 256 * q1 + 256] = (
                jnp.sum(a * a + b * b, axis=0, keepdims=True) * scale
            )
    sums = jnp.zeros((32, 128), F32)
    steps = lax.broadcasted_iota(jnp.int32, (128, 128), 0).astype(F32).astype(BF)
    one, none = jnp.ones((128, 128), BF), jnp.zeros((128, 128), BF)
    for e in range(2):
        value = power_ref[e : e + 1, :]
        bins = bins_ref[e : e + 1, :]
        coarse = lax.broadcasted_iota(jnp.int32, (8, NY), 0) == (bins >> 7)
        within = jnp.broadcast_to((bins & 127).astype(F32), (16, NY)).astype(BF)
        fine = []
        for n in range(NY // 128):
            tile = within[:, 128 * n : 128 * n + 128]
            fine.append(jnp.where(steps == jnp.concatenate([tile] * 8, axis=0), one, none))
        spread = jnp.where(coarse, value, 0.0)
        first = spread.astype(BF).astype(F32)
        second = (spread - first).astype(BF).astype(F32)
        third = spread - first - second
        pieces = jnp.concatenate([third, second, first, jnp.zeros_like(first)], axis=0).astype(BF)
        sums += lax.dot_general(pieces, jnp.concatenate(fine, axis=1), ACROSS, preferred_element_type=F32)
    sums = sums[0:8] + sums[8:16] + sums[16:24]
    sums = sums * (NB / (KZ * NY))
    for copy in range(sums_ref.shape[0]):
        sums_ref[copy] = sums


def on_device(field_b, density, level_y, level_z, bins):
    y_local, z_local = field_b.shape[2], field_b.shape[3]

    def shift(cells, axis, step):
        count = lax.axis_size(axis)
        return lax.ppermute(cells, axis, [(i, (i + step) % count) for i in range(count)])

    small = pltpu.CompilerParams(vmem_limit_bytes=16 * 2**20)
    far = [
        pltpu.with_memory_space_constraint(x, pltpu.HBM)
        for x in (level_y[None, :], level_z[None, :], field_b, density)
    ]
    upper, lower = pl.pallas_call(
        border_kernel,
        out_shape=(jax.ShapeDtypeStruct((16, z_local), F32), jax.ShapeDtypeStruct((4, z_local), F32)),
        in_specs=[pl.BlockSpec(memory_space=pltpu.HBM)] * 3,
        scratch_shapes=[
            pltpu.VMEM((1, y_local), jnp.int32),
            pltpu.VMEM((3, 2, 8, z_local), F32),
            pltpu.VMEM((3, 2, 8, z_local), F32),
            pltpu.VMEM((2, 8, z_local), F32),
            pltpu.SemaphoreType.DMA((4,)),
        ],
        compiler_params=small,
    )(far[0], far[2], far[3])
    after = shift(upper, GY, -1)
    before = shift(lower, GY, 1)
    scratch = [
        pltpu.VMEM((1, y_local), jnp.int32),
        pltpu.VMEM((1, z_local), jnp.int32),
        pltpu.VMEM(field_b.shape, F32),
        pltpu.VMEM(density.shape, F32),
        pltpu.SemaphoreType.DMA((5,)),
    ]
    made = (
        jax.ShapeDtypeStruct((16, 64, z_local), BF),
        jax.ShapeDtypeStruct((y_local, z_local), F32),
        jax.ShapeDtypeStruct(field_b.shape, BF),
    )
    rows = [jax.ShapeDtypeStruct(shape, F32) for shape in ((6, 8, z_local), (16, z_local), (16, z_local))]
    table = pltpu.with_memory_space_constraint(jnp.asarray(z_table()), pltpu.HBM)
    message, held, inside, tips, low, last, half = pl.pallas_call(
        message_kernel,
        out_shape=made + tuple(rows) + (jax.ShapeDtypeStruct(table.shape[1:], BF),),
        in_specs=[pl.BlockSpec(memory_space=pltpu.HBM)] * 5,
        scratch_shapes=scratch,
        compiler_params=small,
        cost_estimate=pl.CostEstimate(flops=2_000_000, bytes_accessed=2_000_000, transcendentals=0),
    )(*far, table)
    message, held, inside = pl.pallas_call(rim_kernel, out_shape=made, compiler_params=small)(
        after, message, held, inside, tips, last
    )
    lines = lax.all_to_all(message, GZ, 0, 0, tiled=True)
    z_modes, emf = pl.pallas_call(
        z_kernel,
        out_shape=(jax.ShapeDtypeStruct((512, 128), BF), jax.ShapeDtypeStruct(field_b.shape, BF)),
        scratch_shapes=[pltpu.VMEM((512, 128), F32)],
        compiler_params=small,
    )(lines, half, held, inside, low, before)
    spread = lax.all_to_all(z_modes.reshape(256, 2, 128), ("yh", "yl") + GY, 0, 0, tiled=True).reshape(512, 128)
    first = ("yh", "yl", "c")
    second = ("xh", "z", "xl")
    mode_power, sums = pl.pallas_call(
        y_kernel,
        out_shape=(
            jax.ShapeDtypeStruct((2, NY), F32),
            jax.ShapeDtypeStruct((lax.axis_size(first), 8, 128), F32),
        ),
        compiler_params=small,
    )(spread, *y_tables(), bins)
    sums = jnp.sum(lax.all_to_all(sums, first, 0, 0, tiled=True), axis=0)
    copies = jnp.broadcast_to(sums.astype(BF)[None], (lax.axis_size(second), 8, 128))
    spectrum = jnp.sum(lax.all_to_all(copies, second, 0, 0, tiled=True).astype(F32), axis=0).reshape(NB)
    return (emf, mode_power, spectrum)


def solution(mesh):
    fine = Mesh(mesh.devices.reshape(4, 2, 2, 8, 2, 2), GZ + GY)
    placed = (
        P(None, None, GY, GZ),
        P(None, GY, GZ),
        P(GY),
        P(GZ),
        P(GZ + GY, None),
    )
    return jax.shard_map(
        on_device,
        mesh=fine,
        in_specs=placed,
        out_specs=(P(None, None, GY, GZ), P(GZ + GY, None), P()),
        check_vma=False,
    )
```

```python
import math

import jax
import jax.numpy as jnp
import numpy as np
from jax import lax
from jax.experimental import pallas as pl
from jax.experimental.pallas import tpu as pltpu
from jax.sharding import Mesh, PartitionSpec as P

NY = 2048
NZ = 2048
NB = 1024
KZ = 1024
BF = jnp.bfloat16
F32 = jnp.float32
GZ = ("yh", "yl", "xh")
GY = ('z', 'xl', 'c')
ACROSS = (((1,), (1,)), ((), ()))


def angle(a, b, length):
    return 2.0 * math.pi * ((a[:, None] * b[None, :]) % length) / length


def z_table():
    part, kappa, y, jh = np.meshgrid(*(np.arange(n) for n in (2, 16, 8, 4)), indexing="ij")
    modes = (16 * (8 * y + 4 * part + jh) + kappa).reshape(2, 1, 512, 1)
    turn = (modes * np.arange(128) % NZ + 128 * np.arange(8).reshape(1, 8, 1, 1)) % NZ
    return (np.cos(2.0 * math.pi * turn / NZ) / math.sqrt(NZ)).astype(jnp.bfloat16)


def y_tables():
    inner = angle((8 * np.arange(32)[None, :] + np.arange(8)[:, None]).reshape(-1), np.arange(256), 256)
    cos, sin = np.cos(inner), np.sin(inner)
    table = np.stack([np.stack([cos, -sin], axis=1), np.stack([sin, cos], axis=1)], axis=1)
    turn = angle(np.arange(8), np.arange(256), NY)
    order = np.zeros((128, 128), np.float32)
    for e in range(2):
        for cp in range(6):
            for y0 in range(8):
                order[16 * y0 + 8 * e + cp, 64 * e + 8 * cp + y0] = 1.0
    return (
        table.reshape(512, 512).astype(jnp.bfloat16),
        np.stack([np.cos(turn), np.sin(turn)]).astype(np.float32),
        order.astype(jnp.bfloat16),
    )


def metric(level):
    return 1.0 / (1.0 + 0.25 * level.astype(F32))


def roll(x, by, axis):
    return pltpu.roll(x, by % x.shape[axis], axis)


def hall(p, fb, den, my, mz):
    rows, lanes = fb.shape[2], fb.shape[3]
    row = lax.broadcasted_iota(jnp.int32, (rows, lanes), 0)
    lane = lax.broadcasted_iota(jnp.int32, (rows, lanes), 1)

    def d_y(f):
        return (jnp.where(row == rows - 1, 0.0, roll(f, -1, 0)) - jnp.where(row == 0, 0.0, roll(f, 1, 0))) * my

    def d_z(f):
        return (jnp.where(lane == lanes - 1, 0.0, roll(f, -1, 1)) - jnp.where(lane == 0, 0.0, roll(f, 1, 1))) * mz

    b_x, b_y, b_z = fb[0, p], fb[1, p], fb[2, p]
    half = 0.5 if p == 0 else -0.5
    cur_x = d_y(b_z) - d_z(b_y)
    cur_y = d_z(b_x) - half * fb[2, 1 - p]
    cur_z = half * fb[1, 1 - p] - d_y(b_x)
    dens = den[p]
    return (
        (cur_y * b_z - cur_z * b_y) / dens,
        (cur_z * b_x - cur_x * b_z) / dens,
        (cur_x * b_y - cur_y * b_x) / dens,
    )


def fetched(far, near, sems):
    copies = [pltpu.make_async_copy(a, b, sems.at[n]) for n, (a, b) in enumerate(zip(far, near))]
    for copy in copies:
        copy.start()
    for copy in copies:
        copy.wait()


def metrics(ly_ref, lz_ref, shape):
    half_y = jnp.broadcast_to(0.5 * metric(ly_ref[...]), (8, shape[0]))
    return jnp.broadcast_to(jnp.transpose(half_y)[:, 0:1], shape), 0.5 * metric(lz_ref[...])


def border_kernel(ly_far, fb_far, den_far, upper_ref, lower_ref, levels, top, bottom, dens, sems):
    last = fb_far.shape[2] - 8
    far = (ly_far, fb_far.at[:, :, 0:8, :], fb_far.at[:, :, last : last + 8, :], den_far.at[:, 0:8, :])
    fetched(far, (levels, top, bottom, dens), sems)
    for p in range(2):
        for comp in range(3):
            upper_ref[2 * comp + p : 2 * comp + p + 1, :] = top[comp, p, 0:1, :]
        for n, comp in enumerate((0, 2)):
            upper_ref[6 + 2 * n + p : 7 + 2 * n + p, :] = top[comp, p, 1:2, :]
            lower_ref[2 * n + p : 2 * n + p + 1, :] = bottom[comp, p, 7:8, :]
        upper_ref[10 + p : 11 + p, :] = dens[p, 0:1, :]
    scale = 0.5 * metric(levels[...])[:, 0:1]
    upper_ref[12:16, :] = jnp.broadcast_to(scale, (4, upper_ref.shape[1]))


def message_kernel(*refs):
    far, table_ref, outs, near, sems = refs[0:4], refs[4], refs[5:12], refs[12:16], refs[16]
    msg_ref, held_ref, emf_ref, tips_ref, low_ref, last_ref, half_ref = outs
    table_copy = pltpu.make_async_copy(table_ref.at[lax.axis_index("xh")], half_ref, sems.at[4])
    table_copy.start()
    fetched(far, near, sems)
    ly_ref, lz_ref, fb, den = near
    shape = fb.shape[2:]
    my, mz = metrics(ly_ref, lz_ref, shape)
    lane = lax.broadcasted_iota(jnp.int32, shape, 1)
    edge = (lane == 0) | (lane == 127)
    slot = lane >> 1
    signed = jnp.where(lane == 0, -mz, mz)
    inside, held = [], []
    own = jnp.zeros(shape, F32)
    for p in range(2):
        parts = hall(p, fb, den, my, mz)
        inverse = 1.0 / den[p]
        weight = signed * inverse
        downward, upward = -my[0:1] * inverse[0:1], my[63:64] * inverse[63:64]
        for comp in range(3):
            tips_ref[2 * comp + p] = parts[comp][56:64]
            low_ref[2 * comp + p : 2 * comp + p + 1, :] = parts[comp][0:1]
            low_ref[6 + 3 * p + comp : 7 + 3 * p + comp, :] = downward * fb[comp, p, 0:1, :]
            last_ref[3 * p + comp : 3 * p + comp + 1, :] = upward * fb[comp, p, 63:64, :]
            last_ref[6 + 2 * comp + p : 7 + 2 * comp + p, :] = fb[comp, p, 63:64, :]
        fields = [fb[comp, p] for comp in range(3)]
        inside.append([jnp.where(edge, 0.0, part) for part in parts])
        terms = list(parts) + [f * weight for f in fields] + fields[0:2]
        packed = jnp.zeros(shape, F32)
        for q, term in enumerate(terms):
            packed = jnp.where(slot == q, roll(term, 2 * q + 1, 1), packed)
        held.append(packed)
        for comp in range(2):
            k = 2 * p + comp
            own = jnp.where(slot == k, roll(fields[comp], 2 * k + 1, 1), own)
        for comp in range(3):
            emf_ref[comp, p] = inside[p][comp].astype(BF)
    last_ref[12:13, :] = mz
    last_ref[13:16, :] = jnp.zeros((3, shape[1]), F32)
    low_ref[12:16, :] = jnp.zeros((4, shape[1]), F32)
    held_ref[...] = held[0] + roll(held[1], 16, 1)
    first = own.astype(BF).astype(F32)
    own = own - first
    second = own.astype(BF).astype(F32)
    own = first + roll(second, 8, 1) + roll(own - second, 16, 1)
    folded = roll(own[0:16], 32, 1)
    for block in range(1, 4):
        folded = folded + roll(own[16 * block : 16 * block + 16], 32 + 24 * block, 1)
    held = [roll(x, -1, 0) for x in held]
    inside = [[roll(x, -1, 0) for x in plane] for plane in inside]
    for block in range(8):
        rows = slice(8 * block, 8 * block + 8)
        tile = jnp.concatenate([held[0][rows], held[1][rows]], axis=0)
        high = tile.astype(BF).astype(F32)
        low = (tile - high).astype(BF).astype(F32)
        values = [jnp.concatenate([inside[0][comp][rows], inside[1][comp][rows]], axis=0) for comp in range(3)]
        values.append(high + roll(low, 16, 1) + folded)
        for n, value in enumerate(values):
            for copy in range(2):
                msg_ref[2 * block + copy, 16 * n : 16 * n + 16, :] = value.astype(BF)
    table_copy.wait()


def changes(f_x, f_z, weights_ref, at):
    w_x, w_y, w_z = (weights_ref[at + comp : at + comp + 1, :] for comp in range(3))
    return (f_x * w_y, -(f_x * w_x + f_z * w_z), f_z * w_y)


def rim_kernel(next_ref, msg_ref, held_ref, emf_ref, tips_ref, last_ref, msg_out, held_out, emf_out):
    msg_out[...] = msg_ref[...]
    held_out[...] = held_ref[...]
    emf_out[...] = emf_ref[...]
    shape = (8, emf_ref.shape[3])
    row = lax.broadcasted_iota(jnp.int32, shape, 0)
    lane = lax.broadcasted_iota(jnp.int32, shape, 1)
    inner = (lane > 0) & (lane < 127)
    slot = lane >> 1
    mz = last_ref[12:13, :]
    line = lax.broadcasted_iota(jnp.int32, (1, shape[1]), 1)
    signed = jnp.where(line == 0, -mz, mz)
    beyond = next_ref[...]
    wide = lax.broadcasted_iota(jnp.int32, beyond.shape, 1)
    slope = (jnp.where(wide == 127, 0.0, roll(beyond, -1, 1)) - jnp.where(wide == 0, 0.0, roll(beyond, 1, 1))) * mz
    my = beyond[12:13]
    rows = slice(56, 64)
    held = held_ref[rows, :]
    values, tiles = [], []
    for p in range(2):
        f = [beyond[2 * comp + p : 2 * comp + p + 1] for comp in range(3)]
        g = [beyond[2 * comp + 1 - p : 2 * comp + 2 - p] for comp in range(3)]
        d_z = [slope[2 * comp + p : 2 * comp + p + 1] for comp in range(2)]
        dy_x = (beyond[6 + p : 7 + p] - last_ref[6 + p : 7 + p, :]) * my
        dy_z = (beyond[8 + p : 9 + p] - last_ref[10 + p : 11 + p, :]) * my
        half = 0.5 if p == 0 else -0.5
        cur_x, cur_y, cur_z = dy_z - d_z[1], d_z[0] - half * g[2], half * g[1] - dy_x
        dens = beyond[10 + p : 11 + p]
        made = [
            (cur_y * f[2] - cur_z * f[1]) / dens,
            (cur_z * f[0] - cur_x * f[2]) / dens,
            (cur_x * f[1] - cur_y * f[0]) / dens,
        ]
        weight = signed / dens
        terms = made + [x * weight for x in f] + f[0:2]
        packed = jnp.zeros(shape, F32)
        for q, term in enumerate(terms):
            packed = jnp.where(slot == q, roll(jnp.broadcast_to(term, shape), 2 * q + 1, 1), packed)
        extra = changes(f[0], f[2], last_ref, 3 * p)
        for comp in range(3):
            change = jnp.where(row == 7, extra[comp], 0.0)
            value = jnp.where(inner, tips_ref[2 * comp + p] + change, 0.0)
            emf_out[comp, p, rows, :] = value.astype(BF)
            values.append(jnp.where(row == 7, jnp.where(inner, made[comp], 0.0), roll(value, -1, 0)))
            held = held + jnp.where(slot == 8 * p + comp, roll(change, 16 * p + 2 * comp + 1, 1), 0.0)
        tiles.append(packed)
    held_out[rows, :] = held
    for p in range(2):
        moved = roll(held if p == 0 else roll(held, -16, 1), -1, 0)
        tiles[p] = jnp.where(lane < 16, jnp.where(row == 7, tiles[p], moved), 0.0)
    tile = jnp.concatenate(tiles, axis=0)
    high = tile.astype(BF).astype(F32)
    low = (tile - high).astype(BF).astype(F32)
    old = msg_ref[14, 48:64, :].astype(F32)
    tiles = [jnp.concatenate([values[comp], values[3 + comp]], axis=0) for comp in range(3)]
    tiles.append(jnp.where(wide < 32, high + roll(low, 16, 1), old))
    for n, value in enumerate(tiles):
        for copy in range(2):
            msg_out[14 + copy, 16 * n : 16 * n + 16, :] = value.astype(BF)


def finished(held, beside):
    slot = (lax.broadcasted_iota(jnp.int32, held.shape, 1) >> 1) & 7
    flat = roll(beside, -12, 1) * jnp.where(slot == 0, roll(held, -10, 1), roll(held, -8, 1))
    upright = roll(beside, -10, 1) * roll(held, -4, 1) + roll(beside, -8, 1) * roll(held, -2, 1)
    return held + jnp.where(slot == 2, -upright, flat)


def at_edges(values, spot):
    lane = lax.broadcasted_iota(jnp.int32, values.shape, 1)
    return jnp.where((lane == 0) | (lane == 127), roll(values, -spot, 1), 0.0).astype(BF)


def line_edges(x_ref):
    held = jnp.concatenate([x_ref[i, 48:64, :] for i in range(16)], axis=0).astype(F32)
    held = held + roll(held, -16, 1)
    lane = lax.broadcasted_iota(jnp.int32, held.shape, 1)
    beside = jnp.where((lane & 1) == 0, roll(roll(held, -16, 0), -1, 1), roll(roll(held, 16, 0), 1, 1))
    values = finished(held, beside)
    return [at_edges(values, 2 * comp + 1) for comp in range(3)]


def finish_emf(x_ref, held_ref, inside_ref, low_ref, before_ref, emf_ref):
    me = lax.axis_index("yh") * 4 + lax.axis_index("yl") * 2 + lax.axis_index("xh")

    def fields(block):
        folded = x_ref[block, 48:64, :].astype(F32)
        rows = []
        for n in range(4):
            own = roll(folded, -(32 + 24 * n), 1)
            rows.append(own + (roll(own, -8, 1) + roll(own, -16, 1)))
        return jnp.concatenate(rows, axis=0)

    low, high = fields(lax.rem(me + 15, 16)), fields(lax.rem(me + 1, 16))
    lane = lax.broadcasted_iota(jnp.int32, low.shape, 1)
    beside = jnp.where((lane & 1) == 0, roll(high, -1, 1), roll(low, 1, 1))
    beside = jnp.where(lane < 16, roll(beside, 12, 1), roll(beside, 24, 1))
    shape = (8, low.shape[1])
    row = lax.broadcasted_iota(jnp.int32, shape, 0)
    lane = lax.broadcasted_iota(jnp.int32, shape, 1)
    inner = (lane > 0) & (lane < 127)
    tips = {}
    held = held_ref[0:8, :]
    for p in range(2):
        extra = changes(before_ref[p : p + 1, :], before_ref[2 + p : 3 + p, :], low_ref, 6 + 3 * p)
        for comp in range(3):
            change = jnp.where(row == 0, extra[comp], 0.0)
            value = low_ref[2 * comp + p : 2 * comp + p + 1, :] + extra[comp]
            plain = inside_ref[comp, p, 0:8, :].astype(F32)
            tips[comp, p] = jnp.where(row == 0, jnp.where(inner, value, 0.0), plain)
            moved = roll(change, 16 * p + 2 * comp + 1, 1)
            held = held + jnp.where((lane >> 1) == 8 * p + comp, moved, 0.0)
    values = finished(jnp.concatenate([held, held_ref[8:64, :]], axis=0), beside)
    for comp in range(3):
        for p in range(2):
            edges = at_edges(values, 16 * p + 2 * comp + 1)
            emf_ref[comp, p] = inside_ref[comp, p] + edges
            emf_ref[comp, p, 0:8, :] = (tips[comp, p] + edges[0:8].astype(F32)).astype(BF)


def z_kernel(x_ref, table_ref, held_ref, inside_ref, low_ref, before_ref, out_ref, emf_ref, mix_ref):
    edges = line_edges(x_ref)
    zero = jnp.zeros((16, 512), BF)
    total = None
    for n in range(2):
        sums, gaps = [], []
        for i in range(4 * n, 4 * n + 4):
            for side, pair in ((sums, 1), (gaps, -1)):
                tiles = []
                for c in range(3):
                    near, far = (
                        x_ref[m, 16 * c : 16 * c + 16, :] + edges[c][16 * m : 16 * m + 16] for m in (i, i + 8)
                    )
                    tiles.append(near + far if pair > 0 else near - far)
                side.append(jnp.concatenate(tiles, axis=0))
        sums, gaps = (jnp.concatenate([jnp.concatenate(x, axis=1), zero], axis=0) for x in (sums, gaps))
        empty = jnp.zeros((64, 512), BF)
        lines = jnp.concatenate(
            [jnp.concatenate([sums, empty], axis=0), jnp.concatenate([empty, gaps], axis=0)], axis=1
        )
        blocks = []
        for c in range(2):
            for jl in range(8):
                row = []
                for kappa in (2 * jl, 2 * jl + 1):
                    for i in range(4 * n, 4 * n + 4):
                        m = (kappa * i + 4 * c) % 16
                        cell = table_ref[m % 8, 32 * kappa : 32 * kappa + 32, :]
                        row.append(-cell if m >= 8 else cell)
                blocks.append(jnp.concatenate(row, axis=1))
        product = lax.dot_general(jnp.concatenate(blocks, axis=0), lines, ACROSS, preferred_element_type=F32)
        total = product if n == 0 else total + product
    for c in range(2):
        for jl in range(8):
            at = 32 * (8 * c + jl)
            mix_ref[pl.ds(2 * jl + c, 32, stride=16), :] = total[at : at + 32]
    out_ref[...] = mix_ref[...].astype(BF)
    finish_emf(x_ref, held_ref, inside_ref, low_ref, before_ref, emf_ref)


def add(a, b):
    return (a[0] + b[0], a[1] + b[1])


def sub(a, b):
    return (a[0] - b[0], a[1] - b[1])


def turned(a, eighths):
    eighths %= 16
    if eighths == 0:
        return a
    if eighths == 4:
        return (a[1], -a[0])
    if eighths == 2:
        r = math.sqrt(0.5)
        return ((a[0] + a[1]) * r, (a[1] - a[0]) * r)
    if eighths == 6:
        r = math.sqrt(0.5)
        return ((a[1] - a[0]) * r, -(a[0] + a[1]) * r)
    cos, sin = math.cos(math.pi * eighths / 8), math.sin(math.pi * eighths / 8)
    return (a[0] * cos + a[1] * sin, a[1] * cos - a[0] * sin)


def fourier4(x):
    s, d = add(x[0], x[2]), sub(x[0], x[2])
    t, u = add(x[1], x[3]), turned(sub(x[1], x[3]), 4)
    return [add(s, t), add(d, u), sub(s, t), sub(d, u)]


def fourier8(x):
    even = fourier4([x[0], x[2], x[4], x[6]])
    odd = fourier4([x[1], x[3], x[5], x[7]])
    odd = [turned(value, 2 * k) for k, value in enumerate(odd)]
    return [add(a, b) for a, b in zip(even, odd)] + [sub(a, b) for a, b in zip(even, odd)]


def y_kernel(x_ref, table_ref, turn_ref, order_ref, bins_ref, power_ref, sums_ref):
    lhs = lax.dot_general(order_ref[...], x_ref[...], ACROSS, preferred_element_type=F32).astype(BF)
    product = jnp.dot(lhs, table_ref[...], preferred_element_type=F32)
    scale = 1.0 / (6.0 * NY)
    for e in range(2):
        held = []
        for y0 in range(8):
            at = 16 * y0 + 8 * e
            a, b = product[at : at + 8, 0:256], product[at : at + 8, 256:512]
            if y0 > 0:
                cos, sin = turn_ref[0, y0 : y0 + 1, :], turn_ref[1, y0 : y0 + 1, :]
                a, b = a * cos + b * sin, b * cos - a * sin
            held.append((a, b))
        for q1, (a, b) in enumerate(fourier8(held)):
            power_ref[e : e + 1, 256 * q1 : 256 * q1 + 256] = (
                jnp.sum(a * a + b * b, axis=0, keepdims=True) * scale
            )
    sums = jnp.zeros((32, 128), F32)
    steps = lax.broadcasted_iota(jnp.int32, (128, 128), 0).astype(F32).astype(BF)
    one, none = jnp.ones((128, 128), BF), jnp.zeros((128, 128), BF)
    for e in range(2):
        value = power_ref[e : e + 1, :]
        bins = bins_ref[e : e + 1, :]
        coarse = lax.broadcasted_iota(jnp.int32, (8, NY), 0) == (bins >> 7)
        within = jnp.broadcast_to((bins & 127).astype(F32), (16, NY)).astype(BF)
        fine = []
        for n in range(NY // 128):
            tile = within[:, 128 * n : 128 * n + 128]
            fine.append(jnp.where(steps == jnp.concatenate([tile] * 8, axis=0), one, none))
        spread = jnp.where(coarse, value, 0.0)
        first = spread.astype(BF).astype(F32)
        second = (spread - first).astype(BF).astype(F32)
        third = spread - first - second
        pieces = jnp.concatenate([third, second, first, jnp.zeros_like(first)], axis=0).astype(BF)
        sums += lax.dot_general(pieces, jnp.concatenate(fine, axis=1), ACROSS, preferred_element_type=F32)
    sums = sums[0:8] + sums[8:16] + sums[16:24]
    sums = sums * (NB / (KZ * NY))
    for copy in range(sums_ref.shape[0]):
        sums_ref[copy] = sums


def on_device(field_b, density, level_y, level_z, bins):
    y_local, z_local = field_b.shape[2], field_b.shape[3]

    def shift(cells, axis, step):
        count = lax.axis_size(axis)
        return lax.ppermute(cells, axis, [(i, (i + step) % count) for i in range(count)])

    small = pltpu.CompilerParams(vmem_limit_bytes=16 * 2**20)
    far = [
        pltpu.with_memory_space_constraint(x, pltpu.HBM)
        for x in (level_y[None, :], level_z[None, :], field_b, density)
    ]
    upper, lower = pl.pallas_call(
        border_kernel,
        out_shape=(jax.ShapeDtypeStruct((16, z_local), F32), jax.ShapeDtypeStruct((4, z_local), F32)),
        in_specs=[pl.BlockSpec(memory_space=pltpu.HBM)] * 3,
        scratch_shapes=[
            pltpu.VMEM((1, y_local), jnp.int32),
            pltpu.VMEM((3, 2, 8, z_local), F32),
            pltpu.VMEM((3, 2, 8, z_local), F32),
            pltpu.VMEM((2, 8, z_local), F32),
            pltpu.SemaphoreType.DMA((4,)),
        ],
        compiler_params=small,
    )(far[0], far[2], far[3])
    after = shift(upper, GY, -1)
    before = shift(lower, GY, 1)
    scratch = [
        pltpu.VMEM((1, y_local), jnp.int32),
        pltpu.VMEM((1, z_local), jnp.int32),
        pltpu.VMEM(field_b.shape, F32),
        pltpu.VMEM(density.shape, F32),
        pltpu.SemaphoreType.DMA((5,)),
    ]
    made = (
        jax.ShapeDtypeStruct((16, 64, z_local), BF),
        jax.ShapeDtypeStruct((y_local, z_local), F32),
        jax.ShapeDtypeStruct(field_b.shape, BF),
    )
    rows = [jax.ShapeDtypeStruct(shape, F32) for shape in ((6, 8, z_local), (16, z_local), (16, z_local))]
    table = pltpu.with_memory_space_constraint(jnp.asarray(z_table()), pltpu.HBM)
    message, held, inside, tips, low, last, half = pl.pallas_call(
        message_kernel,
        out_shape=made + tuple(rows) + (jax.ShapeDtypeStruct(table.shape[1:], BF),),
        in_specs=[pl.BlockSpec(memory_space=pltpu.HBM)] * 5,
        scratch_shapes=scratch,
        compiler_params=small,
        cost_estimate=pl.CostEstimate(flops=2_000_000, bytes_accessed=2_000_000, transcendentals=0),
    )(*far, table)
    message, held, inside = pl.pallas_call(rim_kernel, out_shape=made, compiler_params=small)(
        after, message, held, inside, tips, last
    )
    lines = lax.all_to_all(message, GZ, 0, 0, tiled=True)
    z_modes, emf = pl.pallas_call(
        z_kernel,
        out_shape=(jax.ShapeDtypeStruct((512, 128), BF), jax.ShapeDtypeStruct(field_b.shape, BF)),
        scratch_shapes=[pltpu.VMEM((512, 128), F32)],
        compiler_params=small,
    )(lines, half, held, inside, low, before)
    spread = lax.all_to_all(z_modes.reshape(256, 2, 128), ("yh", "yl") + GY, 0, 0, tiled=True).reshape(512, 128)
    first = ('xh', 'xl', 'c')
    second = ('yh', 'yl', 'z')
    mode_power, sums = pl.pallas_call(
        y_kernel,
        out_shape=(
            jax.ShapeDtypeStruct((2, NY), F32),
            jax.ShapeDtypeStruct((lax.axis_size(first), 8, 128), F32),
        ),
        compiler_params=small,
    )(spread, *y_tables(), bins)
    sums = jnp.sum(lax.all_to_all(sums, first, 0, 0, tiled=True), axis=0)
    copies = jnp.broadcast_to(sums.astype(BF)[None], (lax.axis_size(second), 8, 128))
    spectrum = jnp.sum(lax.all_to_all(copies, second, 0, 0, tiled=True).astype(F32), axis=0).reshape(NB)
    return (emf, mode_power, spectrum)


def solution(mesh):
    fine = Mesh(mesh.devices.reshape(4, 2, 2, 8, 2, 2), GZ + GY)
    placed = (
        P(None, None, GY, GZ),
        P(None, GY, GZ),
        P(GY),
        P(GZ),
        P(GZ + GY, None),
    )
    return jax.shard_map(
        on_device,
        mesh=fine,
        in_specs=placed,
        out_specs=(P(None, None, GY, GZ), P(GZ + GY, None), P()),
        check_vma=False,
    )
```

```python
import math

import jax
import jax.numpy as jnp
import numpy as np
from jax import lax
from jax.experimental import pallas as pl
from jax.experimental.pallas import tpu as pltpu
from jax.sharding import Mesh, PartitionSpec as P

NY = 2048
NZ = 2048
NB = 1024
KZ = 1024
BF = jnp.bfloat16
F32 = jnp.float32
GZ = ("yh", "yl", "xh")
GY = ('z', 'xl', 'c')
ACROSS = (((1,), (1,)), ((), ()))


def angle(a, b, length):
    return 2.0 * math.pi * ((a[:, None] * b[None, :]) % length) / length


def z_table():
    part, kappa, y, jh = np.meshgrid(*(np.arange(n) for n in (2, 16, 8, 4)), indexing="ij")
    modes = (16 * (8 * y + 4 * part + jh) + kappa).reshape(2, 1, 512, 1)
    turn = (modes * np.arange(128) % NZ + 128 * np.arange(8).reshape(1, 8, 1, 1)) % NZ
    return (np.cos(2.0 * math.pi * turn / NZ) / math.sqrt(NZ)).astype(jnp.bfloat16)


def y_tables():
    inner = angle((8 * np.arange(32)[None, :] + np.arange(8)[:, None]).reshape(-1), np.arange(256), 256)
    cos, sin = np.cos(inner), np.sin(inner)
    table = np.stack([np.stack([cos, -sin], axis=1), np.stack([sin, cos], axis=1)], axis=1)
    turn = angle(np.arange(8), np.arange(256), NY)
    order = np.zeros((128, 128), np.float32)
    for e in range(2):
        for cp in range(6):
            for y0 in range(8):
                order[16 * y0 + 8 * e + cp, 64 * e + 8 * cp + y0] = 1.0
    return (
        table.reshape(512, 512).astype(jnp.bfloat16),
        np.stack([np.cos(turn), np.sin(turn)]).astype(np.float32),
        order.astype(jnp.bfloat16),
    )


def metric(level):
    return 1.0 / (1.0 + 0.25 * level.astype(F32))


def roll(x, by, axis):
    return pltpu.roll(x, by % x.shape[axis], axis)


def hall(p, fb, den, my, mz):
    rows, lanes = fb.shape[2], fb.shape[3]
    row = lax.broadcasted_iota(jnp.int32, (rows, lanes), 0)
    lane = lax.broadcasted_iota(jnp.int32, (rows, lanes), 1)

    def d_y(f):
        return (jnp.where(row == rows - 1, 0.0, roll(f, -1, 0)) - jnp.where(row == 0, 0.0, roll(f, 1, 0))) * my

    def d_z(f):
        return (jnp.where(lane == lanes - 1, 0.0, roll(f, -1, 1)) - jnp.where(lane == 0, 0.0, roll(f, 1, 1))) * mz

    b_x, b_y, b_z = fb[0, p], fb[1, p], fb[2, p]
    half = 0.5 if p == 0 else -0.5
    cur_x = d_y(b_z) - d_z(b_y)
    cur_y = d_z(b_x) - half * fb[2, 1 - p]
    cur_z = half * fb[1, 1 - p] - d_y(b_x)
    dens = den[p]
    return (
        (cur_y * b_z - cur_z * b_y) / dens,
        (cur_z * b_x - cur_x * b_z) / dens,
        (cur_x * b_y - cur_y * b_x) / dens,
    )


def fetched(far, near, sems):
    copies = [pltpu.make_async_copy(a, b, sems.at[n]) for n, (a, b) in enumerate(zip(far, near))]
    for copy in copies:
        copy.start()
    for copy in copies:
        copy.wait()


def metrics(ly_ref, lz_ref, shape):
    half_y = jnp.broadcast_to(0.5 * metric(ly_ref[...]), (8, shape[0]))
    return jnp.broadcast_to(jnp.transpose(half_y)[:, 0:1], shape), 0.5 * metric(lz_ref[...])


def border_kernel(ly_far, fb_far, den_far, upper_ref, lower_ref, levels, top, bottom, dens, sems):
    last = fb_far.shape[2] - 8
    far = (ly_far, fb_far.at[:, :, 0:8, :], fb_far.at[:, :, last : last + 8, :], den_far.at[:, 0:8, :])
    fetched(far, (levels, top, bottom, dens), sems)
    for p in range(2):
        for comp in range(3):
            upper_ref[2 * comp + p : 2 * comp + p + 1, :] = top[comp, p, 0:1, :]
        for n, comp in enumerate((0, 2)):
            upper_ref[6 + 2 * n + p : 7 + 2 * n + p, :] = top[comp, p, 1:2, :]
            lower_ref[2 * n + p : 2 * n + p + 1, :] = bottom[comp, p, 7:8, :]
        upper_ref[10 + p : 11 + p, :] = dens[p, 0:1, :]
    scale = 0.5 * metric(levels[...])[:, 0:1]
    upper_ref[12:16, :] = jnp.broadcast_to(scale, (4, upper_ref.shape[1]))


def message_kernel(*refs):
    far, table_ref, outs, near, sems = refs[0:4], refs[4], refs[5:12], refs[12:16], refs[16]
    msg_ref, held_ref, emf_ref, tips_ref, low_ref, last_ref, half_ref = outs
    table_copy = pltpu.make_async_copy(table_ref.at[lax.axis_index("xh")], half_ref, sems.at[4])
    table_copy.start()
    fetched(far, near, sems)
    ly_ref, lz_ref, fb, den = near
    shape = fb.shape[2:]
    my, mz = metrics(ly_ref, lz_ref, shape)
    lane = lax.broadcasted_iota(jnp.int32, shape, 1)
    edge = (lane == 0) | (lane == 127)
    slot = lane >> 1
    signed = jnp.where(lane == 0, -mz, mz)
    inside, held = [], []
    own = jnp.zeros(shape, F32)
    for p in range(2):
        parts = hall(p, fb, den, my, mz)
        inverse = 1.0 / den[p]
        weight = signed * inverse
        downward, upward = -my[0:1] * inverse[0:1], my[63:64] * inverse[63:64]
        for comp in range(3):
            tips_ref[2 * comp + p] = parts[comp][56:64]
            low_ref[2 * comp + p : 2 * comp + p + 1, :] = parts[comp][0:1]
            low_ref[6 + 3 * p + comp : 7 + 3 * p + comp, :] = downward * fb[comp, p, 0:1, :]
            last_ref[3 * p + comp : 3 * p + comp + 1, :] = upward * fb[comp, p, 63:64, :]
            last_ref[6 + 2 * comp + p : 7 + 2 * comp + p, :] = fb[comp, p, 63:64, :]
        fields = [fb[comp, p] for comp in range(3)]
        inside.append([jnp.where(edge, 0.0, part) for part in parts])
        terms = list(parts) + [f * weight for f in fields] + fields[0:2]
        packed = jnp.zeros(shape, F32)
        for q, term in enumerate(terms):
            packed = jnp.where(slot == q, roll(term, 2 * q + 1, 1), packed)
        held.append(packed)
        for comp in range(2):
            k = 2 * p + comp
            own = jnp.where(slot == k, roll(fields[comp], 2 * k + 1, 1), own)
        for comp in range(3):
            emf_ref[comp, p] = inside[p][comp].astype(BF)
    last_ref[12:13, :] = mz
    last_ref[13:16, :] = jnp.zeros((3, shape[1]), F32)
    low_ref[12:16, :] = jnp.zeros((4, shape[1]), F32)
    held_ref[...] = held[0] + roll(held[1], 16, 1)
    first = own.astype(BF).astype(F32)
    own = own - first
    second = own.astype(BF).astype(F32)
    own = first + roll(second, 8, 1) + roll(own - second, 16, 1)
    folded = roll(own[0:16], 32, 1)
    for block in range(1, 4):
        folded = folded + roll(own[16 * block : 16 * block + 16], 32 + 24 * block, 1)
    held = [roll(x, -1, 0) for x in held]
    inside = [[roll(x, -1, 0) for x in plane] for plane in inside]
    for block in range(8):
        rows = slice(8 * block, 8 * block + 8)
        tile = jnp.concatenate([held[0][rows], held[1][rows]], axis=0)
        high = tile.astype(BF).astype(F32)
        low = (tile - high).astype(BF).astype(F32)
        values = [jnp.concatenate([inside[0][comp][rows], inside[1][comp][rows]], axis=0) for comp in range(3)]
        values.append(high + roll(low, 16, 1) + folded)
        for n, value in enumerate(values):
            for copy in range(2):
                msg_ref[8 * copy + block, 16 * n : 16 * n + 16, :] = value.astype(BF)
    table_copy.wait()


def changes(f_x, f_z, weights_ref, at):
    w_x, w_y, w_z = (weights_ref[at + comp : at + comp + 1, :] for comp in range(3))
    return (f_x * w_y, -(f_x * w_x + f_z * w_z), f_z * w_y)


def rim_kernel(next_ref, msg_ref, held_ref, emf_ref, tips_ref, last_ref, msg_out, held_out, emf_out):
    msg_out[...] = msg_ref[...]
    held_out[...] = held_ref[...]
    emf_out[...] = emf_ref[...]
    shape = (8, emf_ref.shape[3])
    row = lax.broadcasted_iota(jnp.int32, shape, 0)
    lane = lax.broadcasted_iota(jnp.int32, shape, 1)
    inner = (lane > 0) & (lane < 127)
    slot = lane >> 1
    mz = last_ref[12:13, :]
    line = lax.broadcasted_iota(jnp.int32, (1, shape[1]), 1)
    signed = jnp.where(line == 0, -mz, mz)
    beyond = next_ref[...]
    wide = lax.broadcasted_iota(jnp.int32, beyond.shape, 1)
    slope = (jnp.where(wide == 127, 0.0, roll(beyond, -1, 1)) - jnp.where(wide == 0, 0.0, roll(beyond, 1, 1))) * mz
    my = beyond[12:13]
    rows = slice(56, 64)
    held = held_ref[rows, :]
    values, tiles = [], []
    for p in range(2):
        f = [beyond[2 * comp + p : 2 * comp + p + 1] for comp in range(3)]
        g = [beyond[2 * comp + 1 - p : 2 * comp + 2 - p] for comp in range(3)]
        d_z = [slope[2 * comp + p : 2 * comp + p + 1] for comp in range(2)]
        dy_x = (beyond[6 + p : 7 + p] - last_ref[6 + p : 7 + p, :]) * my
        dy_z = (beyond[8 + p : 9 + p] - last_ref[10 + p : 11 + p, :]) * my
        half = 0.5 if p == 0 else -0.5
        cur_x, cur_y, cur_z = dy_z - d_z[1], d_z[0] - half * g[2], half * g[1] - dy_x
        dens = beyond[10 + p : 11 + p]
        made = [
            (cur_y * f[2] - cur_z * f[1]) / dens,
            (cur_z * f[0] - cur_x * f[2]) / dens,
            (cur_x * f[1] - cur_y * f[0]) / dens,
        ]
        weight = signed / dens
        terms = made + [x * weight for x in f] + f[0:2]
        packed = jnp.zeros(shape, F32)
        for q, term in enumerate(terms):
            packed = jnp.where(slot == q, roll(jnp.broadcast_to(term, shape), 2 * q + 1, 1), packed)
        extra = changes(f[0], f[2], last_ref, 3 * p)
        for comp in range(3):
            change = jnp.where(row == 7, extra[comp], 0.0)
            value = jnp.where(inner, tips_ref[2 * comp + p] + change, 0.0)
            emf_out[comp, p, rows, :] = value.astype(BF)
            values.append(jnp.where(row == 7, jnp.where(inner, made[comp], 0.0), roll(value, -1, 0)))
            held = held + jnp.where(slot == 8 * p + comp, roll(change, 16 * p + 2 * comp + 1, 1), 0.0)
        tiles.append(packed)
    held_out[rows, :] = held
    for p in range(2):
        moved = roll(held if p == 0 else roll(held, -16, 1), -1, 0)
        tiles[p] = jnp.where(lane < 16, jnp.where(row == 7, tiles[p], moved), 0.0)
    tile = jnp.concatenate(tiles, axis=0)
    high = tile.astype(BF).astype(F32)
    low = (tile - high).astype(BF).astype(F32)
    old = msg_ref[7, 48:64, :].astype(F32)
    tiles = [jnp.concatenate([values[comp], values[3 + comp]], axis=0) for comp in range(3)]
    tiles.append(jnp.where(wide < 32, high + roll(low, 16, 1), old))
    for n, value in enumerate(tiles):
        for copy in range(2):
            msg_out[8 * copy + 7, 16 * n : 16 * n + 16, :] = value.astype(BF)


def finished(held, beside):
    slot = (lax.broadcasted_iota(jnp.int32, held.shape, 1) >> 1) & 7
    flat = roll(beside, -12, 1) * jnp.where(slot == 0, roll(held, -10, 1), roll(held, -8, 1))
    upright = roll(beside, -10, 1) * roll(held, -4, 1) + roll(beside, -8, 1) * roll(held, -2, 1)
    return held + jnp.where(slot == 2, -upright, flat)


def at_edges(values, spot):
    lane = lax.broadcasted_iota(jnp.int32, values.shape, 1)
    return jnp.where((lane == 0) | (lane == 127), roll(values, -spot, 1), 0.0).astype(BF)


def spot(block):
    return (block & 1) * 8 + (block >> 1)


def line_edges(x_ref):
    held = jnp.concatenate([x_ref[spot(i), 48:64, :] for i in range(16)], axis=0).astype(F32)
    held = held + roll(held, -16, 1)
    lane = lax.broadcasted_iota(jnp.int32, held.shape, 1)
    beside = jnp.where((lane & 1) == 0, roll(roll(held, -16, 0), -1, 1), roll(roll(held, 16, 0), 1, 1))
    values = finished(held, beside)
    return [at_edges(values, 2 * comp + 1) for comp in range(3)]


def finish_emf(x_ref, held_ref, inside_ref, low_ref, before_ref, emf_ref):
    me = lax.axis_index("yh") * 4 + lax.axis_index("yl") * 2 + lax.axis_index("xh")

    def fields(block):
        folded = x_ref[spot(block), 48:64, :].astype(F32)
        rows = []
        for n in range(4):
            own = roll(folded, -(32 + 24 * n), 1)
            rows.append(own + (roll(own, -8, 1) + roll(own, -16, 1)))
        return jnp.concatenate(rows, axis=0)

    low, high = fields(lax.rem(me + 15, 16)), fields(lax.rem(me + 1, 16))
    lane = lax.broadcasted_iota(jnp.int32, low.shape, 1)
    beside = jnp.where((lane & 1) == 0, roll(high, -1, 1), roll(low, 1, 1))
    beside = jnp.where(lane < 16, roll(beside, 12, 1), roll(beside, 24, 1))
    shape = (8, low.shape[1])
    row = lax.broadcasted_iota(jnp.int32, shape, 0)
    lane = lax.broadcasted_iota(jnp.int32, shape, 1)
    inner = (lane > 0) & (lane < 127)
    tips = {}
    held = held_ref[0:8, :]
    for p in range(2):
        extra = changes(before_ref[p : p + 1, :], before_ref[2 + p : 3 + p, :], low_ref, 6 + 3 * p)
        for comp in range(3):
            change = jnp.where(row == 0, extra[comp], 0.0)
            value = low_ref[2 * comp + p : 2 * comp + p + 1, :] + extra[comp]
            plain = inside_ref[comp, p, 0:8, :].astype(F32)
            tips[comp, p] = jnp.where(row == 0, jnp.where(inner, value, 0.0), plain)
            moved = roll(change, 16 * p + 2 * comp + 1, 1)
            held = held + jnp.where((lane >> 1) == 8 * p + comp, moved, 0.0)
    values = finished(jnp.concatenate([held, held_ref[8:64, :]], axis=0), beside)
    for comp in range(3):
        for p in range(2):
            edges = at_edges(values, 16 * p + 2 * comp + 1)
            emf_ref[comp, p] = inside_ref[comp, p] + edges
            emf_ref[comp, p, 0:8, :] = (tips[comp, p] + edges[0:8].astype(F32)).astype(BF)


def z_kernel(x_ref, table_ref, held_ref, inside_ref, low_ref, before_ref, out_ref, emf_ref, mix_ref):
    edges = line_edges(x_ref)
    zero = jnp.zeros((16, 512), BF)
    total = None
    for n in range(2):
        sums, gaps = [], []
        for i in range(4 * n, 4 * n + 4):
            for side, pair in ((sums, 1), (gaps, -1)):
                tiles = []
                for c in range(3):
                    near, far = (
                        x_ref[spot(m), 16 * c : 16 * c + 16, :] + edges[c][16 * m : 16 * m + 16] for m in (i, i + 8)
                    )
                    tiles.append(near + far if pair > 0 else near - far)
                side.append(jnp.concatenate(tiles, axis=0))
        sums, gaps = (jnp.concatenate([jnp.concatenate(x, axis=1), zero], axis=0) for x in (sums, gaps))
        empty = jnp.zeros((64, 512), BF)
        lines = jnp.concatenate(
            [jnp.concatenate([sums, empty], axis=0), jnp.concatenate([empty, gaps], axis=0)], axis=1
        )
        blocks = []
        for c in range(2):
            for jl in range(8):
                row = []
                for kappa in (2 * jl, 2 * jl + 1):
                    for i in range(4 * n, 4 * n + 4):
                        m = (kappa * i + 4 * c) % 16
                        cell = table_ref[m % 8, 32 * kappa : 32 * kappa + 32, :]
                        row.append(-cell if m >= 8 else cell)
                blocks.append(jnp.concatenate(row, axis=1))
        product = lax.dot_general(jnp.concatenate(blocks, axis=0), lines, ACROSS, preferred_element_type=F32)
        total = product if n == 0 else total + product
    for c in range(2):
        for jl in range(8):
            at = 32 * (8 * c + jl)
            mix_ref[pl.ds(2 * jl + c, 32, stride=16), :] = total[at : at + 32]
    out_ref[...] = mix_ref[...].astype(BF)
    finish_emf(x_ref, held_ref, inside_ref, low_ref, before_ref, emf_ref)


def add(a, b):
    return (a[0] + b[0], a[1] + b[1])


def sub(a, b):
    return (a[0] - b[0], a[1] - b[1])


def turned(a, eighths):
    eighths %= 16
    if eighths == 0:
        return a
    if eighths == 4:
        return (a[1], -a[0])
    if eighths == 2:
        r = math.sqrt(0.5)
        return ((a[0] + a[1]) * r, (a[1] - a[0]) * r)
    if eighths == 6:
        r = math.sqrt(0.5)
        return ((a[1] - a[0]) * r, -(a[0] + a[1]) * r)
    cos, sin = math.cos(math.pi * eighths / 8), math.sin(math.pi * eighths / 8)
    return (a[0] * cos + a[1] * sin, a[1] * cos - a[0] * sin)


def fourier4(x):
    s, d = add(x[0], x[2]), sub(x[0], x[2])
    t, u = add(x[1], x[3]), turned(sub(x[1], x[3]), 4)
    return [add(s, t), add(d, u), sub(s, t), sub(d, u)]


def fourier8(x):
    even = fourier4([x[0], x[2], x[4], x[6]])
    odd = fourier4([x[1], x[3], x[5], x[7]])
    odd = [turned(value, 2 * k) for k, value in enumerate(odd)]
    return [add(a, b) for a, b in zip(even, odd)] + [sub(a, b) for a, b in zip(even, odd)]


def y_kernel(x_ref, table_ref, turn_ref, order_ref, bins_ref, power_ref, sums_ref):
    lhs = lax.dot_general(order_ref[...], x_ref[...], ACROSS, preferred_element_type=F32).astype(BF)
    product = jnp.dot(lhs, table_ref[...], preferred_element_type=F32)
    scale = 1.0 / (6.0 * NY)
    for e in range(2):
        held = []
        for y0 in range(8):
            at = 16 * y0 + 8 * e
            a, b = product[at : at + 8, 0:256], product[at : at + 8, 256:512]
            if y0 > 0:
                cos, sin = turn_ref[0, y0 : y0 + 1, :], turn_ref[1, y0 : y0 + 1, :]
                a, b = a * cos + b * sin, b * cos - a * sin
            held.append((a, b))
        for q1, (a, b) in enumerate(fourier8(held)):
            power_ref[e : e + 1, 256 * q1 : 256 * q1 + 256] = (
                jnp.sum(a * a + b * b, axis=0, keepdims=True) * scale
            )
    sums = jnp.zeros((32, 128), F32)
    steps = lax.broadcasted_iota(jnp.int32, (128, 128), 0).astype(F32).astype(BF)
    one, none = jnp.ones((128, 128), BF), jnp.zeros((128, 128), BF)
    for e in range(2):
        value = power_ref[e : e + 1, :]
        bins = bins_ref[e : e + 1, :]
        coarse = lax.broadcasted_iota(jnp.int32, (8, NY), 0) == (bins >> 7)
        within = jnp.broadcast_to((bins & 127).astype(F32), (16, NY)).astype(BF)
        fine = []
        for n in range(NY // 128):
            tile = within[:, 128 * n : 128 * n + 128]
            fine.append(jnp.where(steps == jnp.concatenate([tile] * 8, axis=0), one, none))
        spread = jnp.where(coarse, value, 0.0)
        first = spread.astype(BF).astype(F32)
        second = (spread - first).astype(BF).astype(F32)
        third = spread - first - second
        pieces = jnp.concatenate([third, second, first, jnp.zeros_like(first)], axis=0).astype(BF)
        sums += lax.dot_general(pieces, jnp.concatenate(fine, axis=1), ACROSS, preferred_element_type=F32)
    sums = sums[0:8] + sums[8:16] + sums[16:24]
    sums = sums * (NB / (KZ * NY))
    for copy in range(sums_ref.shape[0]):
        sums_ref[copy] = sums


def on_device(field_b, density, level_y, level_z, bins):
    y_local, z_local = field_b.shape[2], field_b.shape[3]

    def shift(cells, axis, step):
        count = lax.axis_size(axis)
        return lax.ppermute(cells, axis, [(i, (i + step) % count) for i in range(count)])

    small = pltpu.CompilerParams(vmem_limit_bytes=16 * 2**20)
    far = [
        pltpu.with_memory_space_constraint(x, pltpu.HBM)
        for x in (level_y[None, :], level_z[None, :], field_b, density)
    ]
    upper, lower = pl.pallas_call(
        border_kernel,
        out_shape=(jax.ShapeDtypeStruct((16, z_local), F32), jax.ShapeDtypeStruct((4, z_local), F32)),
        in_specs=[pl.BlockSpec(memory_space=pltpu.HBM)] * 3,
        scratch_shapes=[
            pltpu.VMEM((1, y_local), jnp.int32),
            pltpu.VMEM((3, 2, 8, z_local), F32),
            pltpu.VMEM((3, 2, 8, z_local), F32),
            pltpu.VMEM((2, 8, z_local), F32),
            pltpu.SemaphoreType.DMA((4,)),
        ],
        compiler_params=small,
    )(far[0], far[2], far[3])
    after = shift(upper, GY, -1)
    before = shift(lower, GY, 1)
    scratch = [
        pltpu.VMEM((1, y_local), jnp.int32),
        pltpu.VMEM((1, z_local), jnp.int32),
        pltpu.VMEM(field_b.shape, F32),
        pltpu.VMEM(density.shape, F32),
        pltpu.SemaphoreType.DMA((5,)),
    ]
    made = (
        jax.ShapeDtypeStruct((16, 64, z_local), BF),
        jax.ShapeDtypeStruct((y_local, z_local), F32),
        jax.ShapeDtypeStruct(field_b.shape, BF),
    )
    rows = [jax.ShapeDtypeStruct(shape, F32) for shape in ((6, 8, z_local), (16, z_local), (16, z_local))]
    table = pltpu.with_memory_space_constraint(jnp.asarray(z_table()), pltpu.HBM)
    message, held, inside, tips, low, last, half = pl.pallas_call(
        message_kernel,
        out_shape=made + tuple(rows) + (jax.ShapeDtypeStruct(table.shape[1:], BF),),
        in_specs=[pl.BlockSpec(memory_space=pltpu.HBM)] * 5,
        scratch_shapes=scratch,
        compiler_params=small,
        cost_estimate=pl.CostEstimate(flops=2_000_000, bytes_accessed=2_000_000, transcendentals=0),
    )(*far, table)
    message, held, inside = pl.pallas_call(rim_kernel, out_shape=made, compiler_params=small)(
        after, message, held, inside, tips, last
    )
    lines = lax.all_to_all(message, ("xh", "yh", "yl"), 0, 0, tiled=True)
    z_modes, emf = pl.pallas_call(
        z_kernel,
        out_shape=(jax.ShapeDtypeStruct((512, 128), BF), jax.ShapeDtypeStruct(field_b.shape, BF)),
        scratch_shapes=[pltpu.VMEM((512, 128), F32)],
        compiler_params=small,
    )(lines, half, held, inside, low, before)
    spread = lax.all_to_all(z_modes.reshape(256, 2, 128), ("yh", "yl") + GY, 0, 0, tiled=True).reshape(512, 128)
    first = ('c', 'xl', 'xh')
    second = ('yh', 'yl', 'z')
    mode_power, sums = pl.pallas_call(
        y_kernel,
        out_shape=(
            jax.ShapeDtypeStruct((2, NY), F32),
            jax.ShapeDtypeStruct((lax.axis_size(first), 8, 128), F32),
        ),
        compiler_params=small,
    )(spread, *y_tables(), bins)
    sums = jnp.sum(lax.all_to_all(sums, first, 0, 0, tiled=True), axis=0)
    copies = jnp.broadcast_to(sums.astype(BF)[None], (lax.axis_size(second), 8, 128))
    spectrum = jnp.sum(lax.all_to_all(copies, second, 0, 0, tiled=True).astype(F32), axis=0).reshape(NB)
    return (emf, mode_power, spectrum)


def solution(mesh):
    fine = Mesh(mesh.devices.reshape(4, 2, 2, 8, 2, 2), GZ + GY)
    placed = (
        P(None, None, GY, GZ),
        P(None, GY, GZ),
        P(GY),
        P(GZ),
        P(GZ + GY, None),
    )
    return jax.shard_map(
        on_device,
        mesh=fine,
        in_specs=placed,
        out_specs=(P(None, None, GY, GZ), P(GZ + GY, None), P()),
        check_vma=False,
    )
```

```python
import math

import jax
import jax.numpy as jnp
import numpy as np
from jax import lax
from jax.experimental import pallas as pl
from jax.experimental.pallas import tpu as pltpu
from jax.sharding import Mesh, PartitionSpec as P

NY = 2048
NZ = 2048
NB = 1024
KZ = 1024
BF = jnp.bfloat16
F32 = jnp.float32
GZ = ("yh", "yl", "xh")
GY = ('z', 'xl', 'c')
ACROSS = (((1,), (1,)), ((), ()))


def angle(a, b, length):
    return 2.0 * math.pi * ((a[:, None] * b[None, :]) % length) / length


def z_table():
    part, kappa, y, jh = np.meshgrid(*(np.arange(n) for n in (2, 16, 8, 4)), indexing="ij")
    modes = (16 * (8 * y + 4 * part + jh) + kappa).reshape(2, 1, 512, 1)
    turn = (modes * np.arange(128) % NZ + 128 * np.arange(8).reshape(1, 8, 1, 1)) % NZ
    return (np.cos(2.0 * math.pi * turn / NZ) / math.sqrt(NZ)).astype(jnp.bfloat16)


def y_tables():
    inner = angle((8 * np.arange(32)[None, :] + np.arange(8)[:, None]).reshape(-1), np.arange(256), 256)
    cos, sin = np.cos(inner), np.sin(inner)
    table = np.stack([np.stack([cos, -sin], axis=1), np.stack([sin, cos], axis=1)], axis=1)
    turn = angle(np.arange(8), np.arange(256), NY)
    order = np.zeros((128, 128), np.float32)
    for e in range(2):
        for cp in range(6):
            for y0 in range(8):
                order[16 * y0 + 8 * e + cp, 64 * e + 8 * cp + y0] = 1.0
    return (
        table.reshape(512, 512).astype(jnp.bfloat16),
        np.stack([np.cos(turn), np.sin(turn)]).astype(np.float32),
        order.astype(jnp.bfloat16),
    )


def metric(level):
    return 1.0 / (1.0 + 0.25 * level.astype(F32))


def roll(x, by, axis):
    return pltpu.roll(x, by % x.shape[axis], axis)


def hall(p, fb, den, my, mz):
    rows, lanes = fb.shape[2], fb.shape[3]
    row = lax.broadcasted_iota(jnp.int32, (rows, lanes), 0)
    lane = lax.broadcasted_iota(jnp.int32, (rows, lanes), 1)

    def d_y(f):
        return (jnp.where(row == rows - 1, 0.0, roll(f, -1, 0)) - jnp.where(row == 0, 0.0, roll(f, 1, 0))) * my

    def d_z(f):
        return (jnp.where(lane == lanes - 1, 0.0, roll(f, -1, 1)) - jnp.where(lane == 0, 0.0, roll(f, 1, 1))) * mz

    b_x, b_y, b_z = fb[0, p], fb[1, p], fb[2, p]
    half = 0.5 if p == 0 else -0.5
    cur_x = d_y(b_z) - d_z(b_y)
    cur_y = d_z(b_x) - half * fb[2, 1 - p]
    cur_z = half * fb[1, 1 - p] - d_y(b_x)
    dens = den[p]
    return (
        (cur_y * b_z - cur_z * b_y) / dens,
        (cur_z * b_x - cur_x * b_z) / dens,
        (cur_x * b_y - cur_y * b_x) / dens,
    )


def fetched(far, near, sems):
    copies = [pltpu.make_async_copy(a, b, sems.at[n]) for n, (a, b) in enumerate(zip(far, near))]
    for copy in copies:
        copy.start()
    for copy in copies:
        copy.wait()


def metrics(ly_ref, lz_ref, shape):
    half_y = jnp.broadcast_to(0.5 * metric(ly_ref[...]), (8, shape[0]))
    return jnp.broadcast_to(jnp.transpose(half_y)[:, 0:1], shape), 0.5 * metric(lz_ref[...])


def border_kernel(ly_far, fb_far, den_far, upper_ref, lower_ref, levels, top, bottom, dens, sems):
    last = fb_far.shape[2] - 8
    far = (ly_far, fb_far.at[:, :, 0:8, :], fb_far.at[:, :, last : last + 8, :], den_far.at[:, 0:8, :])
    fetched(far, (levels, top, bottom, dens), sems)
    for p in range(2):
        for comp in range(3):
            upper_ref[2 * comp + p : 2 * comp + p + 1, :] = top[comp, p, 0:1, :]
        for n, comp in enumerate((0, 2)):
            upper_ref[6 + 2 * n + p : 7 + 2 * n + p, :] = top[comp, p, 1:2, :]
            lower_ref[2 * n + p : 2 * n + p + 1, :] = bottom[comp, p, 7:8, :]
        upper_ref[10 + p : 11 + p, :] = dens[p, 0:1, :]
    scale = 0.5 * metric(levels[...])[:, 0:1]
    upper_ref[12:16, :] = jnp.broadcast_to(scale, (4, upper_ref.shape[1]))


def message_kernel(*refs):
    far, table_ref, outs, near, sems = refs[0:4], refs[4], refs[5:12], refs[12:16], refs[16]
    msg_ref, held_ref, emf_ref, tips_ref, low_ref, last_ref, half_ref = outs
    table_copy = pltpu.make_async_copy(table_ref.at[lax.axis_index("xh")], half_ref, sems.at[4])
    table_copy.start()
    fetched(far, near, sems)
    ly_ref, lz_ref, fb, den = near
    shape = fb.shape[2:]
    my, mz = metrics(ly_ref, lz_ref, shape)
    lane = lax.broadcasted_iota(jnp.int32, shape, 1)
    edge = (lane == 0) | (lane == 127)
    slot = lane >> 1
    signed = jnp.where(lane == 0, -mz, mz)
    inside, held = [], []
    own = jnp.zeros(shape, F32)
    for p in range(2):
        parts = hall(p, fb, den, my, mz)
        inverse = 1.0 / den[p]
        weight = signed * inverse
        downward, upward = -my[0:1] * inverse[0:1], my[63:64] * inverse[63:64]
        for comp in range(3):
            tips_ref[2 * comp + p] = parts[comp][56:64]
            low_ref[2 * comp + p : 2 * comp + p + 1, :] = parts[comp][0:1]
            low_ref[6 + 3 * p + comp : 7 + 3 * p + comp, :] = downward * fb[comp, p, 0:1, :]
            last_ref[3 * p + comp : 3 * p + comp + 1, :] = upward * fb[comp, p, 63:64, :]
            last_ref[6 + 2 * comp + p : 7 + 2 * comp + p, :] = fb[comp, p, 63:64, :]
        fields = [fb[comp, p] for comp in range(3)]
        inside.append([jnp.where(edge, 0.0, part) for part in parts])
        terms = list(parts) + [f * weight for f in fields] + fields[0:2]
        packed = jnp.zeros(shape, F32)
        for q, term in enumerate(terms):
            packed = jnp.where(slot == q, roll(term, 2 * q + 1, 1), packed)
        held.append(packed)
        for comp in range(2):
            k = 2 * p + comp
            own = jnp.where(slot == k, roll(fields[comp], 2 * k + 1, 1), own)
        for comp in range(3):
            emf_ref[comp, p] = inside[p][comp].astype(BF)
    last_ref[12:13, :] = mz
    last_ref[13:16, :] = jnp.zeros((3, shape[1]), F32)
    low_ref[12:16, :] = jnp.zeros((4, shape[1]), F32)
    held_ref[...] = held[0] + roll(held[1], 16, 1)
    first = own.astype(BF).astype(F32)
    own = own - first
    second = own.astype(BF).astype(F32)
    own = first + roll(second, 8, 1) + roll(own - second, 16, 1)
    folded = roll(own[0:16], 32, 1)
    for block in range(1, 4):
        folded = folded + roll(own[16 * block : 16 * block + 16], 32 + 24 * block, 1)
    held = [roll(x, -1, 0) for x in held]
    inside = [[roll(x, -1, 0) for x in plane] for plane in inside]
    for block in range(8):
        rows = slice(8 * block, 8 * block + 8)
        tile = jnp.concatenate([held[0][rows], held[1][rows]], axis=0)
        high = tile.astype(BF).astype(F32)
        low = (tile - high).astype(BF).astype(F32)
        values = [jnp.concatenate([inside[0][comp][rows], inside[1][comp][rows]], axis=0) for comp in range(3)]
        values.append(high + roll(low, 16, 1) + folded)
        for n, value in enumerate(values):
            for copy in range(2):
                msg_ref[2 * block + copy, 16 * n : 16 * n + 16, :] = value.astype(BF)
    table_copy.wait()


def changes(f_x, f_z, weights_ref, at):
    w_x, w_y, w_z = (weights_ref[at + comp : at + comp + 1, :] for comp in range(3))
    return (f_x * w_y, -(f_x * w_x + f_z * w_z), f_z * w_y)


def rim_kernel(next_ref, msg_ref, held_ref, emf_ref, tips_ref, last_ref, msg_out, held_out, emf_out):
    msg_out[...] = msg_ref[...]
    held_out[...] = held_ref[...]
    emf_out[...] = emf_ref[...]
    shape = (8, emf_ref.shape[3])
    row = lax.broadcasted_iota(jnp.int32, shape, 0)
    lane = lax.broadcasted_iota(jnp.int32, shape, 1)
    inner = (lane > 0) & (lane < 127)
    slot = lane >> 1
    mz = last_ref[12:13, :]
    line = lax.broadcasted_iota(jnp.int32, (1, shape[1]), 1)
    signed = jnp.where(line == 0, -mz, mz)
    beyond = next_ref[...]
    wide = lax.broadcasted_iota(jnp.int32, beyond.shape, 1)
    slope = (jnp.where(wide == 127, 0.0, roll(beyond, -1, 1)) - jnp.where(wide == 0, 0.0, roll(beyond, 1, 1))) * mz
    my = beyond[12:13]
    rows = slice(56, 64)
    held = held_ref[rows, :]
    values, tiles = [], []
    for p in range(2):
        f = [beyond[2 * comp + p : 2 * comp + p + 1] for comp in range(3)]
        g = [beyond[2 * comp + 1 - p : 2 * comp + 2 - p] for comp in range(3)]
        d_z = [slope[2 * comp + p : 2 * comp + p + 1] for comp in range(2)]
        dy_x = (beyond[6 + p : 7 + p] - last_ref[6 + p : 7 + p, :]) * my
        dy_z = (beyond[8 + p : 9 + p] - last_ref[10 + p : 11 + p, :]) * my
        half = 0.5 if p == 0 else -0.5
        cur_x, cur_y, cur_z = dy_z - d_z[1], d_z[0] - half * g[2], half * g[1] - dy_x
        dens = beyond[10 + p : 11 + p]
        made = [
            (cur_y * f[2] - cur_z * f[1]) / dens,
            (cur_z * f[0] - cur_x * f[2]) / dens,
            (cur_x * f[1] - cur_y * f[0]) / dens,
        ]
        weight = signed / dens
        terms = made + [x * weight for x in f] + f[0:2]
        packed = jnp.zeros(shape, F32)
        for q, term in enumerate(terms):
            packed = jnp.where(slot == q, roll(jnp.broadcast_to(term, shape), 2 * q + 1, 1), packed)
        extra = changes(f[0], f[2], last_ref, 3 * p)
        for comp in range(3):
            change = jnp.where(row == 7, extra[comp], 0.0)
            value = jnp.where(inner, tips_ref[2 * comp + p] + change, 0.0)
            emf_out[comp, p, rows, :] = value.astype(BF)
            values.append(jnp.where(row == 7, jnp.where(inner, made[comp], 0.0), roll(value, -1, 0)))
            held = held + jnp.where(slot == 8 * p + comp, roll(change, 16 * p + 2 * comp + 1, 1), 0.0)
        tiles.append(packed)
    held_out[rows, :] = held
    for p in range(2):
        moved = roll(held if p == 0 else roll(held, -16, 1), -1, 0)
        tiles[p] = jnp.where(lane < 16, jnp.where(row == 7, tiles[p], moved), 0.0)
    tile = jnp.concatenate(tiles, axis=0)
    high = tile.astype(BF).astype(F32)
    low = (tile - high).astype(BF).astype(F32)
    old = msg_ref[14, 48:64, :].astype(F32)
    tiles = [jnp.concatenate([values[comp], values[3 + comp]], axis=0) for comp in range(3)]
    tiles.append(jnp.where(wide < 32, high + roll(low, 16, 1), old))
    for n, value in enumerate(tiles):
        for copy in range(2):
            msg_out[14 + copy, 16 * n : 16 * n + 16, :] = value.astype(BF)


def finished(held, beside):
    slot = (lax.broadcasted_iota(jnp.int32, held.shape, 1) >> 1) & 7
    flat = roll(beside, -12, 1) * jnp.where(slot == 0, roll(held, -10, 1), roll(held, -8, 1))
    upright = roll(beside, -10, 1) * roll(held, -4, 1) + roll(beside, -8, 1) * roll(held, -2, 1)
    return held + jnp.where(slot == 2, -upright, flat)


def at_edges(values, spot):
    lane = lax.broadcasted_iota(jnp.int32, values.shape, 1)
    return jnp.where((lane == 0) | (lane == 127), roll(values, -spot, 1), 0.0).astype(BF)


def line_edges(x_ref):
    held = jnp.concatenate([x_ref[i, 48:64, :] for i in range(16)], axis=0).astype(F32)
    held = held + roll(held, -16, 1)
    lane = lax.broadcasted_iota(jnp.int32, held.shape, 1)
    beside = jnp.where((lane & 1) == 0, roll(roll(held, -16, 0), -1, 1), roll(roll(held, 16, 0), 1, 1))
    values = finished(held, beside)
    return [at_edges(values, 2 * comp + 1) for comp in range(3)]


def finish_emf(x_ref, held_ref, inside_ref, low_ref, before_ref, emf_ref):
    me = lax.axis_index("yh") * 4 + lax.axis_index("yl") * 2 + lax.axis_index("xh")

    def fields(block):
        folded = x_ref[block, 48:64, :].astype(F32)
        rows = []
        for n in range(4):
            own = roll(folded, -(32 + 24 * n), 1)
            rows.append(own + (roll(own, -8, 1) + roll(own, -16, 1)))
        return jnp.concatenate(rows, axis=0)

    low, high = fields(lax.rem(me + 15, 16)), fields(lax.rem(me + 1, 16))
    lane = lax.broadcasted_iota(jnp.int32, low.shape, 1)
    beside = jnp.where((lane & 1) == 0, roll(high, -1, 1), roll(low, 1, 1))
    beside = jnp.where(lane < 16, roll(beside, 12, 1), roll(beside, 24, 1))
    shape = (8, low.shape[1])
    row = lax.broadcasted_iota(jnp.int32, shape, 0)
    lane = lax.broadcasted_iota(jnp.int32, shape, 1)
    inner = (lane > 0) & (lane < 127)
    tips = {}
    held = held_ref[0:8, :]
    for p in range(2):
        extra = changes(before_ref[p : p + 1, :], before_ref[2 + p : 3 + p, :], low_ref, 6 + 3 * p)
        for comp in range(3):
            change = jnp.where(row == 0, extra[comp], 0.0)
            value = low_ref[2 * comp + p : 2 * comp + p + 1, :] + extra[comp]
            plain = inside_ref[comp, p, 0:8, :].astype(F32)
            tips[comp, p] = jnp.where(row == 0, jnp.where(inner, value, 0.0), plain)
            moved = roll(change, 16 * p + 2 * comp + 1, 1)
            held = held + jnp.where((lane >> 1) == 8 * p + comp, moved, 0.0)
    values = finished(jnp.concatenate([held, held_ref[8:64, :]], axis=0), beside)
    for comp in range(3):
        for p in range(2):
            edges = at_edges(values, 16 * p + 2 * comp + 1)
            emf_ref[comp, p] = inside_ref[comp, p] + edges
            emf_ref[comp, p, 0:8, :] = (tips[comp, p] + edges[0:8].astype(F32)).astype(BF)


def z_kernel(x_ref, table_ref, held_ref, inside_ref, low_ref, before_ref, out_ref, emf_ref, mix_ref):
    edges = line_edges(x_ref)
    zero = jnp.zeros((16, 512), BF)
    total = None
    for n in range(2):
        sums, gaps = [], []
        for i in range(4 * n, 4 * n + 4):
            for side, pair in ((sums, 1), (gaps, -1)):
                tiles = []
                for c in range(3):
                    near, far = (
                        x_ref[m, 16 * c : 16 * c + 16, :] + edges[c][16 * m : 16 * m + 16] for m in (i, i + 8)
                    )
                    tiles.append(near + far if pair > 0 else near - far)
                side.append(jnp.concatenate(tiles, axis=0))
        sums, gaps = (jnp.concatenate([jnp.concatenate(x, axis=1), zero], axis=0) for x in (sums, gaps))
        empty = jnp.zeros((64, 512), BF)
        lines = jnp.concatenate(
            [jnp.concatenate([sums, empty], axis=0), jnp.concatenate([empty, gaps], axis=0)], axis=1
        )
        blocks = []
        for c in range(2):
            for jl in range(8):
                row = []
                for kappa in (2 * jl, 2 * jl + 1):
                    for i in range(4 * n, 4 * n + 4):
                        m = (kappa * i + 4 * c) % 16
                        cell = table_ref[m % 8, 32 * kappa : 32 * kappa + 32, :]
                        row.append(-cell if m >= 8 else cell)
                blocks.append(jnp.concatenate(row, axis=1))
        product = lax.dot_general(jnp.concatenate(blocks, axis=0), lines, ACROSS, preferred_element_type=F32)
        total = product if n == 0 else total + product
    for c in range(2):
        for jl in range(8):
            at = 32 * (8 * c + jl)
            mix_ref[pl.ds(2 * jl + c, 32, stride=16), :] = total[at : at + 32]
    out_ref[...] = mix_ref[...].astype(BF)
    finish_emf(x_ref, held_ref, inside_ref, low_ref, before_ref, emf_ref)


def add(a, b):
    return (a[0] + b[0], a[1] + b[1])


def sub(a, b):
    return (a[0] - b[0], a[1] - b[1])


def turned(a, eighths):
    eighths %= 16
    if eighths == 0:
        return a
    if eighths == 4:
        return (a[1], -a[0])
    if eighths == 2:
        r = math.sqrt(0.5)
        return ((a[0] + a[1]) * r, (a[1] - a[0]) * r)
    if eighths == 6:
        r = math.sqrt(0.5)
        return ((a[1] - a[0]) * r, -(a[0] + a[1]) * r)
    cos, sin = math.cos(math.pi * eighths / 8), math.sin(math.pi * eighths / 8)
    return (a[0] * cos + a[1] * sin, a[1] * cos - a[0] * sin)


def fourier4(x):
    s, d = add(x[0], x[2]), sub(x[0], x[2])
    t, u = add(x[1], x[3]), turned(sub(x[1], x[3]), 4)
    return [add(s, t), add(d, u), sub(s, t), sub(d, u)]


def fourier8(x):
    even = fourier4([x[0], x[2], x[4], x[6]])
    odd = fourier4([x[1], x[3], x[5], x[7]])
    odd = [turned(value, 2 * k) for k, value in enumerate(odd)]
    return [add(a, b) for a, b in zip(even, odd)] + [sub(a, b) for a, b in zip(even, odd)]


def y_kernel(x_ref, table_ref, turn_ref, order_ref, bins_ref, power_ref, sums_ref):
    lhs = lax.dot_general(order_ref[...], x_ref[...], ACROSS, preferred_element_type=F32).astype(BF)
    product = jnp.dot(lhs, table_ref[...], preferred_element_type=F32)
    scale = 1.0 / (6.0 * NY)
    for e in range(2):
        held = []
        for y0 in range(8):
            at = 16 * y0 + 8 * e
            a, b = product[at : at + 8, 0:256], product[at : at + 8, 256:512]
            if y0 > 0:
                cos, sin = turn_ref[0, y0 : y0 + 1, :], turn_ref[1, y0 : y0 + 1, :]
                a, b = a * cos + b * sin, b * cos - a * sin
            held.append((a, b))
        for q1, (a, b) in enumerate(fourier8(held)):
            power_ref[e : e + 1, 256 * q1 : 256 * q1 + 256] = (
                jnp.sum(a * a + b * b, axis=0, keepdims=True) * scale
            )
    sums = jnp.zeros((32, 128), F32)
    steps = lax.broadcasted_iota(jnp.int32, (128, 128), 0).astype(F32).astype(BF)
    one, none = jnp.ones((128, 128), BF), jnp.zeros((128, 128), BF)
    for e in range(2):
        value = power_ref[e : e + 1, :]
        bins = bins_ref[e : e + 1, :]
        coarse = lax.broadcasted_iota(jnp.int32, (8, NY), 0) == (bins >> 7)
        within = jnp.broadcast_to((bins & 127).astype(F32), (16, NY)).astype(BF)
        fine = []
        for n in range(NY // 128):
            tile = within[:, 128 * n : 128 * n + 128]
            fine.append(jnp.where(steps == jnp.concatenate([tile] * 8, axis=0), one, none))
        spread = jnp.where(coarse, value, 0.0)
        first = spread.astype(BF).astype(F32)
        second = (spread - first).astype(BF).astype(F32)
        third = spread - first - second
        pieces = jnp.concatenate([third, second, first, jnp.zeros_like(first)], axis=0).astype(BF)
        sums += lax.dot_general(pieces, jnp.concatenate(fine, axis=1), ACROSS, preferred_element_type=F32)
    sums = sums[0:8] + sums[8:16] + sums[16:24]
    sums = sums * (NB / (KZ * NY))
    for copy in range(sums_ref.shape[0]):
        sums_ref[copy] = sums


def on_device(field_b, density, level_y, level_z, bins):
    y_local, z_local = field_b.shape[2], field_b.shape[3]

    def shift(cells, axis, step):
        count = lax.axis_size(axis)
        return lax.ppermute(cells, axis, [(i, (i + step) % count) for i in range(count)])

    small = pltpu.CompilerParams(vmem_limit_bytes=16 * 2**20)
    far = [
        pltpu.with_memory_space_constraint(x, pltpu.HBM)
        for x in (level_y[None, :], level_z[None, :], field_b, density)
    ]
    upper, lower = pl.pallas_call(
        border_kernel,
        out_shape=(jax.ShapeDtypeStruct((16, z_local), F32), jax.ShapeDtypeStruct((4, z_local), F32)),
        in_specs=[pl.BlockSpec(memory_space=pltpu.HBM)] * 3,
        scratch_shapes=[
            pltpu.VMEM((1, y_local), jnp.int32),
            pltpu.VMEM((3, 2, 8, z_local), F32),
            pltpu.VMEM((3, 2, 8, z_local), F32),
            pltpu.VMEM((2, 8, z_local), F32),
            pltpu.SemaphoreType.DMA((4,)),
        ],
        compiler_params=small,
    )(far[0], far[2], far[3])
    after = shift(upper, GY, -1)
    before = shift(lower, GY, 1)
    scratch = [
        pltpu.VMEM((1, y_local), jnp.int32),
        pltpu.VMEM((1, z_local), jnp.int32),
        pltpu.VMEM(field_b.shape, F32),
        pltpu.VMEM(density.shape, F32),
        pltpu.SemaphoreType.DMA((5,)),
    ]
    made = (
        jax.ShapeDtypeStruct((16, 64, z_local), BF),
        jax.ShapeDtypeStruct((y_local, z_local), F32),
        jax.ShapeDtypeStruct(field_b.shape, BF),
    )
    rows = [jax.ShapeDtypeStruct(shape, F32) for shape in ((6, 8, z_local), (16, z_local), (16, z_local))]
    table = pltpu.with_memory_space_constraint(jnp.asarray(z_table()), pltpu.HBM)
    message, held, inside, tips, low, last, half = pl.pallas_call(
        message_kernel,
        out_shape=made + tuple(rows) + (jax.ShapeDtypeStruct(table.shape[1:], BF),),
        in_specs=[pl.BlockSpec(memory_space=pltpu.HBM)] * 5,
        scratch_shapes=scratch,
        compiler_params=small,
        cost_estimate=pl.CostEstimate(flops=2_000_000, bytes_accessed=2_000_000, transcendentals=0),
    )(*far, table)
    message, held, inside = pl.pallas_call(rim_kernel, out_shape=made, compiler_params=small)(
        after, message, held, inside, tips, last
    )
    lines = lax.all_to_all(message, GZ, 0, 0, tiled=True)
    z_modes, emf = pl.pallas_call(
        z_kernel,
        out_shape=(jax.ShapeDtypeStruct((512, 128), BF), jax.ShapeDtypeStruct(field_b.shape, BF)),
        scratch_shapes=[pltpu.VMEM((512, 128), F32)],
        compiler_params=small,
    )(lines, half, held, inside, low, before)
    spread = lax.all_to_all(z_modes.reshape(256, 2, 128), ("yh", "yl") + GY, 0, 0, tiled=True).reshape(512, 128)
    first = ('c', 'xl', 'xh')
    second = ('yh', 'yl', 'z')
    mode_power, sums = pl.pallas_call(
        y_kernel,
        out_shape=(
            jax.ShapeDtypeStruct((2, NY), F32),
            jax.ShapeDtypeStruct((lax.axis_size(first), 8, 128), F32),
        ),
        compiler_params=small,
    )(spread, *y_tables(), bins)
    sums = jnp.sum(lax.all_to_all(sums, first, 0, 0, tiled=True), axis=0)
    copies = jnp.broadcast_to(sums.astype(BF)[None], (lax.axis_size(second), 8, 128))
    spectrum = jnp.sum(lax.all_to_all(copies, second, 0, 0, tiled=True).astype(F32), axis=0).reshape(NB)
    return (emf, mode_power, spectrum)


def solution(mesh):
    fine = Mesh(mesh.devices.reshape(4, 2, 2, 8, 2, 2), GZ + GY)
    placed = (
        P(None, None, GY, GZ),
        P(None, GY, GZ),
        P(GY),
        P(GZ),
        P(GZ + GY, None),
    )
    return jax.shard_map(
        on_device,
        mesh=fine,
        in_specs=placed,
        out_specs=(P(None, None, GY, GZ), P(GZ + GY, None), P()),
        check_vma=False,
    )
```
